32 devices in a mesh: sub: 8 (over z, y), grp: 4 (over x, core).
Axes of the slice: x: 2, y: 2, z: 4, core: 2. Of those that a mesh axis runs over, the one named last changes fastest.
Arguments:
- schur: bfloat16 [8, 2048, 2048], P('sub', 'grp'), may hold values from -0.125 to 0.125
- rhs: float32 [8, 2048, 192], P('sub', 'grp'), may hold values from -6 to 6
- start: float32 [8, 2048, 192], P('sub', 'grp'), may hold values from -6 to 6
- project: bfloat16 [8, 32, 4096], P('sub', 'grp'), may hold values from -0.75 to 0.75
- coarse_basis: bfloat16 [8, 8, 2048], P('sub', None, 'grp'), may hold values from -0.375 to 0.375
- owner_of_face: int32 [8, 32, 1], replicated, may hold values from 0 to 4; in each aligned block of 32 rows (0 to 31, 32 to 63, ..., all dimensions but the last counted through in order) at most 8 rows name the same one
- mortar_of_face: int32 [8, 32], replicated, may hold values from 0 to 15
- mortar_order: int32 [8, 16], replicated, may hold values from 3 to 7
- subdomain_map: int32 [8], replicated, may hold values from 0 to 7, each once
- vertex_ids: int32 [8, 8], replicated, may hold values from 0 to 15, all different within a row
Outputs:
- solution: float32 [8, 2048, 192], P('sub', 'grp')
The draws below stay inside these ranges and needn't reach their ends.
Inputs may be any that keep to these rules, and one draw needn't show every extreme that they name: `owner_of_face`: the 32 faces of one subdomain name one offset at most 8 times. `mortar_of_face`: faces with the same owner and the same number lie on one mortar. `mortar_order`: row o holds the orders of the mortars owned by index o. `subdomain_map`: each subdomain once. `vertex_ids`: the 8 vertices of a subdomain differ; every vertex belongs to some subdomain.
All inputs are finite; a program needn't handle non-finite values.
Results may differ from the reference program's by a relative error of at most 0.0031.
Values may be sent and summed in bfloat16 or wider, within the bound.
No kernel may reach another device: no remote copies, remote signals or barrier semaphores. Data moves between devices by JAX's collectives and lax.ppermute only.
A program may use at most 64 MiB of HBM per device.

```python
import math
import jax
import jax.numpy as jnp
import numpy as np
from jax import lax

DEG = 8
FPTS = 64
MODES = 64
FACES = 32
M = 2048
R = 192
NCV = 8
MORT_OWN = 16
ITERS = 2
REACH = 2
NB = 5
CAP = 8
SUBS = 8
NV = 16


def place_ends(result, key, smallest, largest):
    longest = result.shape.index(max(result.shape))
    spots = []
    for shift in (0, 1):
        where = [jax.random.randint(jax.random.fold_in(key, axis), (), 0, length) for axis, length in enumerate(result.shape)]
        where[longest] = (where[longest] + shift) % result.shape[longest]
        spots.append(tuple(where))
    return result.at[spots[0]].set(smallest).at[spots[1]].set(largest)


def shard_levels(own_key, extent, shards, low, high):
    level, own = 1.0, jax.random.fold_in(own_key, 6)
    for dim, shards_of in shards:
        steps = jnp.exp(jax.random.uniform(jax.random.fold_in(own, dim), (shards_of,), jnp.float32, low / len(shards), high / len(shards)))
        level = level * jnp.repeat(steps, extent[dim] // shards_of).reshape([-1 if axis == dim else 1 for axis in range(len(extent))])
    return level


def distinct(key, rows, count, top, lift):
    ranking = jax.random.permutation(jax.random.fold_in(key, 1), count)
    pull = ranking
    for power in range(3):
        pull = pull * pull // count
    pull = pull * lift // count
    tickets = jax.random.randint(jax.random.fold_in(key, 2), (rows, count), 0, 4096) + pull
    fixed_rows = jax.random.permutation(jax.random.fold_in(key, 3), rows)[jnp.arange(count) % rows]
    tickets = jnp.where(jnp.arange(rows)[:, None] == fixed_rows[None, :], 1 << 14, tickets)
    score = tickets * count + jnp.arange(count)
    return lax.top_k(score.astype(jnp.int32), top)[1].astype(jnp.int32)


def assign_block(key, own, number, rows, amount, top, bound, skew):
    order = jax.random.permutation(key, amount)
    crowded, usual = shares(amount, rows * top, bound, skew, True), shares(amount, rows * top, bound, skew, False)
    places = jnp.arange(amount)

    def named(tallies, offset_by):
        used = int((tallies > 0).sum())
        fixed = max(1, used // 4)
        moved = fixed + (places - fixed + offset_by * (used - fixed)) % max(1, amount - fixed)
        return jnp.zeros((amount,), jnp.int32).at[order[jnp.where(places < fixed, places, moved)]].set(jnp.asarray(tallies, jnp.int32))

    tallies = jnp.where(number % 4 == 0, named(crowded, number // 4), named(usual, number - number // 4 - 1))
    mixed = jax.random.permutation(jax.random.fold_in(own, 3), amount)
    donor, sink = mixed[0:amount // 2 * 2:2], mixed[1:amount // 2 * 2:2]
    room = jnp.minimum(tallies[donor] - 1, bound - tallies[sink]) // 2
    room = jnp.where((donor == order[0]) | (sink == order[0]) | (tallies[sink] == 0), 0, jnp.maximum(room, 0))
    moved = jax.random.randint(jax.random.fold_in(own, 4), (amount // 2,), 0, 1 << 20) % (room + 1)
    tallies = tallies.at[donor].add(-moved).at[sink].add(moved)
    members = jnp.searchsorted(jnp.cumsum(tallies), jnp.arange(rows * top), side="right").astype(jnp.int32)
    grid = members.reshape(top, rows).T
    grid = grid[jax.random.permutation(jax.random.fold_in(own, 1), rows)]
    offset_by = jax.random.randint(jax.random.fold_in(own, 2), (rows, 1), 0, top)
    return jnp.take_along_axis(grid, (jnp.arange(top)[None, :] + offset_by) % top, axis=1)


def shares(count, total, reach, lean, full):
    portions = [(1 << 20) // math.isqrt(rank ** lean) + 1 for rank in range(1, count + 1)]
    largest = reach if full else min(reach, max(-(-total // count), total * portions[0] // sum(portions)))
    least = 1 if total - largest >= count - 1 else 0
    given, surplus = [largest] + [least] * (count - 1), total - largest - least * (count - 1)
    while surplus > 0:
        free = [i for i in range(1, count) if given[i] < largest] or [i for i in range(1, count) if given[i] < reach]
        pool, budget = sum([portions[i] for i in free]), surplus
        for i in free:
            addition = min(reach - given[i], max(1, budget * portions[i] // pool), surplus)
            given[i] = given[i] + addition
            surplus = surplus - addition
    return np.array(given)


def scatter_about(rng, shape, deviation, most, cuts=(), kind=jnp.bfloat16):
    level = shard_levels(rng, shape, cuts, -0.22, 0.18) if cuts else 1.0
    values = jax.random.normal(rng, shape, jnp.float32) * deviation * level
    return jnp.minimum(jnp.maximum(values, -most), most).astype(kind)


def setup_inputs(seed: int = 0) -> dict:
    key_list = jax.random.split(jax.random.key(seed), 11)
    schur = scatter_about(key_list[0], (SUBS, M, M), M ** -0.5, 0.125, ((0, 8), (1, 4)))
    rhs = scatter_about(key_list[1], (SUBS, M, R), 1.0, 6.0, ((0, 8), (1, 4)), jnp.float32)
    start = scatter_about(key_list[2], (SUBS, M, R), 1.0, 6.0, ((0, 8), (1, 4)), jnp.float32)
    project = scatter_about(key_list[3], (SUBS, FACES, MODES * FPTS), FPTS ** -0.5, 0.75, ((0, 8), (1, 4)))
    coarse_basis = scatter_about(key_list[4], (SUBS, NCV, M), (M // NCV) ** -0.5, 0.375, ((0, 8), (2, 4)))
    owner_of_face_keys = jax.random.split(jax.random.fold_in(key_list[5], 1), SUBS * FACES // FACES)
    owner_of_face_turns = jax.random.permutation(jax.random.fold_in(key_list[5], 3), SUBS * FACES // FACES)
    owner_of_face = jax.vmap(lambda own, number: assign_block(jax.random.fold_in(key_list[5], 2), own, number, FACES, NB, 1, CAP, 2))(owner_of_face_keys, owner_of_face_turns).reshape((SUBS, FACES, 1))
    mortar_of_face = place_ends(jax.random.randint(key_list[6], (SUBS, FACES), 0, MORT_OWN), jax.random.fold_in(key_list[6], 1), 0, MORT_OWN - 1).astype(jnp.int32)
    mortar_order = place_ends(jax.random.randint(key_list[7], (SUBS, MORT_OWN), DEG // 2 - 1, DEG), jax.random.fold_in(key_list[7], 1), DEG // 2 - 1, DEG - 1).astype(jnp.int32)
    subdomain_map = jax.random.permutation(key_list[8], SUBS).astype(jnp.int32)
    vertex_ids = distinct(key_list[9], SUBS, NV, NCV, 0)
    return {"schur": schur, "rhs": rhs, "start": start, "project": project, "coarse_basis": coarse_basis, "owner_of_face": owner_of_face, "mortar_of_face": mortar_of_face, "mortar_order": mortar_order, "subdomain_map": subdomain_map, "vertex_ids": vertex_ids}


relax_weight = 0.5
coarse_weight = 0.5


def apply_one(operands):
    matrix, vector = operands
    return jnp.dot(matrix, vector, preferred_element_type=jnp.float32)


def reference(schur, rhs, start, project, coarse_basis, owner_of_face, mortar_of_face, mortar_order, subdomain_map, vertex_ids):
    highest = lax.Precision.HIGHEST
    holder = subdomain_map.astype(jnp.int32)
    offsets = jnp.take(owner_of_face[:, :, 0], holder, axis=0).astype(jnp.int32)
    places = jnp.arange(SUBS, dtype=jnp.int32)[:, None]
    owners = jnp.mod(places + offsets - REACH, SUBS).astype(jnp.int32)
    mortar_local = jnp.take(mortar_of_face, holder, axis=0).astype(jnp.int32)
    corners = jnp.take(vertex_ids, holder, axis=0).reshape(-1).astype(jnp.int32)
    mortar_keys = (owners * MORT_OWN + mortar_local).reshape(-1).astype(jnp.int32)
    all_mortars = SUBS * MORT_OWN
    counts = jax.ops.segment_sum(jnp.ones(mortar_keys.shape, jnp.float32), mortar_keys, num_segments=all_mortars)
    degree = jnp.arange(MODES, dtype=jnp.int32)
    orders = mortar_order.reshape(all_mortars, 1).astype(jnp.int32)
    keep_mask = ((degree[None, :] // DEG <= orders) & (degree[None, :] % DEG <= orders)).astype(jnp.float32)
    tables = project.reshape(SUBS, FACES, MODES, FPTS).astype(jnp.float32)
    coarse_wide = coarse_basis.astype(jnp.float32)
    traces = start
    for repeat in range(ITERS):
        trace_b = traces.astype(jnp.bfloat16)
        product = lax.map(apply_one, (schur, trace_b))
        residual = (product - rhs).astype(jnp.bfloat16)
        face_res = residual.reshape(SUBS, FACES, FPTS, R).astype(jnp.float32)
        coeffs = jnp.einsum('sfmp,sfpr->sfmr', tables, face_res, precision=highest).astype(jnp.bfloat16)
        mortar_sums = jax.ops.segment_sum(coeffs.astype(jnp.float32).reshape(SUBS * FACES, MODES * R), mortar_keys, num_segments=all_mortars)
        averages = mortar_sums / jnp.maximum(counts, 1.0)[:, None]
        averages = (averages.reshape(all_mortars, MODES, R) * keep_mask[:, :, None]).astype(jnp.bfloat16)
        returned = jnp.take(averages, mortar_keys, axis=0).reshape(SUBS, FACES, MODES, R).astype(jnp.float32)
        lifted = jnp.einsum('sfmp,sfmr->sfpr', tables, returned, precision=highest).reshape(SUBS, M, R)
        partial_value = jnp.einsum('svm,smr->svr', coarse_wide, lifted, precision=highest)
        vertex = jax.ops.segment_sum(partial_value.reshape(SUBS * NCV, R), corners, num_segments=NV)
        picked = jnp.take(vertex, corners, axis=0).reshape(SUBS, NCV, R)
        coarse_corr = jnp.einsum('svm,svr->smr', coarse_wide, picked, precision=highest)
        traces = traces - relax_weight * lifted - coarse_weight * coarse_corr
    return traces
```

```python
import functools

import jax
import jax.numpy as jnp
from jax import lax
from jax.experimental import pallas as pl
from jax.experimental.pallas import tpu as pltpu
from jax.sharding import PartitionSpec as P

DEG = 8
MODES = 64
FPTS = 64
MORT_OWN = 16
REACH = 2
CAP = 8
LINKS = 2 * REACH + 1
SLOTS = LINKS * CAP

relax_weight = 0.5
coarse_weight = 0.5

BF = jnp.bfloat16
F32 = jnp.float32
CONTRACT_FIRST = (((0,), (0,)), ((), ()))
VMEM = pl.BlockSpec(memory_space=pltpu.VMEM)
SMEM = pl.BlockSpec(memory_space=pltpu.SMEM)


def split_two(value):
    high = value.astype(BF)
    return high, (value - high.astype(F32)).astype(BF)


class Sizes:
    def __init__(self, subs, grps, schur, project, coarse_basis, rhs):
        self.subs = subs
        self.grps = grps
        self.rows = schur.shape[1]
        self.all_rows = schur.shape[2]
        self.own = project.shape[1]
        self.faces = self.own * grps
        self.corners = coarse_basis.shape[1]
        self.rhs = rhs.shape[2]
        self.vertices = 2 * subs
        self.share = MODES // grps
        self.wide = -(-(self.rhs + self.vertices) // 128) * 128
        self.lanes = self.rhs // 128 * 128
        self.tail = self.rhs - self.lanes
        self.near = self.vertices == self.share and LINKS <= subs <= 2 * LINKS
        self.extra = 2 if self.near else 0
        self.t_src = 0
        self.t_arr = SLOTS
        self.t_slot = 2 * SLOTS
        self.t_count = self.t_slot + self.faces
        self.t_order = self.t_count + MORT_OWN
        self.t_corner = self.t_order + MORT_OWN
        self.t_end = self.t_corner + self.corners


def call(kernel, sizes, ins, outs, args, scratch=()):
    return pl.pallas_call(
        functools.partial(kernel, sizes),
        out_shape=outs,
        in_specs=ins,
        out_specs=jax.tree.map(lambda _: VMEM, outs),
        scratch_shapes=list(scratch),
    )(*args)


def table_kernel(z, ids, owner, mortar, order, smap, vids, table, used, names):
    s = ids[0]
    g = ids[1]
    d = smap[s]
    for i in range(SLOTS):
        table[z.t_src + i] = 0
    for i in range(LINKS):
        used[i] = 0
    for i in range(MORT_OWN):
        table[z.t_count + i] = 0
        table[z.t_order + i] = order[s * MORT_OWN + i]
    for i in range(z.corners):
        table[z.t_corner + i] = vids[d * z.corners + i]
    for f in range(z.faces):
        o = owner[d * z.faces + f]
        r = used[o]
        used[o] = r + 1
        slot = o * CAP + r
        table[z.t_slot + f] = slot
        table[z.t_src + slot] = ((f // z.own) ^ g) * z.own + f % z.own
    for link in range(LINKS):
        dd = smap[lax.rem(s - link + REACH + z.subs, z.subs)]
        r = jnp.int32(0)
        for f in range(z.faces):
            hit = (owner[dd * z.faces + f] == link).astype(jnp.int32)
            m = mortar[dd * z.faces + f]
            names[r] = m
            table[z.t_count + m] = table[z.t_count + m] + hit
            r = r + hit
        for i in range(CAP):
            table[z.t_arr + link * CAP + i] = jnp.where(i < r, names[i], MORT_OWN)


def narrow_kernel(z, start, out):
    half = z.rows // 2
    value = start[...].astype(BF)
    out[: z.rows, :] = value[:, : z.lanes]
    out[z.rows :, : z.tail] = value[:half, z.lanes :]
    out[z.rows :, z.tail :] = value[half:, z.lanes :]


def first_kernel(z, ids, schur, b0, b1, b2, b3, rhs, tables, cext, o0, o1, o2, o3, res_out, gathered, held, coeffs):
    g = ids[1]
    half = z.rows // 2
    for j, b in enumerate((b0, b1, b2, b3)):
        off = pl.multiple_of((g ^ j) * z.rows, z.rows)
        gathered[pl.ds(off, z.rows), : z.lanes] = b[: z.rows, :]
        gathered[pl.ds(off, half), z.lanes :] = b[z.rows :, : z.tail]
        gathered[pl.ds(off + half, half), z.lanes :] = b[z.rows :, z.tail :]
    product = jnp.dot(schur[...], gathered[...], preferred_element_type=F32)
    residual = product - rhs[...]
    res_out[...] = residual
    held[:, : z.rhs] = residual.astype(BF)
    held[:, z.rhs :] = cext[...]
    for f in range(z.own):
        coeffs[f] = jnp.dot(tables[f, :MODES, :], held[f * FPTS : (f + 1) * FPTS, :], preferred_element_type=F32).astype(BF)
    for j, o in enumerate((o0, o1, o2, o3)):
        at = pl.multiple_of((g ^ j) * z.share, z.share)
        for f in range(z.own):
            o[f] = coeffs[f, pl.ds(at, z.share), :]


def pack_kernel(z, table, c0, c1, c2, c3, o0, o1, o2, o3, o4, data):
    for j, c in enumerate((c0, c1, c2, c3)):
        data[j * z.own : (j + 1) * z.own] = c[...]
    for link, o in enumerate((o0, o1, o2, o3, o4)):
        for i in range(CAP):
            o[i] = data[table[z.t_src + link * CAP + i]]


def average_body(z, ids, table, arrivals, total, held):
    g = ids[1]
    total[...] = jnp.zeros_like(total)
    for link, a in enumerate(arrivals):
        for i in range(CAP):
            m = table[z.t_arr + link * CAP + i]
            total[m] = total[m] + a[i].astype(F32)
    mode = g * z.share + lax.broadcasted_iota(jnp.int32, (z.share, z.rhs), 0)
    degree_a = mode // DEG
    degree_b = mode % DEG
    degree = jnp.maximum(degree_a, degree_b)
    for k in range(MORT_OWN):
        divisor = jnp.maximum(table[z.t_count + k], 1).astype(F32)
        kept = jnp.where(degree <= table[z.t_order + k], 1.0, 0.0)
        value = total[k, :, : z.rhs] / divisor * kept
        held[k] = value.astype(BF)
    held[MORT_OWN] = jnp.zeros_like(held[MORT_OWN])


def reply_body(z, table, held, g_high, g_low, replies, vertex):
    flat = held[:MORT_OWN].reshape(MORT_OWN * z.share, z.rhs)
    value = lax.dot_general(g_high, flat, CONTRACT_FIRST, preferred_element_type=F32)
    value = value + lax.dot_general(g_low, flat, CONTRACT_FIRST, preferred_element_type=F32)
    if z.near:
        high, low = split_two(value)
        vertex[0] = high
        vertex[1] = low
    else:
        vertex[...] = value
    for link, o in enumerate(replies):
        for i in range(CAP):
            o[i] = held[table[z.t_arr + link * CAP + i]]
        if z.near:
            o[CAP] = high
            o[CAP + 1] = low


def average_first(z, ids, table, a0, a1, a2, a3, a4, o0, o1, o2, o3, o4, vertex, g_high, g_low, total, held):
    average_body(z, ids, table, (a0, a1, a2, a3, a4), total, held)
    wide = total[:MORT_OWN, :, z.rhs : z.rhs + z.vertices].reshape(MORT_OWN * z.share, z.vertices)
    high, low = split_two(wide)
    g_high[...] = high
    g_low[...] = low
    reply_body(z, table, held, high, low, (o0, o1, o2, o3, o4), vertex)


def average_second(z, ids, table, a0, a1, a2, a3, a4, g_high, g_low, o0, o1, o2, o3, o4, vertex, total, held):
    average_body(z, ids, table, (a0, a1, a2, a3, a4), total, held)
    reply_body(z, table, held, g_high[...], g_low[...], (o0, o1, o2, o3, o4), vertex)


def near_sum(z, blocks, fars):
    value = None
    for b, at in [(b, CAP) for b in blocks] + [(b, 0) for b in fars]:
        one = b[at].astype(F32) + b[at + 1].astype(F32)
        value = one if value is None else value + one
    return split_two(value)


def spread_first(z, table, *refs):
    fars = refs[LINKS:-2]
    blocks, out, data = refs[:LINKS], refs[-2], refs[-1]
    for link, b in enumerate(blocks):
        data[link * CAP : (link + 1) * CAP] = b[:CAP]
    quarter = z.own // 2
    for f in range(z.faces):
        out[f] = data[table[z.t_slot + f], :, : z.lanes]
    for member in range(z.grps):
        for i in range(quarter):
            f = member * z.own + i
            left = data[table[z.t_slot + f], :, z.lanes :]
            right = data[table[z.t_slot + f + quarter], :, z.lanes :]
            out[z.faces + member * quarter + i] = jnp.concatenate([left, right], axis=1)
    if z.near:
        high, low = near_sum(z, blocks, fars)
        at = z.faces + z.faces // 2
        out[at] = high[:, : z.lanes]
        out[at + 1] = low[:, : z.lanes]
        out[at + 2] = jnp.concatenate([high[:, z.lanes :], low[:, z.lanes :]], axis=1)


def spread_second(z, ids, table, *refs):
    fars = refs[LINKS : -1 - z.grps]
    blocks, outs, data = refs[:LINKS], refs[-1 - z.grps : -1], refs[-1]
    g = ids[1]
    for link, b in enumerate(blocks):
        data[link * CAP : (link + 1) * CAP] = b[:CAP]
    for j, o in enumerate(outs):
        for i in range(z.own):
            o[i] = data[table[z.t_slot + (g ^ j) * z.own + i]]
    if z.near:
        high, low = near_sum(z, blocks, fars)
        for o in outs:
            o[z.own] = high
            o[z.own + 1] = low


def picked_rows(z, table, whole):
    rows = [whole[pl.ds(table[z.t_corner + i], 1), :] for i in range(z.corners)]
    high, low = split_two(jnp.concatenate(rows, axis=0))
    return jnp.concatenate([high.astype(F32), low.astype(F32)], axis=0).astype(BF)


def second_kernel(z, ids, table, schur, *refs):
    n = z.grps
    shares, refs = refs[:n], refs[n:]
    exts, refs = refs[:n], refs[n:]
    vertex_in, resid, refs = refs[0], refs[1], refs[2:]
    outs, refs = refs[:n], refs[n:]
    own_out, averages, gathered, whole, held, coeffs = refs
    g = ids[1]
    quarter = z.own // 2
    if z.near:
        at = z.faces + z.faces // 2
        for j, a in enumerate(shares):
            main = a[at].astype(F32) + a[at + 1].astype(F32)
            both = a[at + 2].astype(F32)
            tail = both[:, : z.tail] + both[:, z.tail :]
            if j:
                main = main + whole[:, : z.lanes]
                tail = tail + whole[:, z.lanes :]
            whole[:, : z.lanes] = main
            whole[:, z.lanes :] = tail
    else:
        whole[...] = vertex_in[...]
    picked = picked_rows(z, table, whole)
    for j, e in enumerate(exts):
        member = g ^ j
        for i in range(z.own):
            f = member * z.own + i
            for jj, a in enumerate(shares):
                rows = pl.ds(pl.multiple_of((g ^ jj) * z.share, z.share), z.share)
                averages[f, rows, : z.lanes] = a[f]
                low = (i // quarter) * z.tail
                averages[f, rows, z.lanes :] = a[z.faces + member * quarter + i % quarter, :, low : low + z.tail]
            averages[f, MODES:, :] = picked
            lifted = lax.dot_general(e[i], averages[f], CONTRACT_FIRST, preferred_element_type=F32)
            gathered[pl.ds(pl.multiple_of(f * FPTS, FPTS), FPTS), :] = lifted.astype(BF)
            if j == 0:
                own_out[i] = averages[f]
    product = jnp.dot(schur[...], gathered[...], preferred_element_type=F32)
    held[...] = (resid[...] - 0.5 * product).astype(BF)
    for f in range(z.own):
        coeffs[f] = jnp.dot(exts[0][f, :MODES, :], held[f * FPTS : (f + 1) * FPTS, :], preferred_element_type=F32).astype(BF)
    for j, o in enumerate(outs):
        at = pl.multiple_of((g ^ j) * z.share, z.share)
        for f in range(z.own):
            o[f] = coeffs[f, pl.ds(at, z.share), :]


def last_kernel(z, ids, table, *refs):
    n = z.grps
    shares, refs = refs[:n], refs[n:]
    ext, vertex_in, earlier, start, out, averages, whole = refs
    g = ids[1]
    if z.near:
        value = None
        for c in shares:
            one = c[z.own].astype(F32) + c[z.own + 1].astype(F32)
            value = one if value is None else value + one
        whole[...] = value
    else:
        whole[...] = vertex_in[...]
    picked = picked_rows(z, table, whole)
    for i in range(z.own):
        for j, c in enumerate(shares):
            rows = pl.ds(pl.multiple_of((g ^ j) * z.share, z.share), z.share)
            averages[i, rows, :] = c[i]
        averages[i, MODES:, :] = picked
        both = lax.dot_general(ext[i], averages[i], CONTRACT_FIRST, preferred_element_type=F32)
        both = both + lax.dot_general(ext[i], earlier[i], CONTRACT_FIRST, preferred_element_type=F32)
        rows = slice(i * FPTS, (i + 1) * FPTS)
        out[rows, :] = start[rows, :] - 0.5 * both


def passed_along(value, steps):
    count = lax.axis_size("sub")
    return lax.ppermute(value, "sub", [(s, (s + steps) % count) for s in range(count)])


def swapped(value, mask):
    count = lax.axis_size("grp")
    return lax.ppermute(value, "grp", [(s, s ^ mask) for s in range(count)])


def hypercube(value):
    two = swapped(value, 2)
    one = swapped(value, 1)
    return [value, one, two, swapped(two, 1)]


def exchanged(blocks):
    return [blocks[0]] + [swapped(blocks[j], j) for j in range(1, len(blocks))]


def along_links(blocks, sign):
    return [b if link == REACH else passed_along(b, sign * (link - REACH)) for link, b in enumerate(blocks)]


def body(schur, rhs, start, project, coarse_basis, owner_of_face, mortar_of_face, mortar_order, subdomain_map, vertex_ids):
    subs, grps = lax.axis_size("sub"), lax.axis_size("grp")
    z = Sizes(subs, grps, schur, project, coarse_basis, rhs)
    ids = jnp.stack([lax.axis_index("sub"), lax.axis_index("grp")]).astype(jnp.int32)
    shape = jax.ShapeDtypeStruct
    matrix, target, first = schur[0], rhs[0], start[0]

    packed_rows = z.rows + z.rows * z.tail // z.lanes
    trace_b = call(narrow_kernel, z, [VMEM], shape((packed_rows, z.lanes), BF), (first,))
    blocks = hypercube(trace_b)

    table = pl.pallas_call(
        functools.partial(table_kernel, z),
        out_shape=shape((z.t_end,), jnp.int32),
        in_specs=[SMEM] * 6,
        out_specs=SMEM,
        scratch_shapes=[pltpu.SMEM((LINKS,), jnp.int32), pltpu.SMEM((z.faces + 1,), jnp.int32)],
    )(ids, owner_of_face.reshape(-1), mortar_of_face.reshape(-1), mortar_order.reshape(-1), subdomain_map, vertex_ids.reshape(-1))

    joined = jnp.concatenate([project[0], coarse_basis[0]], axis=1) if z.own == z.corners else None
    assert joined is not None

    def extended(value):
        tables = value[:, : MODES * FPTS].reshape(z.own, MODES, FPTS)
        coarse = value[:, MODES * FPTS :].reshape(z.corners, z.own, FPTS).transpose(1, 0, 2)
        return jnp.concatenate([tables, coarse, coarse], axis=1)

    ext_own = extended(joined)
    exts = [ext_own] + [extended(v) for v in hypercube(joined)[1:]]

    my_corners = lax.dynamic_index_in_dim(
        vertex_ids, lax.dynamic_index_in_dim(subdomain_map, lax.axis_index("sub"), 0, False), 0, False
    )
    corner_hot = (my_corners[:, None] == jnp.arange(z.wide - z.rhs, dtype=jnp.int32)[None, :]).astype(BF)
    cext = lax.dot_general(coarse_basis[0], corner_hot, CONTRACT_FIRST, preferred_element_type=F32).astype(BF)

    part = shape((z.own, z.share, z.wide), BF)
    thin = shape((z.own, z.share, z.rhs), BF)
    link_wide = [shape((CAP, z.share, z.wide), BF)] * LINKS
    link_thin = [shape((CAP, z.share, z.rhs), BF)] * LINKS
    reply = [shape((CAP + z.extra, z.share, z.rhs), BF)] * LINKS
    vertex_shape = shape((2, z.vertices, z.rhs), BF) if z.near else shape((z.vertices, z.rhs), F32)
    g_shape = [shape((MORT_OWN * z.share, z.vertices), BF)] * 2

    def far(vertex):
        if not z.near:
            return []
        return [passed_along(vertex, off) for off in range(REACH + 1, subs - REACH)]

    def summed(vertex):
        if z.near:
            return jnp.zeros((8, 128), F32)
        return lax.psum(vertex, ("sub", "grp"))

    *parts, resid = call(
        first_kernel,
        z,
        [SMEM] + [VMEM] * 8,
        [part] * grps + [shape((z.rows, z.rhs), F32)],
        (ids, matrix, *blocks, target, ext_own, cext),
        (
            pltpu.VMEM((z.all_rows, z.rhs), BF),
            pltpu.VMEM((z.rows, z.wide), BF),
            pltpu.VMEM((z.own, MODES, z.wide), BF),
        ),
    )
    parts = exchanged(parts)
    outgoing = call(pack_kernel, z, [SMEM] + [VMEM] * 4, link_wide, (table, *parts), (pltpu.VMEM((z.faces, z.share, z.wide), BF),))
    arrived = along_links(outgoing, 1)
    *replies, vertex, g_high, g_low = call(
        average_first,
        z,
        [SMEM] * 2 + [VMEM] * LINKS,
        reply + [vertex_shape] + g_shape,
        (ids, table, *arrived),
        (pltpu.VMEM((MORT_OWN + 1, z.share, z.wide), F32), pltpu.VMEM((MORT_OWN + 1, z.share, z.rhs), BF)),
    )
    answered = along_links(replies, -1)
    fars = far(vertex)
    count = z.faces + z.faces // 2 + (3 if z.near else 0)
    spread = call(
        spread_first,
        z,
        [SMEM] + [VMEM] * (LINKS + len(fars)),
        shape((count, z.share, z.lanes), BF),
        (table, *answered, *fars),
        (pltpu.VMEM((SLOTS, z.share, z.rhs), BF),),
    )
    shares = hypercube(spread)
    *parts, earlier = call(
        second_kernel,
        z,
        [SMEM] * 2 + [VMEM] * (1 + 2 * grps + 2),
        [thin] * grps + [shape((z.own, MODES + 2 * z.corners, z.rhs), BF)],
        (ids, table, matrix, *shares, *exts, summed(vertex), resid),
        (
            pltpu.VMEM((z.faces, MODES + 2 * z.corners, z.rhs), BF),
            pltpu.VMEM((z.all_rows, z.rhs), BF),
            pltpu.VMEM((z.vertices, z.rhs), F32),
            pltpu.VMEM((z.rows, z.rhs), BF),
            pltpu.VMEM((z.own, MODES, z.rhs), BF),
        ),
    )
    parts = exchanged(parts)
    outgoing = call(pack_kernel, z, [SMEM] + [VMEM] * 4, link_thin, (table, *parts), (pltpu.VMEM((z.faces, z.share, z.rhs), BF),))
    arrived = along_links(outgoing, 1)
    *replies, vertex = call(
        average_second,
        z,
        [SMEM] * 2 + [VMEM] * (LINKS + 2),
        reply + [vertex_shape],
        (ids, table, *arrived, g_high, g_low),
        (pltpu.VMEM((MORT_OWN + 1, z.share, z.rhs), F32), pltpu.VMEM((MORT_OWN + 1, z.share, z.rhs), BF)),
    )
    answered = along_links(replies, -1)
    fars = far(vertex)
    outs = call(
        spread_second,
        z,
        [SMEM] * 2 + [VMEM] * (LINKS + len(fars)),
        [shape((z.own + z.extra, z.share, z.rhs), BF)] * grps,
        (ids, table, *answered, *fars),
        (pltpu.VMEM((SLOTS, z.share, z.rhs), BF),),
    )
    shares = exchanged(outs)
    result = call(
        last_kernel,
        z,
        [SMEM] * 2 + [VMEM] * (grps + 4),
        shape((z.rows, z.rhs), F32),
        (ids, table, *shares, ext_own, summed(vertex), earlier, first),
        (
            pltpu.VMEM((z.own, MODES + 2 * z.corners, z.rhs), BF),
            pltpu.VMEM((z.vertices, z.rhs), F32),
        ),
    )
    return result[None]


def solution(mesh):
    return jax.shard_map(
        body,
        mesh=mesh,
        in_specs=(
            P("sub", "grp", None),
            P("sub", "grp", None),
            P("sub", "grp", None),
            P("sub", "grp", None),
            P("sub", None, "grp"),
            P(),
            P(),
            P(),
            P(),
            P(),
        ),
        out_specs=P("sub", "grp", None),
        check_vma=False,
    )
```

```python
import functools

import jax
import jax.numpy as jnp
from jax import lax
from jax.experimental import pallas as pl
from jax.experimental.pallas import tpu as pltpu
from jax.sharding import PartitionSpec as P

DEG = 8
MODES = 64
FPTS = 64
MORT_OWN = 16
REACH = 2
CAP = 8
LINKS = 2 * REACH + 1
SLOTS = LINKS * CAP

BF = jnp.bfloat16
F32 = jnp.float32
CONTRACT_FIRST = (((0,), (0,)), ((), ()))
CONTRACT_LAST = (((1,), (1,)), ((), ()))
VMEM = pl.BlockSpec(memory_space=pltpu.VMEM)
SMEM = pl.BlockSpec(memory_space=pltpu.SMEM)
HBM = pl.BlockSpec(memory_space=pltpu.HBM)


def split_two(value):
    high = value.astype(BF)
    return high, (value - high.astype(F32)).astype(BF)


class Sizes:
    def __init__(self, subs, grps, schur, project, coarse_basis, rhs):
        self.subs = subs
        self.grps = grps
        self.rows = schur.shape[1]
        self.all_rows = schur.shape[2]
        self.own = project.shape[1]
        self.faces = self.own * grps
        self.corners = coarse_basis.shape[1]
        self.rhs = rhs.shape[2]
        self.vertices = 2 * subs
        self.share = MODES // grps
        self.wide = -(-(self.rhs + self.vertices) // 128) * 128
        self.lanes = self.rhs // 128 * 128
        self.tail = self.rhs - self.lanes
        self.near = self.vertices == self.share and LINKS <= subs <= 2 * LINKS
        self.extra = 2 if self.near else 0
        self.t_src = 0
        self.t_arr = SLOTS
        self.t_slot = 2 * SLOTS
        self.t_count = self.t_slot + self.faces
        self.t_order = self.t_count + MORT_OWN
        self.t_corner = self.t_order + MORT_OWN
        self.t_end = self.t_corner + self.corners


def call(kernel, sizes, outs, args, scratch=()):
    single = not isinstance(outs, list)
    outs = [outs] if single else outs
    ins = [SMEM if a.dtype == jnp.int32 else VMEM for a in args]
    args = [
        pltpu.with_memory_space_constraint(a, pltpu.SMEM if a.dtype == jnp.int32 else pltpu.VMEM) for a in args
    ]
    results = pl.pallas_call(
        functools.partial(kernel, sizes),
        out_shape=[pltpu.VMEM(o.shape, o.dtype) for o in outs],
        in_specs=ins,
        out_specs=[VMEM for _ in outs],
        scratch_shapes=list(scratch),
        compiler_params=pltpu.CompilerParams(vmem_limit_bytes=16 << 20),
    )(*args)
    return results[0] if single else results


def table_kernel(z, owner, mortar, order, smap, vids, table, used, names):
    s = lax.axis_index("sub")
    g = lax.axis_index("grp")
    d = smap[s]
    for i in range(SLOTS):
        table[z.t_src + i] = 0
    for i in range(LINKS):
        used[i] = 0
    for i in range(MORT_OWN):
        table[z.t_count + i] = 0
        table[z.t_order + i] = order[s, i]
    for i in range(z.corners):
        table[z.t_corner + i] = vids[d, i]
    for f in range(z.faces):
        o = owner[d, 0, f]
        r = used[o]
        used[o] = r + 1
        slot = o * CAP + r
        table[z.t_slot + f] = slot
        table[z.t_src + slot] = ((f // z.own) ^ g) * z.own + f % z.own
    for link in range(LINKS):
        dd = smap[lax.rem(s - link + REACH + z.subs, z.subs)]
        r = jnp.int32(0)
        for f in range(z.faces):
            hit = (owner[dd, 0, f] == link).astype(jnp.int32)
            m = mortar[dd, f]
            names[r] = m
            table[z.t_count + m] = table[z.t_count + m] + hit
            r = r + hit
        for i in range(CAP):
            table[z.t_arr + link * CAP + i] = jnp.where(i < r, names[i], MORT_OWN)


def narrow_kernel(z, start, out):
    out[...] = start[...].astype(BF)


def load_kernel(schur, rhs, schur_out, rhs_out, sems):
    copies = [
        pltpu.make_async_copy(schur, schur_out, sems.at[0]),
        pltpu.make_async_copy(rhs, rhs_out, sems.at[1]),
    ]
    for c in copies:
        c.start()
    for c in copies:
        c.wait()


def join_kernel(z, tables, coarse, out):
    half = MODES // 2
    for f in range(z.own):
        out[f, :half, :] = jnp.concatenate([tables[f, :half, :], tables[f, half:, :]], axis=1)
        one = coarse[:, f * FPTS : (f + 1) * FPTS].astype(F32)
        two = jnp.concatenate([one, one], axis=0).astype(BF)
        out[f, half:, :] = jnp.concatenate([two, two], axis=1)


def tables_of(ext):
    half = MODES // 2
    return jnp.concatenate([ext[:half, :FPTS], ext[:half, FPTS:]], axis=0)


def lifting(ext):
    half = MODES // 2
    return jnp.concatenate([ext[:, :FPTS], ext[:half, FPTS:]], axis=0)


def share_rows(z, member):
    at = member * z.share
    gap = 2 * z.corners
    return pl.ds(pl.multiple_of(jnp.where(at < MODES // 2, at, at + gap), z.share), z.share)


def coarse_rows(z):
    return slice(MODES // 2, MODES // 2 + 2 * z.corners)


def first_kernel(z, table, schur, b0, b1, b2, b3, rhs, tables, coarse, o0, o1, o2, o3, res_out, gathered, held, coeffs):
    g = lax.axis_index("grp")
    for j, b in enumerate((b0, b1, b2, b3)):
        gathered[:, pl.ds(pl.multiple_of((g ^ j) * z.rows, z.rows), z.rows)] = b[...]
    product = lax.dot_general(schur[...], gathered[...], CONTRACT_LAST, preferred_element_type=F32)
    residual = product - rhs[...].T
    res_out[...] = residual
    held[:, : z.rhs] = residual.astype(BF)
    column = lax.broadcasted_iota(jnp.int32, (1, z.wide - z.rhs), 1)
    hot = jnp.concatenate(
        [jnp.where(column == table[z.t_corner + i], 1.0, 0.0) for i in range(z.corners)], axis=0
    ).astype(BF)
    held[:, z.rhs :] = lax.dot_general(coarse[...], hot, CONTRACT_FIRST, preferred_element_type=F32).astype(BF)
    for f in range(z.own):
        coeffs[f] = jnp.dot(tables_of(tables[f]), held[f * FPTS : (f + 1) * FPTS, :], preferred_element_type=F32).astype(BF)
    for j, o in enumerate((o0, o1, o2, o3)):
        at = pl.multiple_of((g ^ j) * z.share, z.share)
        for f in range(z.own):
            o[f] = coeffs[f, pl.ds(at, z.share), :]


def pack_kernel(z, table, c0, c1, c2, c3, o0, o1, o2, o3, o4, data):
    for j, c in enumerate((c0, c1, c2, c3)):
        data[j * z.own : (j + 1) * z.own] = c[...]
    for link, o in enumerate((o0, o1, o2, o3, o4)):
        for i in range(CAP):
            o[i] = data[table[z.t_src + link * CAP + i]]


def average_body(z, table, arrivals, total, held):
    g = lax.axis_index("grp")
    total[...] = jnp.zeros_like(total)
    for link, a in enumerate(arrivals):
        for i in range(CAP):
            m = table[z.t_arr + link * CAP + i]
            total[m] = total[m] + a[i].astype(F32)
    mode = g * z.share + lax.broadcasted_iota(jnp.int32, (z.share, z.rhs), 0)
    degree_a = mode // DEG
    degree_b = mode % DEG
    degree = jnp.maximum(degree_a, degree_b)
    for k in range(MORT_OWN):
        divisor = jnp.maximum(table[z.t_count + k], 1).astype(F32)
        kept = jnp.where(degree <= table[z.t_order + k], 1.0, 0.0)
        value = total[k, :, : z.rhs] / divisor * kept
        held[k] = value.astype(BF)
    held[MORT_OWN] = jnp.zeros_like(held[MORT_OWN])


def reply_body(z, table, held, g_high, g_low, replies, vertex):
    flat = held[:MORT_OWN].reshape(MORT_OWN * z.share, z.rhs)
    value = lax.dot_general(g_high, flat, CONTRACT_FIRST, preferred_element_type=F32)
    value = value + lax.dot_general(g_low, flat, CONTRACT_FIRST, preferred_element_type=F32)
    if z.near:
        high, low = split_two(value)
        vertex[0] = high
        vertex[1] = low
    else:
        vertex[...] = value
    for link, o in enumerate(replies):
        for i in range(CAP):
            o[i] = held[table[z.t_arr + link * CAP + i]]
        if z.near:
            o[CAP] = high
            o[CAP + 1] = low


def average_first(z, table, a0, a1, a2, a3, a4, o0, o1, o2, o3, o4, vertex, g_high, g_low, total, held):
    average_body(z, table, (a0, a1, a2, a3, a4), total, held)
    wide = total[:MORT_OWN, :, z.rhs : z.rhs + z.vertices].reshape(MORT_OWN * z.share, z.vertices)
    high, low = split_two(wide)
    g_high[...] = high
    g_low[...] = low
    reply_body(z, table, held, high, low, (o0, o1, o2, o3, o4), vertex)


def average_second(z, table, a0, a1, a2, a3, a4, g_high, g_low, o0, o1, o2, o3, o4, vertex, total, held):
    average_body(z, table, (a0, a1, a2, a3, a4), total, held)
    reply_body(z, table, held, g_high[...], g_low[...], (o0, o1, o2, o3, o4), vertex)


def near_sum(blocks, fars):
    value = None
    for b, at in [(b, CAP) for b in blocks] + [(b, 0) for b in fars]:
        one = b[at].astype(F32) + b[at + 1].astype(F32)
        value = one if value is None else value + one
    return split_two(value)


def spread_first(z, table, *refs):
    fars = refs[LINKS:-2]
    blocks, out, data = refs[:LINKS], refs[-2], refs[-1]
    for link, b in enumerate(blocks):
        data[link * CAP : (link + 1) * CAP] = b[:CAP]
    quarter = z.own // 2
    for f in range(z.faces):
        out[f] = data[table[z.t_slot + f], :, : z.lanes]
    for member in range(z.grps):
        for i in range(quarter):
            f = member * z.own + i
            left = data[table[z.t_slot + f], :, z.lanes :]
            right = data[table[z.t_slot + f + quarter], :, z.lanes :]
            out[z.faces + member * quarter + i] = jnp.concatenate([left, right], axis=1)
    if z.near:
        high, low = near_sum(blocks, fars)
        at = z.faces + z.faces // 2
        out[at] = high[:, : z.lanes]
        out[at + 1] = low[:, : z.lanes]
        out[at + 2] = jnp.concatenate([high[:, z.lanes :], low[:, z.lanes :]], axis=1)


def spread_second(z, table, *refs):
    fars = refs[LINKS : -1 - z.grps]
    blocks, outs, data = refs[:LINKS], refs[-1 - z.grps : -1], refs[-1]
    g = lax.axis_index("grp")
    for link, b in enumerate(blocks):
        data[link * CAP : (link + 1) * CAP] = b[:CAP]
    for j, o in enumerate(outs):
        for i in range(z.own):
            o[i] = data[table[z.t_slot + (g ^ j) * z.own + i]]
    if z.near:
        high, low = near_sum(blocks, fars)
        for o in outs:
            o[z.own] = high
            o[z.own + 1] = low


def picked_rows(z, table, whole):
    rows = [whole[pl.ds(table[z.t_corner + i], 1), :] for i in range(z.corners)]
    high, low = split_two(jnp.concatenate(rows, axis=0))
    return jnp.concatenate([high.astype(F32), low.astype(F32)], axis=0).astype(BF)


def second_kernel(z, table, schur, *refs):
    n = z.grps
    shares, refs = refs[:n], refs[n:]
    exts, refs = refs[:n], refs[n:]
    vertex_in, resid, refs = refs[0], refs[1], refs[2:]
    outs, refs = refs[:n], refs[n:]
    own_out, averages, gathered, whole, held, coeffs = refs
    g = lax.axis_index("grp")
    quarter = z.own // 2
    if z.near:
        at = z.faces + z.faces // 2
        for j, a in enumerate(shares):
            main = a[at].astype(F32) + a[at + 1].astype(F32)
            both = a[at + 2].astype(F32)
            tail = both[:, : z.tail] + both[:, z.tail :]
            if j:
                main = main + whole[:, : z.lanes]
                tail = tail + whole[:, z.lanes :]
            whole[:, : z.lanes] = main
            whole[:, z.lanes :] = tail
    else:
        whole[...] = vertex_in[...]
    picked = picked_rows(z, table, whole)
    for j, e in enumerate(exts):
        member = g ^ j
        for i in range(z.own):
            f = member * z.own + i
            for jj, a in enumerate(shares):
                rows = share_rows(z, g ^ jj)
                averages[f, rows, : z.lanes] = a[f]
                low = (i // quarter) * z.tail
                averages[f, rows, z.lanes :] = a[z.faces + member * quarter + i % quarter, :, low : low + z.tail]
            averages[f, coarse_rows(z), :] = picked
            lifted = lax.dot_general(lifting(e[i]), averages[f], CONTRACT_FIRST, preferred_element_type=F32)
            gathered[pl.ds(pl.multiple_of(f * FPTS, FPTS), FPTS), :] = lifted.astype(BF)
            if j == 0:
                own_out[i] = averages[f]
    product = jnp.dot(schur[...], gathered[...], preferred_element_type=F32)
    held[...] = (resid[...] - 0.5 * product).astype(BF)
    for f in range(z.own):
        coeffs[f] = jnp.dot(tables_of(exts[0][f]), held[f * FPTS : (f + 1) * FPTS, :], preferred_element_type=F32).astype(BF)
    for j, o in enumerate(outs):
        at = pl.multiple_of((g ^ j) * z.share, z.share)
        for f in range(z.own):
            o[f] = coeffs[f, pl.ds(at, z.share), :]


def last_kernel(z, table, *refs):
    n = z.grps
    shares, refs = refs[:n], refs[n:]
    ext, vertex_in, earlier, start, out, averages, whole, whole_change = refs
    g = lax.axis_index("grp")
    if z.near:
        value = None
        for c in shares:
            one = c[z.own].astype(F32) + c[z.own + 1].astype(F32)
            value = one if value is None else value + one
        whole[...] = value
    else:
        whole[...] = vertex_in[...]
    picked = picked_rows(z, table, whole)
    for i in range(z.own):
        for j, c in enumerate(shares):
            averages[i, share_rows(z, g ^ j), :] = c[i]
        averages[i, coarse_rows(z), :] = picked
        lift = lifting(ext[i])
        both = lax.dot_general(lift, averages[i], CONTRACT_FIRST, preferred_element_type=F32)
        both = both + lax.dot_general(lift, earlier[i], CONTRACT_FIRST, preferred_element_type=F32)
        whole_change[i * FPTS : (i + 1) * FPTS, :] = both
    out[...] = start[...] - 0.5 * whole_change[...].T


def passed_along(value, steps):
    count = lax.axis_size("sub")
    return lax.ppermute(value, "sub", [(s, (s + steps) % count) for s in range(count)])


def swapped(value, mask):
    count = lax.axis_size("grp")
    return lax.ppermute(value, "grp", [(s, s ^ mask) for s in range(count)])


def hypercube(value):
    two = swapped(value, 2)
    one = swapped(value, 1)
    return [value, one, two, swapped(two, 1)]


def exchanged(blocks):
    return [blocks[0]] + [swapped(blocks[j], j) for j in range(1, len(blocks))]


def along_links(blocks, sign):
    return [b if link == REACH else passed_along(b, sign * (link - REACH)) for link, b in enumerate(blocks)]


def run(schur, rhs, start, project, coarse_basis, owner_of_face, mortar_of_face, mortar_order, subdomain_map, vertex_ids):
    subs, grps = lax.axis_size("sub"), lax.axis_size("grp")
    z = Sizes(subs, grps, schur, project, coarse_basis, rhs)
    shape = jax.ShapeDtypeStruct
    matrix, target, first = schur[0], rhs[0].T, start[0].T

    trace_b = call(narrow_kernel, z, shape((z.rhs, z.rows), BF), (first,))
    block_two = swapped(trace_b, 2)
    block_one = swapped(trace_b, 1)

    table = pl.pallas_call(
        functools.partial(table_kernel, z),
        out_shape=pltpu.SMEM((z.t_end,), jnp.int32),
        in_specs=[SMEM] * 5,
        out_specs=SMEM,
        scratch_shapes=[pltpu.SMEM((LINKS,), jnp.int32), pltpu.SMEM((z.faces + 1,), jnp.int32)],
    )(owner_of_face.transpose(0, 2, 1), mortar_of_face, mortar_order, subdomain_map, vertex_ids)
    matrix, target = pl.pallas_call(
        load_kernel,
        out_shape=[pltpu.VMEM(matrix.shape, BF), pltpu.VMEM(target.shape, F32)],
        in_specs=[HBM] * 2,
        out_specs=[VMEM] * 2,
        scratch_shapes=[pltpu.SemaphoreType.DMA((2,))],
        compiler_params=pltpu.CompilerParams(vmem_limit_bytes=16 << 20),
    )(*[pltpu.with_memory_space_constraint(a, pltpu.HBM) for a in (matrix, target)])
    assert z.own == z.corners
    ext_shape = shape((z.own, MODES // 2 + 2 * z.corners, 2 * FPTS), BF)
    ext_own = call(join_kernel, z, ext_shape, (project[0].reshape(z.own, MODES, FPTS), coarse_basis[0]))
    ext_two = swapped(ext_own, 2)
    block_three = swapped(block_two, 1)
    blocks = [trace_b, block_one, block_two, block_three]

    part = shape((z.own, z.share, z.wide), BF)
    thin = shape((z.own, z.share, z.rhs), BF)
    link_wide = [shape((CAP, z.share, z.wide), BF)] * LINKS
    link_thin = [shape((CAP, z.share, z.rhs), BF)] * LINKS
    reply = [shape((CAP + z.extra, z.share, z.rhs), BF)] * LINKS
    vertex_shape = shape((2, z.vertices, z.rhs), BF) if z.near else shape((z.vertices, z.rhs), F32)
    g_shape = [shape((MORT_OWN * z.share, z.vertices), BF)] * 2

    def far(vertex):
        if not z.near:
            return []
        return [passed_along(vertex, off) for off in range(REACH + 1, subs - REACH)]

    def summed(vertex):
        if z.near:
            return jnp.zeros((8, 128), F32)
        return lax.psum(vertex, ("sub", "grp"))

    *parts, resid = call(
        first_kernel,
        z,
        [part] * grps + [shape((z.rows, z.rhs), F32)],
        (table, matrix, *blocks, target, ext_own, coarse_basis[0]),
        (
            pltpu.VMEM((z.rhs, z.all_rows), BF),
            pltpu.VMEM((z.rows, z.wide), BF),
            pltpu.VMEM((z.own, MODES, z.wide), BF),
        ),
    )
    parts, ext_two = lax.optimization_barrier((parts, ext_two))
    parts = exchanged(parts)
    exts = [ext_own, swapped(ext_own, 1), ext_two, swapped(ext_two, 1)]
    parts, exts = lax.optimization_barrier((parts, exts))
    outgoing = call(pack_kernel, z, link_wide, (table, *parts), (pltpu.VMEM((z.faces, z.share, z.wide), BF),))
    arrived = along_links(outgoing, 1)
    *replies, vertex, g_high, g_low = call(
        average_first,
        z,
        reply + [vertex_shape] + g_shape,
        (table, *arrived),
        (pltpu.VMEM((MORT_OWN + 1, z.share, z.wide), F32), pltpu.VMEM((MORT_OWN + 1, z.share, z.rhs), BF)),
    )
    answered = along_links(replies, -1)
    fars = far(vertex)
    count = z.faces + z.faces // 2 + (3 if z.near else 0)
    spread = call(
        spread_first,
        z,
        shape((count, z.share, z.lanes), BF),
        (table, *answered, *fars),
        (pltpu.VMEM((SLOTS, z.share, z.rhs), BF),),
    )
    shares = hypercube(spread)
    *parts, earlier = call(
        second_kernel,
        z,
        [thin] * grps + [shape((z.own, MODES + 2 * z.corners, z.rhs), BF)],
        (table, matrix, *shares, *exts, summed(vertex), resid),
        (
            pltpu.VMEM((z.faces, MODES + 2 * z.corners, z.rhs), BF),
            pltpu.VMEM((z.all_rows, z.rhs), BF),
            pltpu.VMEM((z.vertices, z.rhs), F32),
            pltpu.VMEM((z.rows, z.rhs), BF),
            pltpu.VMEM((z.own, MODES, z.rhs), BF),
        ),
    )
    parts = exchanged(parts)
    outgoing = call(pack_kernel, z, link_thin, (table, *parts), (pltpu.VMEM((z.faces, z.share, z.rhs), BF),))
    arrived = along_links(outgoing, 1)
    *replies, vertex = call(
        average_second,
        z,
        reply + [vertex_shape],
        (table, *arrived, g_high, g_low),
        (pltpu.VMEM((MORT_OWN + 1, z.share, z.rhs), F32), pltpu.VMEM((MORT_OWN + 1, z.share, z.rhs), BF)),
    )
    answered = along_links(replies, -1)
    fars = far(vertex)
    outs = call(
        spread_second,
        z,
        [shape((z.own + z.extra, z.share, z.rhs), BF)] * grps,
        (table, *answered, *fars),
        (pltpu.VMEM((SLOTS, z.share, z.rhs), BF),),
    )
    shares = exchanged(outs)
    result = call(
        last_kernel,
        z,
        shape((z.rhs, z.rows), F32),
        (table, *shares, ext_own, summed(vertex), earlier, first),
        (
            pltpu.VMEM((z.own, MODES + 2 * z.corners, z.rhs), BF),
            pltpu.VMEM((z.vertices, z.rhs), F32),
            pltpu.VMEM((z.rows, z.rhs), F32),
        ),
    )
    return result.T[None]


def solution(mesh):
    return jax.shard_map(
        run,
        mesh=mesh,
        in_specs=(
            P("sub", "grp", None),
            P("sub", "grp", None),
            P("sub", "grp", None),
            P("sub", "grp", None),
            P("sub", None, "grp"),
            P(),
            P(),
            P(),
            P(),
            P(),
        ),
        out_specs=P("sub", "grp", None),
        check_vma=False,
    )
```

```python
import functools

import jax
import jax.numpy as jnp
from jax import lax
from jax.experimental import pallas as pl
from jax.experimental.pallas import tpu as pltpu
from jax.sharding import PartitionSpec as P

DEG = 8
MODES = 64
FPTS = 64
MORT_OWN = 16
REACH = 2
CAP = 8
LINKS = 2 * REACH + 1
SLOTS = LINKS * CAP

BF = jnp.bfloat16
F32 = jnp.float32
CONTRACT_FIRST = (((0,), (0,)), ((), ()))
CONTRACT_LAST = (((1,), (1,)), ((), ()))
VMEM = pl.BlockSpec(memory_space=pltpu.VMEM)
SMEM = pl.BlockSpec(memory_space=pltpu.SMEM)
HBM = pl.BlockSpec(memory_space=pltpu.HBM)


def split_two(value):
    high = value.astype(BF)
    return high, (value - high.astype(F32)).astype(BF)


class Sizes:
    def __init__(self, subs, grps, schur, project, coarse_basis, rhs):
        self.subs = subs
        self.grps = grps
        self.rows = schur.shape[1]
        self.all_rows = schur.shape[2]
        self.own = project.shape[1]
        self.faces = self.own * grps
        self.corners = coarse_basis.shape[1]
        self.rhs = rhs.shape[2]
        self.vertices = 2 * subs
        self.share = MODES // grps
        self.extra = 2 * self.vertices
        self.wide = -(-(self.rhs + self.extra) // 128) * 128
        self.lanes = self.rhs // 128 * 128
        self.tail = self.rhs - self.lanes
        self.missing = range(REACH + 1, subs - REACH)
        self.near = self.vertices == self.share and LINKS <= subs and len(self.missing) <= 3
        self.more = 3 if self.near else 0
        self.dense = self.share * self.rhs // self.lanes
        self.pieces = max(1, 128 // self.extra)
        self.slabs = max(1, self.extra // 128)
        self.head = self.faces + self.faces * self.tail // self.lanes
        self.packed = self.head + self.faces * self.slabs // self.pieces
        self.t_src = 0
        self.t_arr = SLOTS
        self.t_slot = 2 * SLOTS
        self.t_count = self.t_slot + self.faces
        self.t_order = self.t_count + MORT_OWN
        self.t_corner = self.t_order + MORT_OWN
        self.t_end = self.t_corner + self.corners


def call(kernel, sizes, outs, args, scratch=(), static=()):
    single = not isinstance(outs, list)
    outs = [outs] if single else outs
    ins = [SMEM if a.dtype == jnp.int32 else VMEM for a in args]
    args = [
        pltpu.with_memory_space_constraint(a, pltpu.SMEM if a.dtype == jnp.int32 else pltpu.VMEM) for a in args
    ]
    results = pl.pallas_call(
        functools.partial(kernel, sizes, *static),
        out_shape=[pltpu.VMEM(o.shape, o.dtype) for o in outs],
        in_specs=ins,
        out_specs=[VMEM for _ in outs],
        scratch_shapes=list(scratch),
        compiler_params=pltpu.CompilerParams(vmem_limit_bytes=16 << 20),
    )(*args)
    return results[0] if single else results


def meeting_of(link, s):
    odd, high = s % 2 == 1, (s // 2) % 2 == 1
    if link == REACH:
        return 4
    if abs(link - REACH) == 1:
        return jnp.where(odd == (link < REACH), 0, 3)
    return jnp.where(high == (link < REACH), 1, 2)


def table_kernel(z, owner, mortar, order, smap, vids, table, used, names, met):
    s = lax.axis_index("sub")
    g = lax.axis_index("grp")
    d = smap[s]
    for i in range(SLOTS):
        table[z.t_src + i] = 0
    for i in range(LINKS):
        used[i] = 0
        met[i] = jnp.int32(meeting_of(i, s))
    for i in range(MORT_OWN):
        table[z.t_count + i] = 0
        table[z.t_order + i] = order[s, i]
    for i in range(z.corners):
        table[z.t_corner + i] = vids[d, i]
    for f in range(z.faces):
        o = owner[d, 0, f]
        r = used[o]
        used[o] = r + 1
        slot = met[o] * CAP + r
        table[z.t_slot + f] = slot
        table[z.t_src + slot] = ((f // z.own) ^ g) * z.own + f % z.own
    for link in range(LINKS):
        dd = smap[lax.rem(s - link + REACH + z.subs, z.subs)]
        r = jnp.int32(0)
        for f in range(z.faces):
            hit = (owner[dd, 0, f] == link).astype(jnp.int32)
            m = mortar[dd, f]
            names[r] = m
            table[z.t_count + m] = table[z.t_count + m] + hit
            r = r + hit
        for i in range(CAP):
            table[z.t_arr + met[2 * REACH - link] * CAP + i] = jnp.where(i < r, names[i], MORT_OWN)


def narrow_kernel(z, start, coarse, out, held, basis, sems):
    pieces = 4
    size = z.rhs // pieces
    copies = [
        pltpu.make_async_copy(start.at[pl.ds(i * size, size)], held.at[pl.ds(i * size, size)], sems.at[i])
        for i in range(pieces)
    ]
    copies.append(pltpu.make_async_copy(coarse, basis, sems.at[pieces]))
    for c in copies:
        c.start()
    for i in range(pieces):
        copies[i].wait()
        out[i * size : (i + 1) * size, :] = held[i * size : (i + 1) * size, :].astype(BF)
    copies[pieces].wait()
    out[z.rhs :, :] = basis[...]


def unpack_kernel(z, p0, p1, p2, p3, out):
    for j, p in enumerate((p0, p1, p2, p3)):
        for i in range(z.own):
            out[j * z.own + i] = tables_of(p[i])


def load_kernel(schur, rhs, schur_out, rhs_out, sems):
    copies = [
        pltpu.make_async_copy(schur, schur_out, sems.at[0]),
        pltpu.make_async_copy(rhs, rhs_out, sems.at[1]),
    ]
    for c in copies:
        c.start()
    for c in copies:
        c.wait()


def join_kernel(z, tables, out):
    half = MODES // 2
    for f in range(z.own):
        out[f] = jnp.concatenate([tables[f, :half, :], tables[f, half:, :]], axis=1)


def tables_of(pair):
    return jnp.concatenate([pair[:, :FPTS], pair[:, FPTS:]], axis=0)


def share_rows(z, member):
    return pl.ds(pl.multiple_of(member * z.share, z.share), z.share)


def hot_rows(z, table, width, shift):
    column = lax.broadcasted_iota(jnp.int32, (1, width), 1)
    rows = [jnp.where(column == table[z.t_corner + i] + shift, 1.0, 0.0) for i in range(z.corners)]
    return jnp.concatenate(rows, axis=0).astype(BF)


def first_kernel(z, table, schur, b0, b1, b2, b3, rhs, tables, coarse, o0, o1, o2, o3, res_out, ext_out, gathered, held, coeffs):
    g = lax.axis_index("grp")
    for j, b in enumerate((b0, b1, b2, b3)):
        gathered[:, pl.ds(pl.multiple_of((g ^ j) * z.rows, z.rows), z.rows)] = b[...]
    product = lax.dot_general(schur[...], gathered[...], CONTRACT_LAST, preferred_element_type=F32)
    residual = product[:, : z.rhs] - rhs[...].T
    res_out[...] = residual
    held[:, : z.rhs] = residual.astype(BF)
    width = z.wide - z.rhs
    basis = lax.dot_general(coarse[...], hot_rows(z, table, width, 0), CONTRACT_FIRST, preferred_element_type=F32)
    image = jnp.dot(
        product[:, z.rhs :].astype(BF), hot_rows(z, table, width, z.vertices), preferred_element_type=F32
    )
    held[:, z.rhs :] = (basis + image).astype(BF)
    for f in range(z.own):
        coeffs[f] = jnp.dot(tables_of(tables[f]), held[f * FPTS : (f + 1) * FPTS, :], preferred_element_type=F32).astype(BF)
    ext_out[...] = coeffs[:, :, z.rhs :]
    for j, o in enumerate((o0, o1, o2, o3)):
        for f in range(z.own):
            o[f] = coeffs[f, share_rows(z, g ^ j), :]


def pack_kernel(z, sums, table, c0, c1, c2, c3, o0, o1, o2, o3, o4, data):
    parts = (c0, c1, c2, c3)
    for j, c in enumerate(parts):
        data[j * z.own : (j + 1) * z.own] = c[: z.own]
    for k, o in enumerate((o0, o1, o2, o3, o4)):
        for i in range(CAP):
            o[i] = data[table[z.t_src + k * CAP + i]]
    if sums:
        value = sum((c[z.own :].astype(F32) for c in parts[1:]), parts[0][z.own :].astype(F32)).astype(BF)
        for o in (o0, o1, o2, o3, o4):
            o[CAP:] = value


def average_kernel(z, dense, table, *refs):
    arrivals, refs = refs[:LINKS], refs[LINKS:]
    replies, refs = refs[:LINKS], refs[LINKS:]
    near, total, held = refs if dense and z.near else (None, *refs)
    g = lax.axis_index("grp")
    total[...] = jnp.zeros_like(total)
    for k, a in enumerate(arrivals):
        for i in range(CAP):
            m = table[z.t_arr + k * CAP + i]
            total[m] = total[m] + a[i].astype(F32)
    shape = total.shape[1:]
    row = lax.broadcasted_iota(jnp.int32, shape, 0)
    if dense:
        column = lax.broadcasted_iota(jnp.int32, shape, 1)
        half = z.share // 2
        row = jnp.where(row < z.share, row, row - z.share + jnp.where(column < z.tail, 0, half))
    mode = g * z.share + row
    degree = jnp.maximum(mode // DEG, mode % DEG)
    for k in range(MORT_OWN):
        divisor = jnp.maximum(table[z.t_count + k], 1).astype(F32)
        kept = jnp.where(degree <= table[z.t_order + k], 1.0, 0.0)
        held[k] = (total[k] / divisor * kept).astype(BF)
    held[MORT_OWN] = jnp.zeros_like(held[MORT_OWN])
    for k, o in enumerate(replies):
        for i in range(CAP):
            o[i] = held[table[z.t_arr + k * CAP + i]]
    if dense and z.near:
        s = lax.axis_index("sub")
        odd, high = s % 2 == 1, (s // 2) % 2 == 1
        inner_one, inner_two, outer_two, outer_one, own = [a[CAP:].astype(F32) for a in arrivals]
        near[...] = own + inner_one + inner_two + outer_two + outer_one
        after = jnp.where(odd, outer_one, inner_one)
        before = jnp.where(odd, inner_one, outer_one)
        after_two = jnp.where(high, outer_two, inner_two)
        behind = after * (1.0 if len(z.missing) > 0 else 0.0)
        if len(z.missing) > 1:
            behind = behind + after_two
        ahead = before * (1.0 if len(z.missing) > 2 else 0.0)
        replies[1][CAP:] = jnp.where(high, behind, ahead).astype(BF)
        replies[2][CAP:] = jnp.where(high, ahead, behind).astype(BF)


def spread_first(z, table, *refs):
    blocks, out, data = refs[:LINKS], refs[-2], refs[-1]
    for link, b in enumerate(blocks):
        data[link * CAP : (link + 1) * CAP] = b[:CAP]
    half = z.own // 2
    for f in range(z.faces):
        out[f] = data[table[z.t_slot + f], :, : z.lanes]
    for member in range(z.grps):
        for i in range(half):
            f = member * z.own + i
            left = data[table[z.t_slot + f], :, z.lanes : z.rhs]
            right = data[table[z.t_slot + f + half], :, z.lanes : z.rhs]
            out[z.faces + member * half + i] = jnp.concatenate([left, right], axis=1)
    if z.pieces > 1:
        for p in range(z.faces // z.pieces):
            ends = [data[table[z.t_slot + p * z.pieces + i], :, z.rhs : z.rhs + z.extra] for i in range(z.pieces)]
            out[z.head + p] = jnp.concatenate(ends, axis=1)
    else:
        for f in range(z.faces):
            for p in range(z.slabs):
                at = z.rhs + p * 128
                out[z.head + f * z.slabs + p] = data[table[z.t_slot + f], :, at : at + 128]


def spread_second(z, table, *refs):
    n = LINKS + (1 if z.near else 0)
    blocks, near = refs[:LINKS], refs[LINKS:n]
    outs, data = refs[n : n + z.grps], refs[-1]
    g = lax.axis_index("grp")
    for k, b in enumerate(blocks):
        data[k * CAP : (k + 1) * CAP] = b[:CAP]
    for j, o in enumerate(outs):
        for i in range(z.own):
            o[i] = data[table[z.t_slot + (g ^ j) * z.own + i]]
    if z.near:
        refs[n + z.grps][...] = near[0][...] + blocks[1][CAP:].astype(F32) + blocks[2][CAP:].astype(F32)


def to_dense(z, value):
    half = z.share // 2
    tail = jnp.concatenate([value[:half, z.lanes :], value[half:, z.lanes :]], axis=1)
    return jnp.concatenate([value[:, : z.lanes], tail], axis=0)


def from_dense(z, value):
    tail = value[z.share :]
    tail = jnp.concatenate([tail[:, : z.tail], tail[:, z.tail :]], axis=0)
    return jnp.concatenate([value[: z.share], tail], axis=1)


def second_kernel(z, table, schur, *refs):
    n = z.grps
    shares, refs = refs[:n], refs[n:]
    tables, resid, coarse, ext_in, refs = refs[0], refs[1], refs[2], refs[3], refs[4:]
    outs, refs = refs[:n], refs[n:]
    own_out, hits_out, sums_out, averages, gathered, held, coeffs, scales = refs
    g = lax.axis_index("grp")
    half = z.own // 2
    for j in range(n):
        member = g ^ j
        for i in range(z.own):
            f = member * z.own + i
            slot = j * z.own + i
            for jj, a in enumerate(shares):
                rows = share_rows(z, g ^ jj)
                averages[slot, rows, : z.lanes] = a[f]
                low = (i // half) * z.tail
                averages[slot, rows, z.lanes :] = a[z.faces + member * half + i % half, :, low : low + z.tail]
            lifted = lax.dot_general(tables[slot], averages[slot], CONTRACT_FIRST, preferred_element_type=F32)
            gathered[pl.ds(pl.multiple_of(f * FPTS, FPTS), FPTS), :] = lifted.astype(BF)
    product = jnp.dot(schur[...], gathered[...], preferred_element_type=F32)
    held[...] = (resid[...] - 0.5 * product).astype(BF)
    for f in range(z.own):
        coeffs[f] = jnp.dot(tables[f], held[f * FPTS : (f + 1) * FPTS, :], preferred_element_type=F32)
    for j, o in enumerate(outs):
        for f in range(z.own):
            o[f] = to_dense(z, coeffs[f, share_rows(z, g ^ j), :]).astype(BF)
    own_out[...] = averages[: z.own]
    for i in range(z.own):
        for jj, a in enumerate(shares):
            rows = share_rows(z, g ^ jj)
            if z.pieces > 1:
                low = (i % z.pieces) * z.extra
                scales[i, rows, :] = a[z.head + (g * z.own + i) // z.pieces, :, low : low + z.extra]
            else:
                for p in range(z.slabs):
                    scales[i, rows, p * 128 : (p + 1) * 128] = a[z.head + (g * z.own + i) * z.slabs + p]
    hits_out[...] = scales[:, :, z.vertices :]
    own_points = gathered[pl.ds(pl.multiple_of(g * z.rows, z.rows), z.rows), :]
    corner = jnp.dot(coarse[...], own_points, preferred_element_type=F32)
    sums_out[...] = jnp.zeros_like(sums_out)
    for i in range(z.corners):
        sums_out[0, pl.ds(table[z.t_corner + i], 1), : z.rhs] = corner[i : i + 1, :]
    flat = scales[:, :, : z.vertices].reshape(z.own * MODES, z.vertices)
    image = ext_in[:, :, z.vertices : z.extra].reshape(z.own * MODES, z.vertices)
    sums_out[0, :, z.rhs : z.rhs + z.vertices] = -0.5 * lax.dot_general(
        flat, image, CONTRACT_FIRST, preferred_element_type=F32
    )
    sums_out[1, :, : z.rhs] = lax.dot_general(
        flat, coeffs[...].astype(BF).reshape(z.own * MODES, z.rhs), CONTRACT_FIRST, preferred_element_type=F32
    )
    if z.near:
        one = to_dense(z, sums_out[0, :, : z.rhs]).astype(BF)
        two = to_dense(z, sums_out[1, :, : z.rhs]).astype(BF)
        blank = jnp.zeros((z.share, z.rhs - z.vertices), F32)
        between = jnp.concatenate([sums_out[0, :, z.rhs : z.rhs + z.vertices], blank], axis=1)
        between = to_dense(z, between).astype(BF)
        for o in outs:
            o[z.own] = one
            o[z.own + 1] = two
            o[z.own + 2] = between


def last_kernel(z, table, *refs):
    n = z.grps
    shares, refs = refs[:n], refs[n:]
    tables, coarse, sums, hits, earlier, start, out, averages, whole, change = refs
    g = lax.axis_index("grp")
    if z.near:
        one, two = from_dense(z, sums[0]), from_dense(z, sums[1])
        between = sums[2, : z.share, : z.vertices]
    else:
        one, two = sums[0, :, : z.rhs], sums[1, :, : z.rhs]
        between = sums[0, :, z.rhs : z.rhs + z.vertices]
    two = two + jnp.dot(between, one, precision=lax.Precision.HIGHEST, preferred_element_type=F32)
    whole[...] = one + two
    high, low = split_two(one)
    flat = hits[...].reshape(z.own * MODES, z.vertices)
    shift = jnp.dot(flat, high, preferred_element_type=F32) + jnp.dot(flat, low, preferred_element_type=F32)
    rows = [whole[pl.ds(table[z.t_corner + i], 1), :] for i in range(z.corners)]
    high, low = split_two(jnp.concatenate(rows, axis=0))
    coarse_corr = lax.dot_general(coarse[...], high, CONTRACT_FIRST, preferred_element_type=F32)
    coarse_corr = coarse_corr + lax.dot_general(coarse[...], low, CONTRACT_FIRST, preferred_element_type=F32)
    for i in range(z.own):
        for j, c in enumerate(shares):
            averages[i, share_rows(z, g ^ j), :] = from_dense(z, c[i].astype(F32))
        rows = slice(i * FPTS, (i + 1) * FPTS)
        fixed = (averages[i] - 0.5 * shift[i * MODES : (i + 1) * MODES, :]).astype(BF)
        table_i = tables_of(tables[i])
        both = lax.dot_general(
            jnp.concatenate([table_i, table_i], axis=0),
            jnp.concatenate([fixed, earlier[i]], axis=0),
            CONTRACT_FIRST,
            preferred_element_type=F32,
        )
        change[rows, :] = both + coarse_corr[rows, :]
    out[...] = start[...] - 0.5 * change[...].T


def paired(blocks):
    count = lax.axis_size("sub")
    assert count % 4 == 0
    pairs = [[], [], [], []]
    for s in range(count):
        pairs[0].append((s, s ^ 1))
        pairs[1].append((s, s ^ 2))
        pairs[2].append((s, (s + (2 if (s // 2) % 2 else -2)) % count))
        pairs[3].append((s, (s + (1 if s % 2 else -1)) % count))
    return [lax.ppermute(b, "sub", p) for b, p in zip(blocks, pairs)] + [blocks[4]]


def swapped(value, mask):
    count = lax.axis_size("grp")
    return lax.ppermute(value, "grp", [(s, s ^ mask) for s in range(count)])


def exchanged(blocks):
    return [blocks[0]] + [swapped(blocks[j], j) for j in range(1, len(blocks))]


def run(schur, rhs, start, project, coarse_basis, owner_of_face, mortar_of_face, mortar_order, subdomain_map, vertex_ids):
    subs, grps = lax.axis_size("sub"), lax.axis_size("grp")
    z = Sizes(subs, grps, schur, project, coarse_basis, rhs)
    shape = jax.ShapeDtypeStruct
    matrix, target, first = schur[0], rhs[0].T, start[0].T

    trace_b = pl.pallas_call(
        functools.partial(narrow_kernel, z),
        out_shape=pltpu.VMEM((z.rhs + z.corners, z.rows), BF),
        in_specs=[HBM] * 2,
        out_specs=VMEM,
        scratch_shapes=[
            pltpu.VMEM((z.rhs, z.rows), F32),
            pltpu.VMEM((z.corners, z.rows), BF),
            pltpu.SemaphoreType.DMA((5,)),
        ],
        compiler_params=pltpu.CompilerParams(vmem_limit_bytes=16 << 20),
    )(*[pltpu.with_memory_space_constraint(a, pltpu.HBM) for a in (first, coarse_basis[0])])
    block_two = swapped(trace_b, 2)
    block_one = swapped(trace_b, 1)

    table = pl.pallas_call(
        functools.partial(table_kernel, z),
        out_shape=pltpu.SMEM((z.t_end,), jnp.int32),
        in_specs=[SMEM] * 5,
        out_specs=SMEM,
        scratch_shapes=[pltpu.SMEM((LINKS,), jnp.int32), pltpu.SMEM((z.faces + 1,), jnp.int32), pltpu.SMEM((LINKS,), jnp.int32)],
    )(owner_of_face.transpose(0, 2, 1), mortar_of_face, mortar_order, subdomain_map, vertex_ids)
    matrix, target = pl.pallas_call(
        load_kernel,
        out_shape=[pltpu.VMEM(matrix.shape, BF), pltpu.VMEM(target.shape, F32)],
        in_specs=[HBM] * 2,
        out_specs=[VMEM] * 2,
        scratch_shapes=[pltpu.SemaphoreType.DMA((2,))],
        compiler_params=pltpu.CompilerParams(vmem_limit_bytes=16 << 20),
    )(*[pltpu.with_memory_space_constraint(a, pltpu.HBM) for a in (matrix, target)])
    pair_shape = shape((z.own, MODES // 2, 2 * FPTS), BF)
    pair_own = call(join_kernel, z, pair_shape, (project[0].reshape(z.own, MODES, FPTS),))
    block_three = swapped(block_two, 1)
    blocks = [trace_b, block_one, block_two, block_three]

    width = z.wide - z.rhs
    part = shape((z.own, z.share, z.wide), BF)
    part_more = shape((z.own + z.more, z.dense, z.lanes), BF)
    link = shape((CAP, z.share, z.wide), BF)
    thin = shape((CAP, z.dense, z.lanes), BF)
    thin_more = shape((CAP + z.more, z.dense, z.lanes), BF)
    sums_shape = shape((2, z.vertices, z.wide), F32)

    *parts, resid, ext = call(
        first_kernel,
        z,
        [part] * grps + [shape((z.rows, z.rhs), F32), shape((z.own, MODES, width), BF)],
        (table, matrix, *blocks, target, pair_own, coarse_basis[0]),
        (
            pltpu.VMEM((z.rhs + z.corners, z.all_rows), BF),
            pltpu.VMEM((z.rows, z.wide), BF),
            pltpu.VMEM((z.own, MODES, z.wide), BF),
        ),
    )
    parts = exchanged(parts)
    outgoing = call(pack_kernel, z, [link] * LINKS, (table, *parts), (pltpu.VMEM((z.faces, z.share, z.wide), BF),), (False,))
    outgoing, pair_own = lax.optimization_barrier((outgoing, pair_own))
    arrived = paired(outgoing)
    pair_two = swapped(pair_own, 2)
    arrived, pair_two = lax.optimization_barrier((arrived, pair_two))
    replies = call(
        average_kernel,
        z,
        [link] * LINKS,
        (table, *arrived),
        (pltpu.VMEM((MORT_OWN + 1, z.share, z.wide), F32), pltpu.VMEM((MORT_OWN + 1, z.share, z.wide), BF)),
        (False,),
    )
    replies, pair_own, pair_two = lax.optimization_barrier((replies, pair_own, pair_two))
    answered = paired(replies)
    pair_one, pair_three = swapped(pair_own, 1), swapped(pair_two, 1)
    answered, pair_one, pair_three = lax.optimization_barrier((answered, pair_one, pair_three))
    spread = call(
        spread_first,
        z,
        shape((z.packed, z.share, z.lanes), BF),
        (table, *answered),
        (pltpu.VMEM((SLOTS, z.share, z.wide), BF),),
    )
    spread_two = swapped(spread, 2)
    shares = [spread, swapped(spread, 1), spread_two, swapped(spread_two, 1)]
    tables = call(
        unpack_kernel, z, shape((z.faces, MODES, FPTS), BF), (pair_own, pair_one, pair_two, pair_three)
    )
    *parts, earlier, hits, sums = call(
        second_kernel,
        z,
        [part_more] * grps
        + [shape((z.own, MODES, z.rhs), BF), shape((z.own, MODES, z.vertices), BF), sums_shape],
        (table, matrix, *shares, tables, resid, coarse_basis[0], ext),
        (
            pltpu.VMEM((z.faces, MODES, z.rhs), BF),
            pltpu.VMEM((z.all_rows, z.rhs), BF),
            pltpu.VMEM((z.rows, z.rhs), BF),
            pltpu.VMEM((z.own, MODES, z.rhs), F32),
            pltpu.VMEM((z.own, MODES, z.extra), BF),
        ),
    )
    if not z.near:
        sums = lax.psum(sums, ("sub", "grp"))
    parts = exchanged(parts)
    outgoing = call(
        pack_kernel, z, [thin_more] * LINKS, (table, *parts), (pltpu.VMEM((z.faces, z.dense, z.lanes), BF),), (z.near,)
    )
    arrived = paired(outgoing)
    total_shape = [shape((z.more, z.dense, z.lanes), F32)] if z.near else []
    results = call(
        average_kernel,
        z,
        [thin, thin_more, thin_more, thin, thin] + total_shape,
        (table, *arrived),
        (pltpu.VMEM((MORT_OWN + 1, z.dense, z.lanes), F32), pltpu.VMEM((MORT_OWN + 1, z.dense, z.lanes), BF)),
        (True,),
    )
    answered = paired(results[:LINKS])
    outs = call(
        spread_second,
        z,
        [shape((z.own, z.dense, z.lanes), BF)] * grps + total_shape,
        (table, *answered, *results[LINKS:]),
        (pltpu.VMEM((SLOTS, z.dense, z.lanes), BF),),
    )
    if z.near:
        sums = outs[grps]
    shares = exchanged(outs[:grps])
    result = call(
        last_kernel,
        z,
        shape((z.rhs, z.rows), F32),
        (table, *shares, pair_own, coarse_basis[0], sums, hits, earlier, first),
        (
            pltpu.VMEM((z.own, MODES, z.rhs), F32),
            pltpu.VMEM((z.vertices, z.rhs), F32),
            pltpu.VMEM((z.rows, z.rhs), F32),
        ),
    )
    return result.T[None]


def solution(mesh):
    return jax.shard_map(
        run,
        mesh=mesh,
        in_specs=(
            P("sub", "grp", None),
            P("sub", "grp", None),
            P("sub", "grp", None),
            P("sub", "grp", None),
            P("sub", None, "grp"),
            P(),
            P(),
            P(),
            P(),
            P(),
        ),
        out_specs=P("sub", "grp", None),
        check_vma=False,
    )
```

```python
import functools

import jax
import jax.numpy as jnp
from jax import lax
from jax.experimental import pallas as pl
from jax.experimental.pallas import tpu as pltpu
from jax.sharding import PartitionSpec as P

DEG = 8
MODES = 64
FPTS = 64
MORT_OWN = 16
REACH = 2
CAP = 8
LINKS = 2 * REACH + 1
SLOTS = LINKS * CAP

BF = jnp.bfloat16
F32 = jnp.float32
CONTRACT_FIRST = (((0,), (0,)), ((), ()))
CONTRACT_LAST = (((1,), (1,)), ((), ()))
VMEM = pl.BlockSpec(memory_space=pltpu.VMEM)
SMEM = pl.BlockSpec(memory_space=pltpu.SMEM)
HBM = pl.BlockSpec(memory_space=pltpu.HBM)


def split_two(value):
    high = value.astype(BF)
    return high, (value - high.astype(F32)).astype(BF)


class Sizes:
    def __init__(self, subs, grps, schur, project, coarse_basis, rhs):
        self.subs = subs
        self.grps = grps
        self.rows = schur.shape[1]
        self.all_rows = schur.shape[2]
        self.own = project.shape[1]
        self.faces = self.own * grps
        self.corners = coarse_basis.shape[1]
        self.rhs = rhs.shape[2]
        self.vertices = 2 * subs
        self.share = MODES // grps
        self.extra = 2 * self.vertices
        self.wide = -(-(self.rhs + self.extra) // 128) * 128
        self.lanes = self.rhs // 128 * 128
        self.tail = self.rhs - self.lanes
        self.missing = range(REACH + 1, subs - REACH)
        self.near = self.vertices == self.share and LINKS <= subs and len(self.missing) <= 3 <= grps
        self.more = 1 if self.near else 0
        self.dense = self.share * self.rhs // self.lanes
        self.pieces = max(1, 128 // self.extra)
        self.slabs = max(1, self.extra // 128)
        self.head = self.faces + self.faces * self.tail // self.lanes
        self.packed = self.head + self.faces * self.slabs // self.pieces
        self.t_src = 0
        self.t_arr = SLOTS
        self.t_slot = 2 * SLOTS
        self.t_count = self.t_slot + self.faces
        self.t_order = self.t_count + MORT_OWN
        self.t_corner = self.t_order + MORT_OWN
        self.t_end = self.t_corner + self.corners


def call(kernel, sizes, outs, args, scratch=(), static=()):
    single = not isinstance(outs, list)
    outs = [outs] if single else outs
    ins = [SMEM if a.dtype == jnp.int32 else VMEM for a in args]
    args = [
        pltpu.with_memory_space_constraint(a, pltpu.SMEM if a.dtype == jnp.int32 else pltpu.VMEM) for a in args
    ]
    results = pl.pallas_call(
        functools.partial(kernel, sizes, *static),
        out_shape=[pltpu.VMEM(o.shape, o.dtype) for o in outs],
        in_specs=ins,
        out_specs=[VMEM for _ in outs],
        scratch_shapes=list(scratch),
        compiler_params=pltpu.CompilerParams(vmem_limit_bytes=16 << 20),
    )(*args)
    return results[0] if single else results


def meeting_of(link, s):
    odd, high = s % 2 == 1, (s // 2) % 2 == 1
    if link == REACH:
        return 4
    if abs(link - REACH) == 1:
        return jnp.where(odd == (link < REACH), 0, 3)
    return jnp.where(high == (link < REACH), 1, 2)


def table_kernel(z, owner, mortar, order, smap, vids, table, used, names, met):
    s = lax.axis_index("sub")
    g = lax.axis_index("grp")
    d = smap[s]
    for i in range(SLOTS):
        table[z.t_src + i] = 0
    for i in range(LINKS):
        used[i] = 0
        met[i] = jnp.int32(meeting_of(i, s))
    for i in range(MORT_OWN):
        table[z.t_count + i] = 0
        table[z.t_order + i] = order[s, i]
    for i in range(z.corners):
        table[z.t_corner + i] = vids[d, i]
    for f in range(z.faces):
        o = owner[d, 0, f]
        r = used[o]
        used[o] = r + 1
        slot = met[o] * CAP + r
        table[z.t_slot + f] = slot
        table[z.t_src + slot] = ((f // z.own) ^ g) * z.own + f % z.own
    for link in range(LINKS):
        dd = smap[lax.rem(s - link + REACH + z.subs, z.subs)]
        r = jnp.int32(0)
        for f in range(z.faces):
            hit = (owner[dd, 0, f] == link).astype(jnp.int32)
            m = mortar[dd, f]
            names[r] = m
            table[z.t_count + m] = table[z.t_count + m] + hit
            r = r + hit
        for i in range(CAP):
            table[z.t_arr + met[2 * REACH - link] * CAP + i] = jnp.where(i < r, names[i], MORT_OWN)


def narrow_kernel(z, start, coarse, out, held, basis, sems):
    pieces = 4
    size = z.rhs // pieces
    copies = [
        pltpu.make_async_copy(start.at[pl.ds(i * size, size)], held.at[pl.ds(i * size, size)], sems.at[i])
        for i in range(pieces)
    ]
    copies.append(pltpu.make_async_copy(coarse, basis, sems.at[pieces]))
    for c in copies:
        c.start()
    for i in range(pieces):
        copies[i].wait()
        out[i * size : (i + 1) * size, :] = held[i * size : (i + 1) * size, :].astype(BF)
    copies[pieces].wait()
    out[z.rhs :, :] = basis[...]


def mode_at(place):
    half = MODES // 2
    return jnp.where(place < half, 2 * place, 2 * (place - half) + 1)


def unpacked(z, raw, rows):
    half = MODES // 2
    value = raw[...].astype(F32)
    for i in range(half):
        rows[pl.ds(i, z.own, stride=half), :] = value[:, i * 2 * FPTS : (i + 1) * 2 * FPTS]
    tables = []
    for f in range(z.own):
        pair = rows[f * half : (f + 1) * half, :]
        tables.append(jnp.concatenate([pair[:, :FPTS], pair[:, FPTS:]], axis=0).astype(BF))
    return tables


def load_kernel(z, schur, rhs, coarse, project, schur_out, rhs_out, coarse_out, tables, raw, rows, sems):
    pairs = ((project, raw), (rhs, rhs_out), (coarse, coarse_out), (schur, schur_out))
    copies = [pltpu.make_async_copy(a, b, sems.at[i]) for i, (a, b) in enumerate(pairs)]
    for c in copies:
        c.start()
    copies[0].wait()
    for f, value in enumerate(unpacked(z, raw, rows)):
        tables[f] = value
    for c in copies[1:]:
        c.wait()


def two_blocks(one, two):
    blank = jnp.zeros_like(one)
    return jnp.concatenate(
        [jnp.concatenate([one, blank], axis=1), jnp.concatenate([blank, two], axis=1)], axis=0
    )


def mix_kernel(z, schur, t0, r1, r2, r3, out, middle, rows):
    g = lax.axis_index("grp")
    width = 2 * FPTS
    for j, r in enumerate((None, r1, r2, r3)):
        t = unpacked(z, r, rows) if j else t0
        for i in range(0, z.own, 2):
            at = pl.ds(pl.multiple_of(((g ^ j) * z.own + i) * FPTS, width), width)
            pair = two_blocks(t[i], t[i + 1])
            middle[:, at] = lax.dot_general(
                schur[:, at], pair, CONTRACT_LAST, preferred_element_type=F32
            ).astype(BF)
    for i in range(0, z.own, 2):
        two = slice(i * MODES, (i + 2) * MODES)
        out[two, :] = jnp.dot(
            two_blocks(t0[i], t0[i + 1]), middle[two, :], preferred_element_type=F32
        ).astype(BF)


def share_rows(z, member):
    return pl.ds(pl.multiple_of(member * z.share, z.share), z.share)


def hot_rows(z, table, width, shift):
    column = lax.broadcasted_iota(jnp.int32, (1, width), 1)
    rows = [jnp.where(column == table[z.t_corner + i] + shift, 1.0, 0.0) for i in range(z.corners)]
    return jnp.concatenate(rows, axis=0).astype(BF)


def first_kernel(z, table, schur, b0, b1, b2, b3, rhs, tables, coarse, o0, o1, o2, o3, wide_out, ext_out, gathered, held, coeffs):
    g = lax.axis_index("grp")
    for j, b in enumerate((b0, b1, b2, b3)):
        gathered[:, pl.ds(pl.multiple_of((g ^ j) * z.rows, z.rows), z.rows)] = b[...]
    product = lax.dot_general(schur[...], gathered[...], CONTRACT_LAST, preferred_element_type=F32)
    residual = product[:, : z.rhs] - rhs[...].T
    held[:, : z.rhs] = residual.astype(BF)
    width = z.wide - z.rhs
    basis = lax.dot_general(coarse[...], hot_rows(z, table, width, 0), CONTRACT_FIRST, preferred_element_type=F32)
    image = jnp.dot(
        product[:, z.rhs :].astype(BF), hot_rows(z, table, width, z.vertices), preferred_element_type=F32
    )
    held[:, z.rhs :] = (basis + image).astype(BF)
    for f in range(z.own):
        value = jnp.dot(tables[f], held[f * FPTS : (f + 1) * FPTS, :], preferred_element_type=F32)
        wide_out[f * MODES : (f + 1) * MODES, :] = value[:, : z.rhs]
        coeffs[f] = value.astype(BF)
    ext_out[...] = coeffs[:, :, z.rhs :]
    for j, o in enumerate((o0, o1, o2, o3)):
        for f in range(z.own):
            o[f] = coeffs[f, share_rows(z, g ^ j), :]


def pack_kernel(z, sums, table, c0, c1, c2, c3, o0, o1, o2, o3, o4, data):
    parts = (c0, c1, c2, c3)
    for j, c in enumerate(parts):
        data[j * z.own : (j + 1) * z.own] = c[: z.own]
    for k, o in enumerate((o0, o1, o2, o3, o4)):
        for i in range(CAP):
            o[i] = data[table[z.t_src + k * CAP + i]]
    if sums:
        value = sum((c[z.own :].astype(F32) for c in parts[1:]), parts[0][z.own :].astype(F32)).astype(BF)
        for o in (o0, o1, o2, o3, o4):
            o[CAP:] = value


def average_kernel(z, dense, table, *refs):
    arrivals, refs = refs[:LINKS], refs[LINKS:]
    replies, refs = refs[:LINKS], refs[LINKS:]
    near, total, held = refs if dense and z.near else (None, *refs)
    g = lax.axis_index("grp")
    total[...] = jnp.zeros_like(total)
    for k, a in enumerate(arrivals):
        for i in range(CAP):
            m = table[z.t_arr + k * CAP + i]
            total[m] = total[m] + a[i].astype(F32)
    shape = total.shape[1:]
    row = lax.broadcasted_iota(jnp.int32, shape, 0)
    if dense:
        column = lax.broadcasted_iota(jnp.int32, shape, 1)
        half = z.share // 2
        row = jnp.where(row < z.share, row, row - z.share + jnp.where(column < z.tail, 0, half))
    mode = mode_at(g * z.share + row)
    degree = jnp.maximum(mode // DEG, mode % DEG)
    for k in range(MORT_OWN):
        divisor = jnp.maximum(table[z.t_count + k], 1).astype(F32)
        kept = jnp.where(degree <= table[z.t_order + k], 1.0, 0.0)
        held[k] = (total[k] / divisor * kept).astype(BF)
    held[MORT_OWN] = jnp.zeros_like(held[MORT_OWN])
    for k, o in enumerate(replies):
        for i in range(CAP):
            o[i] = held[table[z.t_arr + k * CAP + i]]
    if dense and z.near:
        s = lax.axis_index("sub")
        odd, high = s % 2 == 1, (s // 2) % 2 == 1
        inner_one, inner_two, outer_two, outer_one, own = [a[CAP:].astype(F32) for a in arrivals]
        near[...] = own + inner_one + inner_two + outer_two + outer_one
        after = jnp.where(odd, outer_one, inner_one)
        before = jnp.where(odd, inner_one, outer_one)
        after_two = jnp.where(high, outer_two, inner_two)
        behind = after * (1.0 if len(z.missing) > 0 else 0.0)
        if len(z.missing) > 1:
            behind = behind + after_two
        ahead = before * (1.0 if len(z.missing) > 2 else 0.0)
        replies[1][CAP:] = jnp.where(high, behind, ahead).astype(BF)
        replies[2][CAP:] = jnp.where(high, ahead, behind).astype(BF)


def spread_first(z, table, *refs):
    blocks, out, data = refs[:LINKS], refs[-2], refs[-1]
    for link, b in enumerate(blocks):
        data[link * CAP : (link + 1) * CAP] = b[:CAP]
    half = z.own // 2
    for f in range(z.faces):
        out[f] = data[table[z.t_slot + f], :, : z.lanes]
    for member in range(z.grps):
        for i in range(half):
            f = member * z.own + i
            left = data[table[z.t_slot + f], :, z.lanes : z.rhs]
            right = data[table[z.t_slot + f + half], :, z.lanes : z.rhs]
            out[z.faces + member * half + i] = jnp.concatenate([left, right], axis=1)
    if z.pieces > 1:
        for p in range(z.faces // z.pieces):
            ends = [data[table[z.t_slot + p * z.pieces + i], :, z.rhs : z.rhs + z.extra] for i in range(z.pieces)]
            out[z.head + p] = jnp.concatenate(ends, axis=1)
    else:
        for f in range(z.faces):
            for p in range(z.slabs):
                at = z.rhs + p * 128
                out[z.head + f * z.slabs + p] = data[table[z.t_slot + f], :, at : at + 128]


def spread_second(z, table, *refs):
    n = LINKS + (1 if z.near else 0)
    blocks, near = refs[:LINKS], refs[LINKS:n]
    outs, data = refs[n : n + z.grps], refs[-1]
    g = lax.axis_index("grp")
    for k, b in enumerate(blocks):
        data[k * CAP : (k + 1) * CAP] = b[:CAP]
    for j, o in enumerate(outs):
        for i in range(z.own):
            o[i] = data[table[z.t_slot + (g ^ j) * z.own + i]]
    if z.near:
        value = (near[0][...] + blocks[1][CAP:].astype(F32) + blocks[2][CAP:].astype(F32)).astype(BF)
        for o in outs:
            o[z.own :] = value


def to_dense(z, value):
    half = z.share // 2
    tail = jnp.concatenate([value[:half, z.lanes :], value[half:, z.lanes :]], axis=1)
    return jnp.concatenate([value[:, : z.lanes], tail], axis=0)


def from_dense(z, value):
    tail = value[z.share :]
    tail = jnp.concatenate([tail[:, : z.tail], tail[:, z.tail :]], axis=0)
    return jnp.concatenate([value[: z.share], tail], axis=1)


def second_kernel(z, table, mixed, *refs):
    n = z.grps
    shares, refs = refs[:n], refs[n:]
    earlier, ext_in, refs = refs[0], refs[1], refs[2:]
    outs, refs = refs[:n], refs[n:]
    own_out, hits_out, sums_out, averages, coeffs, scales = refs
    g = lax.axis_index("grp")
    half = z.own // 2
    for f in range(z.faces):
        member, i = f // z.own, f % z.own
        for jj, a in enumerate(shares):
            rows = pl.ds(pl.multiple_of(f * MODES + (g ^ jj) * z.share, z.share), z.share)
            averages[rows, : z.lanes] = a[f]
            low = (i // half) * z.tail
            averages[rows, z.lanes :] = a[z.faces + member * half + i % half, :, low : low + z.tail]
    coeffs[...] = earlier[...] - 0.5 * jnp.dot(mixed[...], averages[...], preferred_element_type=F32)
    for j, o in enumerate(outs):
        for f in range(z.own):
            rows = pl.ds(pl.multiple_of(f * MODES + (g ^ j) * z.share, z.share), z.share)
            o[f] = to_dense(z, coeffs[rows, :]).astype(BF)
    own = averages[pl.ds(pl.multiple_of(g * z.rows, z.rows), z.rows), :]
    own_out[...] = own
    for i in range(z.own):
        for jj, a in enumerate(shares):
            rows = pl.ds(pl.multiple_of(i * MODES + (g ^ jj) * z.share, z.share), z.share)
            if z.pieces > 1:
                low = (i % z.pieces) * z.extra
                scales[rows, :] = a[z.head + (g * z.own + i) // z.pieces, :, low : low + z.extra]
            else:
                for p in range(z.slabs):
                    scales[rows, p * 128 : (p + 1) * 128] = a[z.head + (g * z.own + i) * z.slabs + p]
    hits_out[...] = scales[:, z.vertices :]
    flat = scales[:, : z.vertices]
    ext = ext_in[...].reshape(z.own * MODES, z.wide - z.rhs)
    one = lax.dot_general(ext[:, : z.vertices], own, CONTRACT_FIRST, preferred_element_type=F32)
    two = lax.dot_general(flat, coeffs[...].astype(BF), CONTRACT_FIRST, preferred_element_type=F32)
    between = lax.dot_general(flat, ext[:, z.vertices : z.extra], CONTRACT_FIRST, preferred_element_type=F32)
    between = -0.5 * between
    if z.near:
        blank = jnp.zeros((z.share, z.rhs - z.vertices), F32)
        between = jnp.concatenate([between, blank], axis=1)
        sums_out[0] = to_dense(z, one).astype(BF)
        sums_out[1] = to_dense(z, two).astype(BF)
        sums_out[2] = to_dense(z, between).astype(BF)
        for i in range(3, n):
            sums_out[i] = jnp.zeros_like(sums_out[i])
        for j, o in enumerate(outs):
            o[z.own] = sums_out[g ^ j]
    else:
        sums_out[...] = jnp.zeros_like(sums_out)
        sums_out[0, :, : z.rhs] = one
        sums_out[0, :, z.rhs : z.rhs + z.vertices] = between
        sums_out[1, :, : z.rhs] = two


def last_kernel(z, table, *refs):
    n = z.grps
    shares, refs = refs[:n], refs[n:]
    tables, coarse, sums, hits, earlier, start, out, averages, whole, gained, done, sems = refs
    g = lax.axis_index("grp")
    if z.near:
        for j, c in enumerate(shares):
            gained[g ^ j] = c[z.own]
        one, two = from_dense(z, gained[0].astype(F32)), from_dense(z, gained[1].astype(F32))
        between = gained[2, : z.share, : z.vertices].astype(F32)
    else:
        one, two = sums[0, :, : z.rhs], sums[1, :, : z.rhs]
        between = sums[0, :, z.rhs : z.rhs + z.vertices]
    two = two + jnp.dot(between, one, precision=lax.Precision.HIGHEST, preferred_element_type=F32)
    whole[...] = one + two
    high, low = split_two(one)
    flat = hits[...]
    shift = jnp.dot(flat, high, preferred_element_type=F32) + jnp.dot(flat, low, preferred_element_type=F32)
    rows = [whole[pl.ds(table[z.t_corner + i], 1), :] for i in range(z.corners)]
    high, low = split_two(jnp.concatenate(rows, axis=0))
    coarse_corr = lax.dot_general(coarse[...], high, CONTRACT_FIRST, preferred_element_type=F32)
    coarse_corr = coarse_corr + lax.dot_general(coarse[...], low, CONTRACT_FIRST, preferred_element_type=F32)
    copies = []
    change = []
    for i in range(z.own):
        for j, c in enumerate(shares):
            averages[i, share_rows(z, g ^ j), :] = from_dense(z, c[i].astype(F32))
        rows = slice(i * MODES, (i + 1) * MODES)
        fixed = (averages[i] - 0.5 * shift[rows, :]).astype(BF)
        both = lax.dot_general(
            jnp.concatenate([tables[i], tables[i]], axis=0),
            jnp.concatenate([fixed, earlier[rows, :]], axis=0),
            CONTRACT_FIRST,
            preferred_element_type=F32,
        )
        change.append(both + coarse_corr[i * FPTS : (i + 1) * FPTS, :])
        if i % 2:
            at = pl.ds((i - 1) * FPTS, 2 * FPTS)
            done[:, at] = start[:, at] - 0.5 * jnp.concatenate(change, axis=0).T
            copies.append(pltpu.make_async_copy(done.at[:, at], out.at[:, at], sems.at[i // 2]))
            copies[-1].start()
            change = []
    for c in copies:
        c.wait()


def paired(blocks):
    count = lax.axis_size("sub")
    assert count % 4 == 0
    pairs = [[], [], [], []]
    for s in range(count):
        pairs[0].append((s, s ^ 1))
        pairs[1].append((s, s ^ 2))
        pairs[2].append((s, (s + (2 if (s // 2) % 2 else -2)) % count))
        pairs[3].append((s, (s + (1 if s % 2 else -1)) % count))
    met = []
    for k, p in enumerate(pairs):
        met.append(lax.ppermute(blocks[k], "sub", p))
    return [*met, blocks[4]]


def swapped(value, mask):
    count = lax.axis_size("grp")
    return lax.ppermute(value, "grp", [(s, s ^ mask) for s in range(count)])


def hypercube(value):
    two = swapped(value, 2)
    one = swapped(value, 1)
    return [value, one, two, swapped(two, 1)]


def exchanged(blocks):
    return [blocks[0]] + [swapped(blocks[j], j) for j in range(1, len(blocks))]


def run(schur, rhs, start, project, coarse_basis, owner_of_face, mortar_of_face, mortar_order, subdomain_map, vertex_ids):
    subs, grps = lax.axis_size("sub"), lax.axis_size("grp")
    z = Sizes(subs, grps, schur, project, coarse_basis, rhs)
    shape = jax.ShapeDtypeStruct
    matrix, target, first = schur[0], rhs[0].T, start[0].T

    trace_b = pl.pallas_call(
        functools.partial(narrow_kernel, z),
        out_shape=pltpu.VMEM((z.rhs + z.corners, z.rows), BF),
        in_specs=[HBM] * 2,
        out_specs=VMEM,
        scratch_shapes=[
            pltpu.VMEM((z.rhs, z.rows), F32),
            pltpu.VMEM((z.corners, z.rows), BF),
            pltpu.SemaphoreType.DMA((5,)),
        ],
        compiler_params=pltpu.CompilerParams(vmem_limit_bytes=16 << 20),
    )(*[pltpu.with_memory_space_constraint(a, pltpu.HBM) for a in (first, coarse_basis[0])])
    block_two = swapped(trace_b, 2)
    pair_two = swapped(project[0], 2)
    block_one = swapped(trace_b, 1)

    table = pl.pallas_call(
        functools.partial(table_kernel, z),
        out_shape=pltpu.SMEM((z.t_end,), jnp.int32),
        in_specs=[SMEM] * 5,
        out_specs=SMEM,
        scratch_shapes=[pltpu.SMEM((LINKS,), jnp.int32), pltpu.SMEM((z.faces + 1,), jnp.int32), pltpu.SMEM((LINKS,), jnp.int32)],
    )(owner_of_face.transpose(0, 2, 1), mortar_of_face, mortar_order, subdomain_map, vertex_ids)
    loaded = [matrix, target, coarse_basis[0]]
    matrix, target, coarse, own_tables = pl.pallas_call(
        functools.partial(load_kernel, z),
        out_shape=[pltpu.VMEM(a.shape, a.dtype) for a in loaded] + [pltpu.VMEM((z.own, MODES, FPTS), BF)],
        in_specs=[HBM] * 4,
        out_specs=[VMEM] * 4,
        scratch_shapes=[
            pltpu.VMEM((z.own, MODES * FPTS), BF),
            pltpu.VMEM((z.own * MODES // 2, 2 * FPTS), F32),
            pltpu.SemaphoreType.DMA((4,)),
        ],
        compiler_params=pltpu.CompilerParams(vmem_limit_bytes=4 << 20),
    )(*[pltpu.with_memory_space_constraint(a, pltpu.HBM) for a in (*loaded, project[0])])
    block_three = swapped(block_two, 1)
    blocks = [trace_b, block_one, block_two, block_three]

    width = z.wide - z.rhs
    part = shape((z.own, z.share, z.wide), BF)
    part_more = shape((z.own + z.more, z.dense, z.lanes), BF)
    link = shape((CAP, z.share, z.wide), BF)
    thin = shape((CAP, z.dense, z.lanes), BF)
    thin_more = shape((CAP + z.more, z.dense, z.lanes), BF)
    sums_shape = shape((grps, z.dense, z.lanes), BF) if z.near else shape((2, z.vertices, z.wide), F32)

    *parts, wide, ext = call(
        first_kernel,
        z,
        [part] * grps + [shape((z.own * MODES, z.rhs), F32), shape((z.own, MODES, width), BF)],
        (table, matrix, *blocks, target, own_tables, coarse),
        (
            pltpu.VMEM((z.rhs + z.corners, z.all_rows), BF),
            pltpu.VMEM((z.rows, z.wide), BF),
            pltpu.VMEM((z.own, MODES, z.wide), BF),
        ),
    )
    part_one = swapped(parts[1], 1)
    part_two = swapped(parts[2], 2)
    part_three = swapped(parts[3], 3)
    parts = [parts[0], part_one, part_two, part_three]
    pair_one = swapped(project[0], 1)
    pair_three = swapped(pair_two, 1)
    outgoing = call(pack_kernel, z, [link] * LINKS, (table, *parts), (pltpu.VMEM((z.faces, z.share, z.wide), BF),), (False,))
    arrived = paired(outgoing)
    arrived, pair_one, pair_two, pair_three = lax.optimization_barrier((arrived, pair_one, pair_two, pair_three))
    replies = call(
        average_kernel,
        z,
        [link] * LINKS,
        (table, *arrived),
        (pltpu.VMEM((MORT_OWN + 1, z.share, z.wide), F32), pltpu.VMEM((MORT_OWN + 1, z.share, z.wide), BF)),
        (False,),
    )
    answered = paired(replies)
    mixed = call(
        mix_kernel,
        z,
        shape((z.rows, z.all_rows), BF),
        (matrix, own_tables, pair_one, pair_two, pair_three),
        (pltpu.VMEM((z.rows, z.all_rows), BF), pltpu.VMEM((z.own * MODES // 2, 2 * FPTS), F32)),
    )
    spread = call(
        spread_first,
        z,
        shape((z.packed, z.share, z.lanes), BF),
        (table, *answered),
        (pltpu.VMEM((SLOTS, z.share, z.wide), BF),),
    )
    shares = hypercube(spread)
    *parts, earlier, hits, sums = call(
        second_kernel,
        z,
        [part_more] * grps
        + [shape((z.rows, z.rhs), BF), shape((z.own * MODES, z.vertices), BF), sums_shape],
        (table, mixed, *shares, wide, ext),
        (
            pltpu.VMEM((z.all_rows, z.rhs), BF),
            pltpu.VMEM((z.rows, z.rhs), F32),
            pltpu.VMEM((z.own * MODES, z.extra), BF),
        ),
    )
    if not z.near:
        sums = lax.psum(sums, ("sub", "grp"))
    parts = exchanged(parts)
    outgoing = call(
        pack_kernel, z, [thin_more] * LINKS, (table, *parts), (pltpu.VMEM((z.faces, z.dense, z.lanes), BF),), (z.near,)
    )
    arrived = paired(outgoing)
    total_shape = [shape((z.more, z.dense, z.lanes), F32)] if z.near else []
    results = call(
        average_kernel,
        z,
        [thin, thin_more, thin_more, thin, thin] + total_shape,
        (table, *arrived),
        (pltpu.VMEM((MORT_OWN + 1, z.dense, z.lanes), F32), pltpu.VMEM((MORT_OWN + 1, z.dense, z.lanes), BF)),
        (True,),
    )
    answered = paired(results[:LINKS])
    outs = call(
        spread_second,
        z,
        [part_more] * grps,
        (table, *answered, *results[LINKS:]),
        (pltpu.VMEM((SLOTS, z.dense, z.lanes), BF),),
    )
    shares = exchanged(outs)
    inputs = (table, *shares, own_tables, coarse, sums, hits, earlier, first)
    result = pl.pallas_call(
        functools.partial(last_kernel, z),
        out_shape=pltpu.HBM((z.rhs, z.rows), F32),
        in_specs=[SMEM] + [VMEM] * (len(inputs) - 1),
        out_specs=HBM,
        scratch_shapes=[
            pltpu.VMEM((z.own, MODES, z.rhs), F32),
            pltpu.VMEM((z.vertices, z.rhs), F32),
            pltpu.VMEM((grps, z.dense, z.lanes), BF),
            pltpu.VMEM((z.rhs, z.rows), F32),
            pltpu.SemaphoreType.DMA((z.own // 2,)),
        ],
        compiler_params=pltpu.CompilerParams(vmem_limit_bytes=16 << 20),
    )(
        *[
            pltpu.with_memory_space_constraint(a, pltpu.SMEM if a.dtype == jnp.int32 else pltpu.VMEM)
            for a in inputs
        ]
    )
    return result.T[None]


def solution(mesh):
    return jax.shard_map(
        run,
        mesh=mesh,
        in_specs=(
            P("sub", "grp", None),
            P("sub", "grp", None),
            P("sub", "grp", None),
            P("sub", "grp", None),
            P("sub", None, "grp"),
            P(),
            P(),
            P(),
            P(),
            P(),
        ),
        out_specs=P("sub", "grp", None),
        check_vma=False,
    )
```

```python
import functools

import jax
import jax.numpy as jnp
from jax import lax
from jax.experimental import pallas as pl
from jax.experimental.pallas import tpu as pltpu
from jax.sharding import PartitionSpec as P

DEG = 8
MODES = 64
FPTS = 64
MORT_OWN = 16
REACH = 2
CAP = 8
LINKS = 2 * REACH + 1
SLOTS = LINKS * CAP

BF = jnp.bfloat16
F32 = jnp.float32
CONTRACT_FIRST = (((0,), (0,)), ((), ()))
CONTRACT_LAST = (((1,), (1,)), ((), ()))
VMEM = pl.BlockSpec(memory_space=pltpu.VMEM)
SMEM = pl.BlockSpec(memory_space=pltpu.SMEM)
HBM = pl.BlockSpec(memory_space=pltpu.HBM)


def split_two(value):
    high = value.astype(BF)
    return high, (value - high.astype(F32)).astype(BF)


class Sizes:
    def __init__(self, subs, grps, schur, project, coarse_basis, rhs):
        self.subs = subs
        self.grps = grps
        self.rows = schur.shape[1]
        self.all_rows = schur.shape[2]
        self.own = project.shape[1]
        self.faces = self.own * grps
        self.corners = coarse_basis.shape[1]
        self.rhs = rhs.shape[2]
        self.vertices = 2 * subs
        self.share = MODES // grps
        self.extra = 2 * self.vertices
        self.wide = -(-(self.rhs + self.extra) // 128) * 128
        self.lanes = self.rhs // 128 * 128
        self.tail = self.rhs - self.lanes
        self.missing = range(REACH + 1, subs - REACH)
        self.near = self.vertices == self.share and LINKS <= subs and len(self.missing) <= 3 <= grps
        self.more = 1 if self.near else 0
        self.dense = self.share * self.rhs // self.lanes
        self.pieces = max(1, 128 // self.extra)
        self.slabs = max(1, self.extra // 128)
        self.head = self.faces + self.faces * self.tail // self.lanes
        self.packed = self.head + self.faces * self.slabs // self.pieces
        self.t_src = 0
        self.t_arr = SLOTS
        self.t_slot = 2 * SLOTS
        self.t_count = self.t_slot + self.faces
        self.t_order = self.t_count + MORT_OWN
        self.t_corner = self.t_order + MORT_OWN
        self.t_end = self.t_corner + self.corners


def call(kernel, sizes, outs, args, scratch=(), static=()):
    single = not isinstance(outs, list)
    outs = [outs] if single else outs
    ins = [SMEM if a.dtype == jnp.int32 else VMEM for a in args]
    args = [
        pltpu.with_memory_space_constraint(a, pltpu.SMEM if a.dtype == jnp.int32 else pltpu.VMEM) for a in args
    ]
    results = pl.pallas_call(
        functools.partial(kernel, sizes, *static),
        out_shape=[pltpu.VMEM(o.shape, o.dtype) for o in outs],
        in_specs=ins,
        out_specs=[VMEM for _ in outs],
        scratch_shapes=list(scratch),
        compiler_params=pltpu.CompilerParams(vmem_limit_bytes=16 << 20),
    )(*args)
    return results[0] if single else results


def meeting_of(link, s):
    odd, high = s % 2 == 1, (s // 2) % 2 == 1
    if link == REACH:
        return 4
    if abs(link - REACH) == 1:
        return jnp.where(odd == (link < REACH), 0, 3)
    return jnp.where(high == (link < REACH), 1, 2)


def table_kernel(z, owner, mortar, order, smap, vids, table, used, names, met):
    s = lax.axis_index("sub")
    g = lax.axis_index("grp")
    d = smap[s]
    for i in range(SLOTS):
        table[z.t_src + i] = 0
    for i in range(LINKS):
        used[i] = 0
        met[i] = jnp.int32(meeting_of(i, s))
    for i in range(MORT_OWN):
        table[z.t_count + i] = 0
        table[z.t_order + i] = order[s, i]
    for i in range(z.corners):
        table[z.t_corner + i] = vids[d, i]
    for f in range(z.faces):
        o = owner[d, 0, f]
        r = used[o]
        used[o] = r + 1
        slot = met[o] * CAP + r
        table[z.t_slot + f] = slot
        table[z.t_src + slot] = ((f // z.own) ^ g) * z.own + f % z.own
    for link in range(LINKS):
        dd = smap[lax.rem(s - link + REACH + z.subs, z.subs)]
        r = jnp.int32(0)
        for f in range(z.faces):
            hit = (owner[dd, 0, f] == link).astype(jnp.int32)
            m = mortar[dd, f]
            names[r] = m
            table[z.t_count + m] = table[z.t_count + m] + hit
            r = r + hit
        for i in range(CAP):
            table[z.t_arr + met[2 * REACH - link] * CAP + i] = jnp.where(i < r, names[i], MORT_OWN)


def narrow_kernel(z, start, coarse, out, held, basis, sems):
    pieces = 4
    size = z.rhs // pieces
    copies = [
        pltpu.make_async_copy(start.at[pl.ds(i * size, size)], held.at[pl.ds(i * size, size)], sems.at[i])
        for i in range(pieces)
    ]
    copies.append(pltpu.make_async_copy(coarse, basis, sems.at[pieces]))
    for c in copies:
        c.start()
    for i in range(pieces):
        copies[i].wait()
        out[i * size : (i + 1) * size, :] = held[i * size : (i + 1) * size, :].astype(BF)
    copies[pieces].wait()
    out[z.rhs :, :] = basis[...]


def mode_at(place):
    half = MODES // 2
    return jnp.where(place < half, 2 * place, 2 * (place - half) + 1)


def unpacked(z, raw, rows):
    half = MODES // 2
    value = raw[...].astype(F32)
    for i in range(half):
        rows[pl.ds(i, z.own, stride=half), :] = value[:, i * 2 * FPTS : (i + 1) * 2 * FPTS]
    tables = []
    for f in range(z.own):
        pair = rows[f * half : (f + 1) * half, :]
        tables.append(jnp.concatenate([pair[:, :FPTS], pair[:, FPTS:]], axis=0).astype(BF))
    return tables


def load_kernel(z, schur, rhs, coarse, project, schur_out, rhs_out, coarse_out, tables, raw, rows, sems):
    pairs = ((project, raw), (rhs, rhs_out), (coarse, coarse_out), (schur, schur_out))
    copies = [pltpu.make_async_copy(a, b, sems.at[i]) for i, (a, b) in enumerate(pairs)]
    for c in copies:
        c.start()
    copies[0].wait()
    for f, value in enumerate(unpacked(z, raw, rows)):
        tables[f] = value
    for c in copies[1:]:
        c.wait()


def two_blocks(one, two):
    blank = jnp.zeros_like(one)
    return jnp.concatenate(
        [jnp.concatenate([one, blank], axis=1), jnp.concatenate([blank, two], axis=1)], axis=0
    )


def mix_kernel(z, schur, t0, r1, r2, r3, out, middle, rows):
    g = lax.axis_index("grp")
    width = 2 * FPTS
    for j, r in enumerate((None, r1, r2, r3)):
        t = unpacked(z, r, rows) if j else t0
        for i in range(0, z.own, 2):
            at = pl.ds(pl.multiple_of(((g ^ j) * z.own + i) * FPTS, width), width)
            pair = two_blocks(t[i], t[i + 1])
            middle[:, at] = lax.dot_general(
                schur[:, at], pair, CONTRACT_LAST, preferred_element_type=F32
            ).astype(BF)
    for i in range(0, z.own, 2):
        two = slice(i * MODES, (i + 2) * MODES)
        out[two, :] = jnp.dot(
            two_blocks(t0[i], t0[i + 1]), middle[two, :], preferred_element_type=F32
        ).astype(BF)


def share_rows(z, member):
    return pl.ds(pl.multiple_of(member * z.share, z.share), z.share)


def hot_rows(z, table, width, shift):
    column = lax.broadcasted_iota(jnp.int32, (1, width), 1)
    rows = [jnp.where(column == table[z.t_corner + i] + shift, 1.0, 0.0) for i in range(z.corners)]
    return jnp.concatenate(rows, axis=0).astype(BF)


def block_product(z, schur, block, j):
    g = lax.axis_index("grp")
    at = pl.ds(pl.multiple_of((g ^ j) * z.rows, z.rows), z.rows)
    return lax.dot_general(schur[:, at], block[...], CONTRACT_LAST, preferred_element_type=F32)


def early_kernel(z, schur, b0, rhs, out):
    product = block_product(z, schur, b0, 0)
    out[:, : z.rhs] = product[:, : z.rhs] - rhs[...].T
    out[:, z.rhs :] = product[:, z.rhs :]


def further_kernel(z, j, schur, block, before, out):
    out[...] = before[...] + block_product(z, schur, block, j)


def first_kernel(z, table, schur, b3, before, tables, coarse, o0, o1, o2, o3, wide_out, ext_out, held, coeffs):
    g = lax.axis_index("grp")
    product = before[...] + block_product(z, schur, b3, 3)
    held[:, : z.rhs] = product[:, : z.rhs].astype(BF)
    width = z.wide - z.rhs
    basis = lax.dot_general(coarse[...], hot_rows(z, table, width, 0), CONTRACT_FIRST, preferred_element_type=F32)
    image = jnp.dot(
        product[:, z.rhs :].astype(BF), hot_rows(z, table, width, z.vertices), preferred_element_type=F32
    )
    held[:, z.rhs :] = (basis + image).astype(BF)
    for f in range(z.own):
        value = jnp.dot(tables[f], held[f * FPTS : (f + 1) * FPTS, :], preferred_element_type=F32)
        wide_out[f * MODES : (f + 1) * MODES, :] = value[:, : z.rhs]
        coeffs[f] = value.astype(BF)
    ext_out[...] = coeffs[:, :, z.rhs :]
    for j, o in enumerate((o0, o1, o2, o3)):
        for f in range(z.own):
            o[f] = coeffs[f, share_rows(z, g ^ j), :]


def pack_kernel(z, sums, table, c0, c1, c2, c3, o0, o1, o2, o3, o4, data):
    parts = (c0, c1, c2, c3)
    for j, c in enumerate(parts):
        data[j * z.own : (j + 1) * z.own] = c[: z.own]
    for k, o in enumerate((o0, o1, o2, o3, o4)):
        for i in range(CAP):
            o[i] = data[table[z.t_src + k * CAP + i]]
    if sums:
        value = sum((c[z.own :].astype(F32) for c in parts[1:]), parts[0][z.own :].astype(F32)).astype(BF)
        for o in (o0, o1, o2, o3, o4):
            o[CAP:] = value


def average_kernel(z, dense, table, *refs):
    arrivals, refs = refs[:LINKS], refs[LINKS:]
    replies, refs = refs[:LINKS], refs[LINKS:]
    near, total, held = refs if dense and z.near else (None, *refs)
    g = lax.axis_index("grp")
    total[...] = jnp.zeros_like(total)
    for k, a in enumerate(arrivals):
        for i in range(CAP):
            m = table[z.t_arr + k * CAP + i]
            total[m] = total[m] + a[i].astype(F32)
    shape = total.shape[1:]
    row = lax.broadcasted_iota(jnp.int32, shape, 0)
    if dense:
        column = lax.broadcasted_iota(jnp.int32, shape, 1)
        half = z.share // 2
        row = jnp.where(row < z.share, row, row - z.share + jnp.where(column < z.tail, 0, half))
    mode = mode_at(g * z.share + row)
    degree = jnp.maximum(mode // DEG, mode % DEG)
    for k in range(MORT_OWN):
        divisor = jnp.maximum(table[z.t_count + k], 1).astype(F32)
        kept = jnp.where(degree <= table[z.t_order + k], 1.0, 0.0)
        held[k] = (total[k] / divisor * kept).astype(BF)
    held[MORT_OWN] = jnp.zeros_like(held[MORT_OWN])
    for k, o in enumerate(replies):
        for i in range(CAP):
            o[i] = held[table[z.t_arr + k * CAP + i]]
    if dense and z.near:
        s = lax.axis_index("sub")
        odd, high = s % 2 == 1, (s // 2) % 2 == 1
        inner_one, inner_two, outer_two, outer_one, own = [a[CAP:].astype(F32) for a in arrivals]
        near[...] = own + inner_one + inner_two + outer_two + outer_one
        after = jnp.where(odd, outer_one, inner_one)
        before = jnp.where(odd, inner_one, outer_one)
        after_two = jnp.where(high, outer_two, inner_two)
        behind = after * (1.0 if len(z.missing) > 0 else 0.0)
        if len(z.missing) > 1:
            behind = behind + after_two
        ahead = before * (1.0 if len(z.missing) > 2 else 0.0)
        replies[1][CAP:] = jnp.where(high, behind, ahead).astype(BF)
        replies[2][CAP:] = jnp.where(high, ahead, behind).astype(BF)


def spread_first(z, table, *refs):
    blocks, out, data = refs[:LINKS], refs[-2], refs[-1]
    for link, b in enumerate(blocks):
        data[link * CAP : (link + 1) * CAP] = b[:CAP]
    half = z.own // 2
    for f in range(z.faces):
        out[f] = data[table[z.t_slot + f], :, : z.lanes]
    for member in range(z.grps):
        for i in range(half):
            f = member * z.own + i
            left = data[table[z.t_slot + f], :, z.lanes : z.rhs]
            right = data[table[z.t_slot + f + half], :, z.lanes : z.rhs]
            out[z.faces + member * half + i] = jnp.concatenate([left, right], axis=1)
    if z.pieces > 1:
        for p in range(z.faces // z.pieces):
            ends = [data[table[z.t_slot + p * z.pieces + i], :, z.rhs : z.rhs + z.extra] for i in range(z.pieces)]
            out[z.head + p] = jnp.concatenate(ends, axis=1)
    else:
        for f in range(z.faces):
            for p in range(z.slabs):
                at = z.rhs + p * 128
                out[z.head + f * z.slabs + p] = data[table[z.t_slot + f], :, at : at + 128]


def spread_second(z, table, *refs):
    n = LINKS + (1 if z.near else 0)
    blocks, near = refs[:LINKS], refs[LINKS:n]
    outs, data = refs[n : n + z.grps], refs[-1]
    g = lax.axis_index("grp")
    for k, b in enumerate(blocks):
        data[k * CAP : (k + 1) * CAP] = b[:CAP]
    for j, o in enumerate(outs):
        for i in range(z.own):
            o[i] = data[table[z.t_slot + (g ^ j) * z.own + i]]
    if z.near:
        value = (near[0][...] + blocks[1][CAP:].astype(F32) + blocks[2][CAP:].astype(F32)).astype(BF)
        for o in outs:
            o[z.own :] = value


def to_dense(z, value):
    half = z.share // 2
    tail = jnp.concatenate([value[:half, z.lanes :], value[half:, z.lanes :]], axis=1)
    return jnp.concatenate([value[:, : z.lanes], tail], axis=0)


def from_dense(z, value):
    tail = value[z.share :]
    tail = jnp.concatenate([tail[:, : z.tail], tail[:, z.tail :]], axis=0)
    return jnp.concatenate([value[: z.share], tail], axis=1)


def second_kernel(z, table, mixed, *refs):
    n = z.grps
    shares, refs = refs[:n], refs[n:]
    earlier, ext_in, refs = refs[0], refs[1], refs[2:]
    outs, refs = refs[:n], refs[n:]
    own_out, hits_out, sums_out, averages, coeffs, scales = refs
    g = lax.axis_index("grp")
    half = z.own // 2
    for f in range(z.faces):
        member, i = f // z.own, f % z.own
        for jj, a in enumerate(shares):
            rows = pl.ds(pl.multiple_of(f * MODES + (g ^ jj) * z.share, z.share), z.share)
            averages[rows, : z.lanes] = a[f]
            low = (i // half) * z.tail
            averages[rows, z.lanes :] = a[z.faces + member * half + i % half, :, low : low + z.tail]
    coeffs[...] = earlier[...] - 0.5 * jnp.dot(mixed[...], averages[...], preferred_element_type=F32)
    for j, o in enumerate(outs):
        for f in range(z.own):
            rows = pl.ds(pl.multiple_of(f * MODES + (g ^ j) * z.share, z.share), z.share)
            o[f] = to_dense(z, coeffs[rows, :]).astype(BF)
    own = averages[pl.ds(pl.multiple_of(g * z.rows, z.rows), z.rows), :]
    own_out[...] = own
    for i in range(z.own):
        for jj, a in enumerate(shares):
            rows = pl.ds(pl.multiple_of(i * MODES + (g ^ jj) * z.share, z.share), z.share)
            if z.pieces > 1:
                low = (i % z.pieces) * z.extra
                scales[rows, :] = a[z.head + (g * z.own + i) // z.pieces, :, low : low + z.extra]
            else:
                for p in range(z.slabs):
                    scales[rows, p * 128 : (p + 1) * 128] = a[z.head + (g * z.own + i) * z.slabs + p]
    hits_out[...] = scales[:, z.vertices :]
    flat = scales[:, : z.vertices]
    ext = ext_in[...].reshape(z.own * MODES, z.wide - z.rhs)
    one = lax.dot_general(ext[:, : z.vertices], own, CONTRACT_FIRST, preferred_element_type=F32)
    two = lax.dot_general(flat, coeffs[...].astype(BF), CONTRACT_FIRST, preferred_element_type=F32)
    between = lax.dot_general(flat, ext[:, z.vertices : z.extra], CONTRACT_FIRST, preferred_element_type=F32)
    between = -0.5 * between
    if z.near:
        blank = jnp.zeros((z.share, z.rhs - z.vertices), F32)
        between = jnp.concatenate([between, blank], axis=1)
        sums_out[0] = to_dense(z, one).astype(BF)
        sums_out[1] = to_dense(z, two).astype(BF)
        sums_out[2] = to_dense(z, between).astype(BF)
        for i in range(3, n):
            sums_out[i] = jnp.zeros_like(sums_out[i])
        for j, o in enumerate(outs):
            o[z.own] = sums_out[g ^ j]
    else:
        sums_out[...] = jnp.zeros_like(sums_out)
        sums_out[0, :, : z.rhs] = one
        sums_out[0, :, z.rhs : z.rhs + z.vertices] = between
        sums_out[1, :, : z.rhs] = two


def prior_kernel(z, tables, earlier, start, out):
    for i in range(0, z.own, 2):
        at = slice(i * FPTS, (i + 2) * FPTS)
        pair = two_blocks(tables[i], tables[i + 1])
        lifted = lax.dot_general(
            earlier[i * MODES : (i + 2) * MODES, :], pair, CONTRACT_FIRST, preferred_element_type=F32
        )
        out[:, at] = start[:, at] - 0.5 * lifted


def last_kernel(z, table, *refs):
    n = z.grps
    shares, refs = refs[:n], refs[n:]
    tables, coarse, sums, hits, prior, out, averages, whole, gained, done, sems = refs
    g = lax.axis_index("grp")
    if z.near:
        for j, c in enumerate(shares):
            gained[g ^ j] = c[z.own]
        one, two = from_dense(z, gained[0].astype(F32)), from_dense(z, gained[1].astype(F32))
        between = gained[2, : z.share, : z.vertices].astype(F32)
    else:
        one, two = sums[0, :, : z.rhs], sums[1, :, : z.rhs]
        between = sums[0, :, z.rhs : z.rhs + z.vertices]
    two = two + jnp.dot(between, one, precision=lax.Precision.HIGHEST, preferred_element_type=F32)
    whole[...] = one + two
    high, low = split_two(one)
    flat = hits[...]
    shift = jnp.dot(flat, high, preferred_element_type=F32) + jnp.dot(flat, low, preferred_element_type=F32)
    rows = [whole[pl.ds(table[z.t_corner + i], 1), :] for i in range(z.corners)]
    high, low = split_two(jnp.concatenate(rows, axis=0))
    both = jnp.concatenate([high.astype(F32), low.astype(F32)], axis=0).astype(BF)
    basis = coarse[...].astype(F32)
    basis = jnp.concatenate([basis, basis], axis=0).astype(BF)
    coarse_corr = lax.dot_general(both, basis, CONTRACT_FIRST, preferred_element_type=F32)
    copies = []
    for i in range(0, z.own, 2):
        fixed = []
        for f in (i, i + 1):
            for j, c in enumerate(shares):
                averages[f, share_rows(z, g ^ j), :] = from_dense(z, c[f].astype(F32))
            fixed.append(averages[f] - 0.5 * shift[f * MODES : (f + 1) * MODES, :])
        lifted = lax.dot_general(
            jnp.concatenate(fixed, axis=0).astype(BF),
            two_blocks(tables[i], tables[i + 1]),
            CONTRACT_FIRST,
            preferred_element_type=F32,
        )
        at = slice(i * FPTS, (i + 2) * FPTS)
        done[:, at] = prior[:, at] - 0.5 * (lifted + coarse_corr[:, at])
        at = pl.ds(i * FPTS, 2 * FPTS)
        copies.append(pltpu.make_async_copy(done.at[:, at], out.at[:, at], sems.at[i // 2]))
        copies[-1].start()
    for c in copies:
        c.wait()


def paired(blocks):
    count = lax.axis_size("sub")
    assert count % 4 == 0
    pairs = [[], [], [], []]
    for s in range(count):
        pairs[0].append((s, s ^ 1))
        pairs[1].append((s, s ^ 2))
        pairs[2].append((s, (s + (2 if (s // 2) % 2 else -2)) % count))
        pairs[3].append((s, (s + (1 if s % 2 else -1)) % count))
    met = []
    for k, p in enumerate(pairs):
        met.append(lax.ppermute(blocks[k], "sub", p))
    return [*met, blocks[4]]


def swapped(value, mask):
    count = lax.axis_size("grp")
    return lax.ppermute(value, "grp", [(s, s ^ mask) for s in range(count)])


def exchanged(blocks):
    return [blocks[0]] + [swapped(blocks[j], j) for j in range(1, len(blocks))]


def run(schur, rhs, start, project, coarse_basis, owner_of_face, mortar_of_face, mortar_order, subdomain_map, vertex_ids):
    subs, grps = lax.axis_size("sub"), lax.axis_size("grp")
    z = Sizes(subs, grps, schur, project, coarse_basis, rhs)
    shape = jax.ShapeDtypeStruct
    matrix, target, first = schur[0], rhs[0].T, start[0].T

    trace_b = pl.pallas_call(
        functools.partial(narrow_kernel, z),
        out_shape=pltpu.VMEM((z.rhs + z.corners, z.rows), BF),
        in_specs=[HBM] * 2,
        out_specs=VMEM,
        scratch_shapes=[
            pltpu.VMEM((z.rhs, z.rows), F32),
            pltpu.VMEM((z.corners, z.rows), BF),
            pltpu.SemaphoreType.DMA((5,)),
        ],
        compiler_params=pltpu.CompilerParams(vmem_limit_bytes=16 << 20),
    )(*[pltpu.with_memory_space_constraint(a, pltpu.HBM) for a in (first, coarse_basis[0])])
    block_two = swapped(trace_b, 2)
    block_one = swapped(trace_b, 1)

    table = pl.pallas_call(
        functools.partial(table_kernel, z),
        out_shape=pltpu.SMEM((z.t_end,), jnp.int32),
        in_specs=[SMEM] * 5,
        out_specs=SMEM,
        scratch_shapes=[pltpu.SMEM((LINKS,), jnp.int32), pltpu.SMEM((z.faces + 1,), jnp.int32), pltpu.SMEM((LINKS,), jnp.int32)],
    )(owner_of_face.transpose(0, 2, 1), mortar_of_face, mortar_order, subdomain_map, vertex_ids)
    loaded = [matrix, target, coarse_basis[0]]
    matrix, target, coarse, own_tables = pl.pallas_call(
        functools.partial(load_kernel, z),
        out_shape=[pltpu.VMEM(a.shape, a.dtype) for a in loaded] + [pltpu.VMEM((z.own, MODES, FPTS), BF)],
        in_specs=[HBM] * 4,
        out_specs=[VMEM] * 4,
        scratch_shapes=[
            pltpu.VMEM((z.own, MODES * FPTS), BF),
            pltpu.VMEM((z.own * MODES // 2, 2 * FPTS), F32),
            pltpu.SemaphoreType.DMA((4,)),
        ],
        compiler_params=pltpu.CompilerParams(vmem_limit_bytes=4 << 20),
    )(*[pltpu.with_memory_space_constraint(a, pltpu.HBM) for a in (*loaded, project[0])])
    block_three = swapped(block_two, 1)
    begun_shape = shape((z.rows, z.rhs + z.corners), F32)
    begun = call(early_kernel, z, begun_shape, (matrix, trace_b, target))
    begun, table, raw = lax.optimization_barrier((begun, table, project[0]))
    pair_two = swapped(raw, 2)
    begun = call(further_kernel, z, begun_shape, (matrix, block_one, begun), (), (1,))
    begun = call(further_kernel, z, begun_shape, (matrix, block_two, begun), (), (2,))

    width = z.wide - z.rhs
    part = shape((z.own, z.share, z.wide), BF)
    part_more = shape((z.own + z.more, z.dense, z.lanes), BF)
    link = shape((CAP, z.share, z.wide), BF)
    thin = shape((CAP, z.dense, z.lanes), BF)
    thin_more = shape((CAP + z.more, z.dense, z.lanes), BF)
    sums_shape = shape((grps, z.dense, z.lanes), BF) if z.near else shape((2, z.vertices, z.wide), F32)

    *parts, wide, ext = call(
        first_kernel,
        z,
        [part] * grps + [shape((z.own * MODES, z.rhs), F32), shape((z.own, MODES, width), BF)],
        (table, matrix, block_three, begun, own_tables, coarse),
        (
            pltpu.VMEM((z.rows, z.wide), BF),
            pltpu.VMEM((z.own, MODES, z.wide), BF),
        ),
    )
    part_one = swapped(parts[1], 1)
    part_two = swapped(parts[2], 2)
    part_three = swapped(parts[3], 3)
    parts = [parts[0], part_one, part_two, part_three]
    outgoing = call(pack_kernel, z, [link] * LINKS, (table, *parts), (pltpu.VMEM((z.faces, z.share, z.wide), BF),), (False,))
    arrived = paired(outgoing)
    pair_one = swapped(raw, 1)
    arrived, pair_one, pair_two = lax.optimization_barrier((arrived, pair_one, pair_two))
    replies = call(
        average_kernel,
        z,
        [link] * LINKS,
        (table, *arrived),
        (pltpu.VMEM((MORT_OWN + 1, z.share, z.wide), F32), pltpu.VMEM((MORT_OWN + 1, z.share, z.wide), BF)),
        (False,),
    )
    answered = paired(replies)
    pair_three = swapped(pair_two, 1)
    answered, pair_three = lax.optimization_barrier((answered, pair_three))
    spread = call(
        spread_first,
        z,
        shape((z.packed, z.share, z.lanes), BF),
        (table, *answered),
        (pltpu.VMEM((SLOTS, z.share, z.wide), BF),),
    )
    spread_two = swapped(spread, 2)
    shares = [spread, swapped(spread, 1), spread_two, swapped(spread_two, 1)]
    mixed = call(
        mix_kernel,
        z,
        shape((z.rows, z.all_rows), BF),
        (matrix, own_tables, pair_one, pair_two, pair_three),
        (pltpu.VMEM((z.rows, z.all_rows), BF), pltpu.VMEM((z.own * MODES // 2, 2 * FPTS), F32)),
    )
    *parts, earlier, hits, sums = call(
        second_kernel,
        z,
        [part_more] * grps
        + [shape((z.rows, z.rhs), BF), shape((z.own * MODES, z.vertices), BF), sums_shape],
        (table, mixed, *shares, wide, ext),
        (
            pltpu.VMEM((z.all_rows, z.rhs), BF),
            pltpu.VMEM((z.rows, z.rhs), F32),
            pltpu.VMEM((z.own * MODES, z.extra), BF),
        ),
    )
    if not z.near:
        sums = lax.psum(sums, ("sub", "grp"))
    parts = exchanged(parts)
    outgoing = call(
        pack_kernel, z, [thin_more] * LINKS, (table, *parts), (pltpu.VMEM((z.faces, z.dense, z.lanes), BF),), (z.near,)
    )
    arrived = paired(outgoing)
    total_shape = [shape((z.more, z.dense, z.lanes), F32)] if z.near else []
    results = call(
        average_kernel,
        z,
        [thin, thin_more, thin_more, thin, thin] + total_shape,
        (table, *arrived),
        (pltpu.VMEM((MORT_OWN + 1, z.dense, z.lanes), F32), pltpu.VMEM((MORT_OWN + 1, z.dense, z.lanes), BF)),
        (True,),
    )
    answered = paired(results[:LINKS])
    outs = call(
        spread_second,
        z,
        [part_more] * grps,
        (table, *answered, *results[LINKS:]),
        (pltpu.VMEM((SLOTS, z.dense, z.lanes), BF),),
    )
    last_two = swapped(outs[2], 2)
    shares = [outs[0], swapped(outs[1], 1), last_two, swapped(outs[3], 3)]
    prior = call(prior_kernel, z, shape((z.rhs, z.rows), F32), (own_tables, earlier, first))
    inputs = (table, *shares, own_tables, coarse, sums, hits, prior)
    result = pl.pallas_call(
        functools.partial(last_kernel, z),
        out_shape=pltpu.HBM((z.rhs, z.rows), F32),
        in_specs=[SMEM] + [VMEM] * (len(inputs) - 1),
        out_specs=HBM,
        scratch_shapes=[
            pltpu.VMEM((z.own, MODES, z.rhs), F32),
            pltpu.VMEM((z.vertices, z.rhs), F32),
            pltpu.VMEM((grps, z.dense, z.lanes), BF),
            pltpu.VMEM((z.rhs, z.rows), F32),
            pltpu.SemaphoreType.DMA((z.own // 2,)),
        ],
        compiler_params=pltpu.CompilerParams(vmem_limit_bytes=16 << 20),
    )(
        *[
            pltpu.with_memory_space_constraint(a, pltpu.SMEM if a.dtype == jnp.int32 else pltpu.VMEM)
            for a in inputs
        ]
    )
    return result.T[None]


def solution(mesh):
    return jax.shard_map(
        run,
        mesh=mesh,
        in_specs=(
            P("sub", "grp", None),
            P("sub", "grp", None),
            P("sub", "grp", None),
            P("sub", "grp", None),
            P("sub", None, "grp"),
            P(),
            P(),
            P(),
            P(),
            P(),
        ),
        out_specs=P("sub", "grp", None),
        check_vma=False,
    )
```

```python
import functools

import jax
import jax.numpy as jnp
from jax import lax
from jax.experimental import pallas as pl
from jax.experimental.pallas import tpu as pltpu
from jax.sharding import PartitionSpec as P

DEG = 8
MODES = 64
FPTS = 64
MORT_OWN = 16
REACH = 2
CAP = 8
LINKS = 2 * REACH + 1
SLOTS = LINKS * CAP

BF = jnp.bfloat16
F32 = jnp.float32
CONTRACT_FIRST = (((0,), (0,)), ((), ()))
CONTRACT_LAST = (((1,), (1,)), ((), ()))
VMEM = pl.BlockSpec(memory_space=pltpu.VMEM)
SMEM = pl.BlockSpec(memory_space=pltpu.SMEM)
HBM = pl.BlockSpec(memory_space=pltpu.HBM)


def split_two(value):
    high = value.astype(BF)
    return high, (value - high.astype(F32)).astype(BF)


class Sizes:
    def __init__(self, subs, grps, schur, project, coarse_basis, rhs):
        self.subs = subs
        self.grps = grps
        self.rows = schur.shape[1]
        self.all_rows = schur.shape[2]
        self.own = project.shape[1]
        self.faces = self.own * grps
        self.corners = coarse_basis.shape[1]
        self.rhs = rhs.shape[2]
        self.vertices = 2 * subs
        self.share = MODES // grps
        self.extra = 2 * self.vertices
        self.wide = -(-(self.rhs + self.extra) // 128) * 128
        self.lanes = self.rhs // 128 * 128
        self.tail = self.rhs - self.lanes
        self.missing = range(REACH + 1, subs - REACH)
        self.near = self.vertices == self.share and LINKS <= subs and len(self.missing) <= 3 <= grps
        self.more = 1 if self.near else 0
        self.dense = self.share * self.rhs // self.lanes
        self.pieces = max(1, 128 // self.extra)
        self.slabs = max(1, self.extra // 128)
        self.head = self.faces + self.faces * self.tail // self.lanes
        self.packed = self.head + self.faces * self.slabs // self.pieces
        self.t_src = 0
        self.t_arr = SLOTS
        self.t_slot = 2 * SLOTS
        self.t_count = self.t_slot + self.faces
        self.t_order = self.t_count + MORT_OWN
        self.t_corner = self.t_order + MORT_OWN
        self.t_end = self.t_corner + self.corners


def call(kernel, sizes, outs, args, scratch=(), static=(), aliases=None):
    single = not isinstance(outs, list)
    outs = [outs] if single else outs
    ins = [SMEM if a.dtype == jnp.int32 else VMEM for a in args]
    args = [
        pltpu.with_memory_space_constraint(a, pltpu.SMEM if a.dtype == jnp.int32 else pltpu.VMEM) for a in args
    ]
    results = pl.pallas_call(
        functools.partial(kernel, sizes, *static),
        out_shape=[pltpu.VMEM(o.shape, o.dtype) for o in outs],
        in_specs=ins,
        out_specs=[VMEM for _ in outs],
        scratch_shapes=list(scratch),
        input_output_aliases=aliases or {},
        compiler_params=pltpu.CompilerParams(vmem_limit_bytes=16 << 20),
    )(*args)
    return results[0] if single else results


def meeting_of(link, s):
    odd, high = s % 2 == 1, (s // 2) % 2 == 1
    if link == REACH:
        return 4
    if abs(link - REACH) == 1:
        return jnp.where(odd == (link < REACH), 0, 3)
    return jnp.where(high == (link < REACH), 1, 2)


def table_kernel(z, owner, mortar, order, smap, vids, table, used, names, met):
    s = lax.axis_index("sub")
    g = lax.axis_index("grp")
    d = smap[s]
    for i in range(SLOTS):
        table[z.t_src + i] = 0
    for i in range(LINKS):
        used[i] = 0
        met[i] = jnp.int32(meeting_of(i, s))
    for i in range(MORT_OWN):
        table[z.t_count + i] = 0
        table[z.t_order + i] = order[s, i]
    for i in range(z.corners):
        table[z.t_corner + i] = vids[d, i]
    for f in range(z.faces):
        o = owner[d, 0, f]
        r = used[o]
        used[o] = r + 1
        slot = met[o] * CAP + r
        table[z.t_slot + f] = slot
        table[z.t_src + slot] = ((f // z.own) ^ g) * z.own + f % z.own
    for link in range(LINKS):
        dd = smap[lax.rem(s - link + REACH + z.subs, z.subs)]
        r = jnp.int32(0)
        for f in range(z.faces):
            hit = (owner[dd, 0, f] == link).astype(jnp.int32)
            m = mortar[dd, f]
            names[r] = m
            table[z.t_count + m] = table[z.t_count + m] + hit
            r = r + hit
        for i in range(CAP):
            table[z.t_arr + met[2 * REACH - link] * CAP + i] = jnp.where(i < r, names[i], MORT_OWN)


def narrow_kernel(z, start, coarse, out, held, basis, sems):
    pieces = 4
    size = z.rhs // pieces
    copies = [
        pltpu.make_async_copy(start.at[pl.ds(i * size, size)], held.at[pl.ds(i * size, size)], sems.at[i])
        for i in range(pieces)
    ]
    copies.append(pltpu.make_async_copy(coarse, basis, sems.at[pieces]))
    for c in copies:
        c.start()
    for i in range(pieces):
        copies[i].wait()
        out[i * size : (i + 1) * size, :] = held[i * size : (i + 1) * size, :].astype(BF)
    copies[pieces].wait()
    out[z.rhs :, :] = basis[...]


def mode_at(place):
    half = MODES // 2
    return jnp.where(place < half, 2 * place, 2 * (place - half) + 1)


def unpacked(z, raw, rows):
    half = MODES // 2
    value = raw[...].astype(F32)
    for i in range(half):
        rows[pl.ds(i, z.own, stride=half), :] = value[:, i * 2 * FPTS : (i + 1) * 2 * FPTS]
    tables = []
    for f in range(z.own):
        pair = rows[f * half : (f + 1) * half, :]
        tables.append(jnp.concatenate([pair[:, :FPTS], pair[:, FPTS:]], axis=0).astype(BF))
    return tables


def load_kernel(z, schur, rhs, coarse, project, schur_out, rhs_out, coarse_out, tables, raw, rows, sems):
    pairs = ((project, raw), (rhs, rhs_out), (coarse, coarse_out), (schur, schur_out))
    copies = [pltpu.make_async_copy(a, b, sems.at[i]) for i, (a, b) in enumerate(pairs)]
    for c in copies:
        c.start()
    copies[0].wait()
    for f, value in enumerate(unpacked(z, raw, rows)):
        tables[f] = value
    for c in copies[1:]:
        c.wait()


def two_blocks(one, two):
    blank = jnp.zeros_like(one)
    return jnp.concatenate(
        [jnp.concatenate([one, blank], axis=1), jnp.concatenate([blank, two], axis=1)], axis=0
    )


def mix_kernel(z, schur, t0, r1, r2, r3, out, middle, rows):
    g = lax.axis_index("grp")
    width = 2 * FPTS
    for j, r in enumerate((None, r1, r2, r3)):
        t = unpacked(z, r, rows) if j else t0
        for i in range(0, z.own, 2):
            at = pl.ds(pl.multiple_of(((g ^ j) * z.own + i) * FPTS, width), width)
            pair = two_blocks(t[i], t[i + 1])
            middle[:, at] = lax.dot_general(
                schur[:, at], pair, CONTRACT_LAST, preferred_element_type=F32
            ).astype(BF)
    for i in range(0, z.own, 2):
        two = slice(i * MODES, (i + 2) * MODES)
        out[two, :] = jnp.dot(
            two_blocks(t0[i], t0[i + 1]), middle[two, :], preferred_element_type=F32
        ).astype(BF)


def share_rows(z, member):
    return pl.ds(pl.multiple_of(member * z.share, z.share), z.share)


def hot_rows(z, table, width, shift):
    column = lax.broadcasted_iota(jnp.int32, (1, width), 1)
    rows = [jnp.where(column == table[z.t_corner + i] + shift, 1.0, 0.0) for i in range(z.corners)]
    return jnp.concatenate(rows, axis=0).astype(BF)


def block_product(z, schur, block, j):
    g = lax.axis_index("grp")
    at = pl.ds(pl.multiple_of((g ^ j) * z.rows, z.rows), z.rows)
    return lax.dot_general(schur[:, at], block[...], CONTRACT_LAST, preferred_element_type=F32)


def early_kernel(z, schur, b0, rhs, out):
    product = block_product(z, schur, b0, 0)
    out[:, : z.rhs] = product[:, : z.rhs] - rhs[...].T
    out[:, z.rhs :] = product[:, z.rhs :]


def further_kernel(z, j, schur, block, before, out):
    out[...] = before[...] + block_product(z, schur, block, j)


def first_kernel(z, table, schur, b3, before, tables, coarse, o0, o1, o2, o3, wide_out, ext_out, held, coeffs):
    g = lax.axis_index("grp")
    product = before[...] + block_product(z, schur, b3, 3)
    held[:, : z.rhs] = product[:, : z.rhs].astype(BF)
    width = z.wide - z.rhs
    basis = lax.dot_general(coarse[...], hot_rows(z, table, width, 0), CONTRACT_FIRST, preferred_element_type=F32)
    image = jnp.dot(
        product[:, z.rhs :].astype(BF), hot_rows(z, table, width, z.vertices), preferred_element_type=F32
    )
    held[:, z.rhs :] = (basis + image).astype(BF)
    for f in range(z.own):
        value = jnp.dot(tables[f], held[f * FPTS : (f + 1) * FPTS, :], preferred_element_type=F32)
        wide_out[f * MODES : (f + 1) * MODES, :] = value[:, : z.rhs]
        coeffs[f] = value.astype(BF)
    ext_out[...] = coeffs[:, :, z.rhs :]
    for j, o in enumerate((o0, o1, o2, o3)):
        for f in range(z.own):
            o[f] = coeffs[f, share_rows(z, g ^ j), :]


def pack_kernel(z, sums, table, c0, c1, c2, c3, o0, o1, o2, o3, o4, data):
    parts = (c0, c1, c2, c3)
    for j, c in enumerate(parts):
        data[j * z.own : (j + 1) * z.own] = c[: z.own]
    for k, o in enumerate((o0, o1, o2, o3, o4)):
        for i in range(CAP):
            o[i] = data[table[z.t_src + k * CAP + i]]
    if sums:
        value = sum((c[z.own :].astype(F32) for c in parts[1:]), parts[0][z.own :].astype(F32)).astype(BF)
        for o in (o0, o1, o2, o3, o4):
            o[CAP:] = value


def average_kernel(z, dense, table, *refs):
    arrivals, refs = refs[:LINKS], refs[LINKS:]
    replies, refs = refs[:LINKS], refs[LINKS:]
    near, total, held = refs if dense and z.near else (None, *refs)
    g = lax.axis_index("grp")
    total[...] = jnp.zeros_like(total)
    for k, a in enumerate(arrivals):
        for i in range(CAP):
            m = table[z.t_arr + k * CAP + i]
            total[m] = total[m] + a[i].astype(F32)
    shape = total.shape[1:]
    row = lax.broadcasted_iota(jnp.int32, shape, 0)
    if dense:
        column = lax.broadcasted_iota(jnp.int32, shape, 1)
        half = z.share // 2
        row = jnp.where(row < z.share, row, row - z.share + jnp.where(column < z.tail, 0, half))
    mode = mode_at(g * z.share + row)
    degree = jnp.maximum(mode // DEG, mode % DEG)
    for k in range(MORT_OWN):
        divisor = jnp.maximum(table[z.t_count + k], 1).astype(F32)
        kept = jnp.where(degree <= table[z.t_order + k], 1.0, 0.0)
        held[k] = (total[k] / divisor * kept).astype(BF)
    held[MORT_OWN] = jnp.zeros_like(held[MORT_OWN])
    for k, o in enumerate(replies):
        for i in range(CAP):
            o[i] = held[table[z.t_arr + k * CAP + i]]
    if dense and z.near:
        s = lax.axis_index("sub")
        odd, high = s % 2 == 1, (s // 2) % 2 == 1
        inner_one, inner_two, outer_two, outer_one, own = [a[CAP:].astype(F32) for a in arrivals]
        near[...] = own + inner_one + inner_two + outer_two + outer_one
        after = jnp.where(odd, outer_one, inner_one)
        before = jnp.where(odd, inner_one, outer_one)
        after_two = jnp.where(high, outer_two, inner_two)
        behind = after * (1.0 if len(z.missing) > 0 else 0.0)
        if len(z.missing) > 1:
            behind = behind + after_two
        ahead = before * (1.0 if len(z.missing) > 2 else 0.0)
        replies[1][CAP:] = jnp.where(high, behind, ahead).astype(BF)
        replies[2][CAP:] = jnp.where(high, ahead, behind).astype(BF)


def spread_first(z, table, *refs):
    blocks, out, data = refs[:LINKS], refs[-2], refs[-1]
    for link, b in enumerate(blocks):
        data[link * CAP : (link + 1) * CAP] = b[:CAP]
    half = z.own // 2
    for f in range(z.faces):
        out[f] = data[table[z.t_slot + f], :, : z.lanes]
    for member in range(z.grps):
        for i in range(half):
            f = member * z.own + i
            left = data[table[z.t_slot + f], :, z.lanes : z.rhs]
            right = data[table[z.t_slot + f + half], :, z.lanes : z.rhs]
            out[z.faces + member * half + i] = jnp.concatenate([left, right], axis=1)
    if z.pieces > 1:
        for p in range(z.faces // z.pieces):
            ends = [data[table[z.t_slot + p * z.pieces + i], :, z.rhs : z.rhs + z.extra] for i in range(z.pieces)]
            out[z.head + p] = jnp.concatenate(ends, axis=1)
    else:
        for f in range(z.faces):
            for p in range(z.slabs):
                at = z.rhs + p * 128
                out[z.head + f * z.slabs + p] = data[table[z.t_slot + f], :, at : at + 128]


def spread_second(z, table, *refs):
    n = LINKS + (1 if z.near else 0)
    blocks, near = refs[:LINKS], refs[LINKS:n]
    outs, data = refs[n : n + z.grps], refs[-1]
    g = lax.axis_index("grp")
    for k, b in enumerate(blocks):
        data[k * CAP : (k + 1) * CAP] = b[:CAP]
    for j, o in enumerate(outs):
        for i in range(z.own):
            o[i] = data[table[z.t_slot + (g ^ j) * z.own + i]]
    if z.near:
        value = (near[0][...] + blocks[1][CAP:].astype(F32) + blocks[2][CAP:].astype(F32)).astype(BF)
        for o in outs:
            o[z.own :] = value


def to_dense(z, value):
    half = z.share // 2
    tail = jnp.concatenate([value[:half, z.lanes :], value[half:, z.lanes :]], axis=1)
    return jnp.concatenate([value[:, : z.lanes], tail], axis=0)


def from_dense(z, value):
    tail = value[z.share :]
    tail = jnp.concatenate([tail[:, : z.tail], tail[:, z.tail :]], axis=0)
    return jnp.concatenate([value[: z.share], tail], axis=1)


def lay_out(z, jj, a, averages):
    g = lax.axis_index("grp")
    half = z.own // 2
    for f in range(z.faces):
        member, i = f // z.own, f % z.own
        rows = pl.ds(pl.multiple_of(f * MODES + (g ^ jj) * z.share, z.share), z.share)
        averages[rows, : z.lanes] = a[f]
        low = (i // half) * z.tail
        averages[rows, z.lanes :] = a[z.faces + member * half + i % half, :, low : low + z.tail]


def begin_kernel(z, a0, a1, averages):
    lay_out(z, 0, a0, averages)
    lay_out(z, 1, a1, averages)


def add_kernel(z, a2, before, averages):
    lay_out(z, 2, a2, averages)


def second_kernel(z, table, mixed, *refs):
    n = z.grps
    shares, refs = refs[:n], refs[n:]
    earlier, ext_in, refs = refs[0], refs[1], refs[3:]
    outs, refs = refs[:n], refs[n:]
    own_out, hits_out, sums_out, averages, coeffs, scales = refs
    g = lax.axis_index("grp")
    lay_out(z, 3, shares[3], averages)
    coeffs[...] = earlier[...] - 0.5 * jnp.dot(mixed[...], averages[...], preferred_element_type=F32)
    for j, o in enumerate(outs):
        for f in range(z.own):
            rows = pl.ds(pl.multiple_of(f * MODES + (g ^ j) * z.share, z.share), z.share)
            o[f] = to_dense(z, coeffs[rows, :]).astype(BF)
    own = averages[pl.ds(pl.multiple_of(g * z.rows, z.rows), z.rows), :]
    own_out[...] = own
    for i in range(z.own):
        for jj, a in enumerate(shares):
            rows = pl.ds(pl.multiple_of(i * MODES + (g ^ jj) * z.share, z.share), z.share)
            if z.pieces > 1:
                low = (i % z.pieces) * z.extra
                scales[rows, :] = a[z.head + (g * z.own + i) // z.pieces, :, low : low + z.extra]
            else:
                for p in range(z.slabs):
                    scales[rows, p * 128 : (p + 1) * 128] = a[z.head + (g * z.own + i) * z.slabs + p]
    hits_out[...] = scales[:, z.vertices :]
    flat = scales[:, : z.vertices]
    ext = ext_in[...].reshape(z.own * MODES, z.wide - z.rhs)
    one = lax.dot_general(ext[:, : z.vertices], own, CONTRACT_FIRST, preferred_element_type=F32)
    two = lax.dot_general(flat, coeffs[...].astype(BF), CONTRACT_FIRST, preferred_element_type=F32)
    between = lax.dot_general(flat, ext[:, z.vertices : z.extra], CONTRACT_FIRST, preferred_element_type=F32)
    between = -0.5 * between
    if z.near:
        blank = jnp.zeros((z.share, z.rhs - z.vertices), F32)
        between = jnp.concatenate([between, blank], axis=1)
        sums_out[0] = to_dense(z, one).astype(BF)
        sums_out[1] = to_dense(z, two).astype(BF)
        sums_out[2] = to_dense(z, between).astype(BF)
        for i in range(3, n):
            sums_out[i] = jnp.zeros_like(sums_out[i])
        for j, o in enumerate(outs):
            o[z.own] = sums_out[g ^ j]
    else:
        sums_out[...] = jnp.zeros_like(sums_out)
        sums_out[0, :, : z.rhs] = one
        sums_out[0, :, z.rhs : z.rhs + z.vertices] = between
        sums_out[1, :, : z.rhs] = two


def prior_kernel(z, tables, earlier, start, out):
    for i in range(0, z.own, 2):
        at = slice(i * FPTS, (i + 2) * FPTS)
        pair = two_blocks(tables[i], tables[i + 1])
        lifted = lax.dot_general(
            earlier[i * MODES : (i + 2) * MODES, :], pair, CONTRACT_FIRST, preferred_element_type=F32
        )
        out[:, at] = start[:, at] - 0.5 * lifted


def last_kernel(z, table, *refs):
    n = z.grps
    shares, refs = refs[:n], refs[n:]
    tables, coarse, sums, hits, prior, out, averages, whole, gained, done, sems = refs
    g = lax.axis_index("grp")
    if z.near:
        for j, c in enumerate(shares):
            gained[g ^ j] = c[z.own]
        one, two = from_dense(z, gained[0].astype(F32)), from_dense(z, gained[1].astype(F32))
        between = gained[2, : z.share, : z.vertices].astype(F32)
    else:
        one, two = sums[0, :, : z.rhs], sums[1, :, : z.rhs]
        between = sums[0, :, z.rhs : z.rhs + z.vertices]
    two = two + jnp.dot(between, one, precision=lax.Precision.HIGHEST, preferred_element_type=F32)
    whole[...] = one + two
    high, low = split_two(one)
    flat = hits[...]
    shift = jnp.dot(flat, high, preferred_element_type=F32) + jnp.dot(flat, low, preferred_element_type=F32)
    rows = [whole[pl.ds(table[z.t_corner + i], 1), :] for i in range(z.corners)]
    high, low = split_two(jnp.concatenate(rows, axis=0))
    both = jnp.concatenate([high.astype(F32), low.astype(F32)], axis=0).astype(BF)
    basis = coarse[...].astype(F32)
    basis = jnp.concatenate([basis, basis], axis=0).astype(BF)
    coarse_corr = lax.dot_general(both, basis, CONTRACT_FIRST, preferred_element_type=F32)
    copies = []
    for i in range(0, z.own, 2):
        fixed = []
        for f in (i, i + 1):
            for j, c in enumerate(shares):
                averages[f, share_rows(z, g ^ j), :] = from_dense(z, c[f].astype(F32))
            fixed.append(averages[f] - 0.5 * shift[f * MODES : (f + 1) * MODES, :])
        lifted = lax.dot_general(
            jnp.concatenate(fixed, axis=0).astype(BF),
            two_blocks(tables[i], tables[i + 1]),
            CONTRACT_FIRST,
            preferred_element_type=F32,
        )
        at = slice(i * FPTS, (i + 2) * FPTS)
        done[:, at] = prior[:, at] - 0.5 * (lifted + coarse_corr[:, at])
        at = pl.ds(i * FPTS, 2 * FPTS)
        copies.append(pltpu.make_async_copy(done.at[:, at], out.at[:, at], sems.at[i // 2]))
        copies[-1].start()
    for c in copies:
        c.wait()


def paired(blocks):
    count = lax.axis_size("sub")
    assert count % 4 == 0
    pairs = [[], [], [], []]
    for s in range(count):
        pairs[0].append((s, s ^ 1))
        pairs[1].append((s, s ^ 2))
        pairs[2].append((s, (s + (2 if (s // 2) % 2 else -2)) % count))
        pairs[3].append((s, (s + (1 if s % 2 else -1)) % count))
    met = []
    for k, p in enumerate(pairs):
        met.append(lax.ppermute(blocks[k], "sub", p))
    return [*met, blocks[4]]


def swapped(value, mask):
    count = lax.axis_size("grp")
    return lax.ppermute(value, "grp", [(s, s ^ mask) for s in range(count)])


def exchanged(blocks):
    met = [blocks[0]]
    for j in range(1, len(blocks)):
        met.append(swapped(blocks[j], j))
    return met


def run(schur, rhs, start, project, coarse_basis, owner_of_face, mortar_of_face, mortar_order, subdomain_map, vertex_ids):
    subs, grps = lax.axis_size("sub"), lax.axis_size("grp")
    z = Sizes(subs, grps, schur, project, coarse_basis, rhs)
    shape = jax.ShapeDtypeStruct
    matrix, target, first = schur[0], rhs[0].T, start[0].T

    trace_b = pl.pallas_call(
        functools.partial(narrow_kernel, z),
        out_shape=pltpu.VMEM((z.rhs + z.corners, z.rows), BF),
        in_specs=[HBM] * 2,
        out_specs=VMEM,
        scratch_shapes=[
            pltpu.VMEM((z.rhs, z.rows), F32),
            pltpu.VMEM((z.corners, z.rows), BF),
            pltpu.SemaphoreType.DMA((5,)),
        ],
        compiler_params=pltpu.CompilerParams(vmem_limit_bytes=16 << 20),
    )(*[pltpu.with_memory_space_constraint(a, pltpu.HBM) for a in (first, coarse_basis[0])])
    block_two = swapped(trace_b, 2)
    block_one = swapped(trace_b, 1)

    table = pl.pallas_call(
        functools.partial(table_kernel, z),
        out_shape=pltpu.SMEM((z.t_end,), jnp.int32),
        in_specs=[SMEM] * 5,
        out_specs=SMEM,
        scratch_shapes=[pltpu.SMEM((LINKS,), jnp.int32), pltpu.SMEM((z.faces + 1,), jnp.int32), pltpu.SMEM((LINKS,), jnp.int32)],
    )(owner_of_face.transpose(0, 2, 1), mortar_of_face, mortar_order, subdomain_map, vertex_ids)
    loaded = [matrix, target, coarse_basis[0]]
    matrix, target, coarse, own_tables = pl.pallas_call(
        functools.partial(load_kernel, z),
        out_shape=[pltpu.VMEM(a.shape, a.dtype) for a in loaded] + [pltpu.VMEM((z.own, MODES, FPTS), BF)],
        in_specs=[HBM] * 4,
        out_specs=[VMEM] * 4,
        scratch_shapes=[
            pltpu.VMEM((z.own, MODES * FPTS), BF),
            pltpu.VMEM((z.own * MODES // 2, 2 * FPTS), F32),
            pltpu.SemaphoreType.DMA((4,)),
        ],
        compiler_params=pltpu.CompilerParams(vmem_limit_bytes=4 << 20),
    )(*[pltpu.with_memory_space_constraint(a, pltpu.HBM) for a in (*loaded, project[0])])
    block_three = swapped(block_two, 1)
    begun_shape = shape((z.rows, z.rhs + z.corners), F32)
    begun = call(early_kernel, z, begun_shape, (matrix, trace_b, target))
    begun, table, raw = lax.optimization_barrier((begun, table, project[0]))
    pair_two = swapped(raw, 2)
    begun = call(further_kernel, z, begun_shape, (matrix, block_one, begun), (), (1,))
    begun = call(further_kernel, z, begun_shape, (matrix, block_two, begun), (), (2,))

    width = z.wide - z.rhs
    part = shape((z.own, z.share, z.wide), BF)
    part_more = shape((z.own + z.more, z.dense, z.lanes), BF)
    link = shape((CAP, z.share, z.wide), BF)
    thin = shape((CAP, z.dense, z.lanes), BF)
    thin_more = shape((CAP + z.more, z.dense, z.lanes), BF)
    sums_shape = shape((grps, z.dense, z.lanes), BF) if z.near else shape((2, z.vertices, z.wide), F32)

    *parts, wide, ext = call(
        first_kernel,
        z,
        [part] * grps + [shape((z.own * MODES, z.rhs), F32), shape((z.own, MODES, width), BF)],
        (table, matrix, block_three, begun, own_tables, coarse),
        (
            pltpu.VMEM((z.rows, z.wide), BF),
            pltpu.VMEM((z.own, MODES, z.wide), BF),
        ),
    )
    parts = exchanged(parts)
    outgoing = call(pack_kernel, z, [link] * LINKS, (table, *parts), (pltpu.VMEM((z.faces, z.share, z.wide), BF),), (False,))
    arrived = paired(outgoing)
    pair_one = swapped(raw, 1)
    arrived, pair_one, pair_two = lax.optimization_barrier((arrived, pair_one, pair_two))
    replies = call(
        average_kernel,
        z,
        [link] * LINKS,
        (table, *arrived),
        (pltpu.VMEM((MORT_OWN + 1, z.share, z.wide), F32), pltpu.VMEM((MORT_OWN + 1, z.share, z.wide), BF)),
        (False,),
    )
    answered = paired(replies)
    pair_three = swapped(pair_two, 1)
    answered, pair_three = lax.optimization_barrier((answered, pair_three))
    spread = call(
        spread_first,
        z,
        shape((z.packed, z.share, z.lanes), BF),
        (table, *answered),
        (pltpu.VMEM((SLOTS, z.share, z.wide), BF),),
    )
    spread_two = swapped(spread, 2)
    spread_one = swapped(spread, 1)
    spread_three = swapped(spread_two, 1)
    shares = [spread, spread_one, spread_two, spread_three]
    laid_shape = shape((z.all_rows, z.rhs), BF)
    laid = call(begin_kernel, z, laid_shape, (spread, spread_one))
    laid = call(add_kernel, z, laid_shape, (spread_two, laid), aliases={1: 0})
    mixed = call(
        mix_kernel,
        z,
        shape((z.rows, z.all_rows), BF),
        (matrix, own_tables, pair_one, pair_two, pair_three),
        (pltpu.VMEM((z.rows, z.all_rows), BF), pltpu.VMEM((z.own * MODES // 2, 2 * FPTS), F32)),
    )
    *parts, earlier, hits, sums, _ = call(
        second_kernel,
        z,
        [part_more] * grps
        + [shape((z.rows, z.rhs), BF), shape((z.own * MODES, z.vertices), BF), sums_shape, laid_shape],
        (table, mixed, *shares, wide, ext, laid),
        (
            pltpu.VMEM((z.rows, z.rhs), F32),
            pltpu.VMEM((z.own * MODES, z.extra), BF),
        ),
        aliases={4 + grps: grps + 3},
    )
    if not z.near:
        sums = lax.psum(sums, ("sub", "grp"))
    parts = exchanged(parts)
    outgoing = call(
        pack_kernel, z, [thin_more] * LINKS, (table, *parts), (pltpu.VMEM((z.faces, z.dense, z.lanes), BF),), (z.near,)
    )
    arrived = paired(outgoing)
    total_shape = [shape((z.more, z.dense, z.lanes), F32)] if z.near else []
    results = call(
        average_kernel,
        z,
        [thin, thin_more, thin_more, thin, thin] + total_shape,
        (table, *arrived),
        (pltpu.VMEM((MORT_OWN + 1, z.dense, z.lanes), F32), pltpu.VMEM((MORT_OWN + 1, z.dense, z.lanes), BF)),
        (True,),
    )
    answered = paired(results[:LINKS])
    outs = call(
        spread_second,
        z,
        [part_more] * grps,
        (table, *answered, *results[LINKS:]),
        (pltpu.VMEM((SLOTS, z.dense, z.lanes), BF),),
    )
    shares = exchanged(outs)
    prior = call(prior_kernel, z, shape((z.rhs, z.rows), F32), (own_tables, earlier, first))
    inputs = (table, *shares, own_tables, coarse, sums, hits, prior)
    result = pl.pallas_call(
        functools.partial(last_kernel, z),
        out_shape=pltpu.HBM((z.rhs, z.rows), F32),
        in_specs=[SMEM] + [VMEM] * (len(inputs) - 1),
        out_specs=HBM,
        scratch_shapes=[
            pltpu.VMEM((z.own, MODES, z.rhs), F32),
            pltpu.VMEM((z.vertices, z.rhs), F32),
            pltpu.VMEM((grps, z.dense, z.lanes), BF),
            pltpu.VMEM((z.rhs, z.rows), F32),
            pltpu.SemaphoreType.DMA((z.own // 2,)),
        ],
        compiler_params=pltpu.CompilerParams(vmem_limit_bytes=16 << 20),
    )(
        *[
            pltpu.with_memory_space_constraint(a, pltpu.SMEM if a.dtype == jnp.int32 else pltpu.VMEM)
            for a in inputs
        ]
    )
    return result.T[None]


def solution(mesh):
    return jax.shard_map(
        run,
        mesh=mesh,
        in_specs=(
            P("sub", "grp", None),
            P("sub", "grp", None),
            P("sub", "grp", None),
            P("sub", "grp", None),
            P("sub", None, "grp"),
            P(),
            P(),
            P(),
            P(),
            P(),
        ),
        out_specs=P("sub", "grp", None),
        check_vma=False,
    )
```

```python
import functools

import jax
import jax.numpy as jnp
from jax import lax
from jax.experimental import pallas as pl
from jax.experimental.pallas import tpu as pltpu
from jax.sharding import PartitionSpec as P

DEG = 8
MODES = 64
FPTS = 64
MORT_OWN = 16
REACH = 2
CAP = 8
LINKS = 2 * REACH + 1
SLOTS = LINKS * CAP

BF = jnp.bfloat16
F32 = jnp.float32
CONTRACT_FIRST = (((0,), (0,)), ((), ()))
CONTRACT_LAST = (((1,), (1,)), ((), ()))
VMEM = pl.BlockSpec(memory_space=pltpu.VMEM)
SMEM = pl.BlockSpec(memory_space=pltpu.SMEM)
HBM = pl.BlockSpec(memory_space=pltpu.HBM)


def split_two(value):
    high = value.astype(BF)
    return high, (value - high.astype(F32)).astype(BF)


class Sizes:
    def __init__(self, subs, grps, schur, project, coarse_basis, rhs):
        self.subs = subs
        self.grps = grps
        self.rows = schur.shape[1]
        self.all_rows = schur.shape[2]
        self.own = project.shape[1]
        self.faces = self.own * grps
        self.corners = coarse_basis.shape[1]
        self.rhs = rhs.shape[2]
        self.vertices = 2 * subs
        self.share = MODES // grps
        self.extra = 2 * self.vertices
        self.wide = -(-(self.rhs + self.extra) // 128) * 128
        self.lanes = self.rhs // 128 * 128
        self.tail = self.rhs - self.lanes
        self.missing = range(REACH + 1, subs - REACH)
        self.near = self.vertices == self.share and LINKS <= subs and len(self.missing) <= 3 <= grps
        self.more = 1 if self.near else 0
        self.dense = self.share * self.rhs // self.lanes
        self.pieces = max(1, 128 // self.extra)
        self.slabs = max(1, self.extra // 128)
        self.head = self.faces + self.faces * self.tail // self.lanes
        self.each = self.own * self.slabs // self.pieces
        self.packed = self.head + 2 * self.each
        self.t_src = 0
        self.t_arr = SLOTS
        self.t_slot = 2 * SLOTS
        self.t_count = self.t_slot + self.faces
        self.t_order = self.t_count + MORT_OWN
        self.t_corner = self.t_order + MORT_OWN
        self.t_end = self.t_corner + self.corners


def call(kernel, sizes, outs, args, scratch=(), static=(), aliases=None):
    single = not isinstance(outs, list)
    outs = [outs] if single else outs
    ins = [SMEM if a.dtype == jnp.int32 else VMEM for a in args]
    args = [
        pltpu.with_memory_space_constraint(a, pltpu.SMEM if a.dtype == jnp.int32 else pltpu.VMEM) for a in args
    ]
    results = pl.pallas_call(
        functools.partial(kernel, sizes, *static),
        out_shape=[pltpu.VMEM(o.shape, o.dtype) for o in outs],
        in_specs=ins,
        out_specs=[VMEM for _ in outs],
        scratch_shapes=list(scratch),
        input_output_aliases=aliases or {},
        compiler_params=pltpu.CompilerParams(vmem_limit_bytes=16 << 20),
    )(*args)
    return results[0] if single else results


def meeting_of(link, s):
    odd, high = s % 2 == 1, (s // 2) % 2 == 1
    if link == REACH:
        return 4
    if abs(link - REACH) == 1:
        return jnp.where(odd == (link < REACH), 0, 3)
    return jnp.where(high == (link < REACH), 1, 2)


def table_kernel(z, owner, mortar, order, smap, vids, table, used, names, met):
    s = lax.axis_index("sub")
    g = lax.axis_index("grp")
    d = smap[s]
    for i in range(SLOTS):
        table[z.t_src + i] = 0
    for i in range(LINKS):
        used[i] = 0
        met[i] = jnp.int32(meeting_of(i, s))
    for i in range(MORT_OWN):
        table[z.t_count + i] = 0
        table[z.t_order + i] = order[s, i]
    for i in range(z.corners):
        table[z.t_corner + i] = vids[d, i]
    for f in range(z.faces):
        o = owner[d, 0, f]
        r = used[o]
        used[o] = r + 1
        slot = met[o] * CAP + r
        table[z.t_slot + f] = slot
        table[z.t_src + slot] = ((f // z.own) ^ g) * z.own + f % z.own
    for link in range(LINKS):
        dd = smap[lax.rem(s - link + REACH + z.subs, z.subs)]
        r = jnp.int32(0)
        for f in range(z.faces):
            hit = (owner[dd, 0, f] == link).astype(jnp.int32)
            m = mortar[dd, f]
            names[r] = m
            table[z.t_count + m] = table[z.t_count + m] + hit
            r = r + hit
        for i in range(CAP):
            table[z.t_arr + met[2 * REACH - link] * CAP + i] = jnp.where(i < r, names[i], MORT_OWN)


def narrow_kernel(z, start, coarse, out, held, basis, sems):
    pieces = 2
    size = z.rhs // pieces
    copies = [
        pltpu.make_async_copy(start.at[pl.ds(i * size, size)], held.at[pl.ds(i * size, size)], sems.at[i])
        for i in range(pieces)
    ]
    copies.append(pltpu.make_async_copy(coarse, basis, sems.at[pieces]))
    for c in copies:
        c.start()
    for i in range(pieces):
        copies[i].wait()
        out[i * size : (i + 1) * size, :] = held[i * size : (i + 1) * size, :].astype(BF)
    copies[pieces].wait()
    out[z.rhs :, :] = basis[...]


def mode_at(place):
    half = MODES // 2
    return jnp.where(place < half, 2 * place, 2 * (place - half) + 1)


def unpacked(z, raw, rows):
    half = MODES // 2
    value = raw[...].astype(F32)
    for i in range(half):
        rows[pl.ds(i, z.own, stride=half), :] = value[:, i * 2 * FPTS : (i + 1) * 2 * FPTS]
    tables = []
    for f in range(z.own):
        pair = rows[f * half : (f + 1) * half, :]
        tables.append(jnp.concatenate([pair[:, :FPTS], pair[:, FPTS:]], axis=0).astype(BF))
    return tables


def load_kernel(z, schur, rhs, coarse, project, schur_out, rhs_out, coarse_out, tables, raw, rows, sems):
    pairs = ((project, raw), (rhs, rhs_out), (coarse, coarse_out), (schur, schur_out))
    copies = [pltpu.make_async_copy(a, b, sems.at[i]) for i, (a, b) in enumerate(pairs)]
    for c in copies:
        c.start()
    copies[0].wait()
    for f, value in enumerate(unpacked(z, raw, rows)):
        tables[f] = value
    for c in copies[1:]:
        c.wait()


def two_blocks(one, two):
    blank = jnp.zeros_like(one)
    return jnp.concatenate(
        [jnp.concatenate([one, blank], axis=1), jnp.concatenate([blank, two], axis=1)], axis=0
    )


def mix_kernel(z, schur, t0, r1, r2, r3, out, middle, rows):
    g = lax.axis_index("grp")
    width = 2 * FPTS
    for j, r in enumerate((None, r1, r2, r3)):
        t = unpacked(z, r, rows) if j else t0
        for i in range(0, z.own, 2):
            at = pl.ds(pl.multiple_of(((g ^ j) * z.own + i) * FPTS, width), width)
            pair = two_blocks(t[i], t[i + 1])
            middle[:, at] = lax.dot_general(
                schur[:, at], pair, CONTRACT_LAST, preferred_element_type=F32
            ).astype(BF)
    for i in range(0, z.own, 2):
        two = slice(i * MODES, (i + 2) * MODES)
        out[two, :] = jnp.dot(
            two_blocks(t0[i], t0[i + 1]), middle[two, :], preferred_element_type=F32
        ).astype(BF)


def share_rows(z, member):
    return pl.ds(pl.multiple_of(member * z.share, z.share), z.share)


def hot_rows(z, table, width, shift):
    column = lax.broadcasted_iota(jnp.int32, (1, width), 1)
    rows = [jnp.where(column == table[z.t_corner + i] + shift, 1.0, 0.0) for i in range(z.corners)]
    return jnp.concatenate(rows, axis=0).astype(BF)


def block_product(z, schur, block, j):
    g = lax.axis_index("grp")
    at = pl.ds(pl.multiple_of((g ^ j) * z.rows, z.rows), z.rows)
    return lax.dot_general(schur[:, at], block[...], CONTRACT_LAST, preferred_element_type=F32)


def early_kernel(z, schur, b0, rhs, out):
    product = block_product(z, schur, b0, 0)
    out[:, : z.rhs] = product[:, : z.rhs] - rhs[...].T
    out[:, z.rhs :] = product[:, z.rhs :]


def further_kernel(z, j, schur, block, before, out):
    out[...] = before[...] + block_product(z, schur, block, j)


def first_kernel(z, table, schur, b3, before, tables, coarse, o0, o1, o2, o3, wide_out, ext_out, held, coeffs):
    g = lax.axis_index("grp")
    product = before[...] + block_product(z, schur, b3, 3)
    held[:, : z.rhs] = product[:, : z.rhs].astype(BF)
    width = z.wide - z.rhs
    basis = lax.dot_general(coarse[...], hot_rows(z, table, width, 0), CONTRACT_FIRST, preferred_element_type=F32)
    image = jnp.dot(
        product[:, z.rhs :].astype(BF), hot_rows(z, table, width, z.vertices), preferred_element_type=F32
    )
    held[:, z.rhs :] = (basis + image).astype(BF)
    for f in range(z.own):
        value = jnp.dot(tables[f], held[f * FPTS : (f + 1) * FPTS, :], preferred_element_type=F32)
        wide_out[f * MODES : (f + 1) * MODES, :] = value[:, : z.rhs]
        coeffs[f] = value.astype(BF)
    ext_out[...] = coeffs[:, :, z.rhs :]
    for j, o in enumerate((o0, o1, o2, o3)):
        for f in range(z.own):
            o[f] = coeffs[f, share_rows(z, g ^ j), :]


def pack_kernel(z, sums, table, c0, c1, c2, c3, o0, o1, o2, o3, o4, data):
    parts = (c0, c1, c2, c3)
    for j, c in enumerate(parts):
        data[j * z.own : (j + 1) * z.own] = c[: z.own]
    for k, o in enumerate((o0, o1, o2, o3, o4)):
        for i in range(CAP):
            o[i] = data[table[z.t_src + k * CAP + i]]
    if sums:
        value = sum((c[z.own :].astype(F32) for c in parts[1:]), parts[0][z.own :].astype(F32)).astype(BF)
        for o in (o0, o1, o2, o3, o4):
            o[CAP:] = value


def average_kernel(z, dense, table, *refs):
    arrivals, refs = refs[:LINKS], refs[LINKS:]
    replies, refs = refs[:LINKS], refs[LINKS:]
    near, total, held = refs if dense and z.near else (None, *refs)
    g = lax.axis_index("grp")
    total[...] = jnp.zeros_like(total)
    for k, a in enumerate(arrivals):
        for i in range(CAP):
            m = table[z.t_arr + k * CAP + i]
            total[m] = total[m] + a[i].astype(F32)
    shape = total.shape[1:]
    row = lax.broadcasted_iota(jnp.int32, shape, 0)
    if dense:
        column = lax.broadcasted_iota(jnp.int32, shape, 1)
        half = z.share // 2
        row = jnp.where(row < z.share, row, row - z.share + jnp.where(column < z.tail, 0, half))
    mode = mode_at(g * z.share + row)
    degree = jnp.maximum(mode // DEG, mode % DEG)
    for k in range(MORT_OWN):
        divisor = jnp.maximum(table[z.t_count + k], 1).astype(F32)
        kept = jnp.where(degree <= table[z.t_order + k], 1.0, 0.0)
        held[k] = (total[k] / divisor * kept).astype(BF)
    held[MORT_OWN] = jnp.zeros_like(held[MORT_OWN])
    for k, o in enumerate(replies):
        for i in range(CAP):
            o[i] = held[table[z.t_arr + k * CAP + i]]
    if dense and z.near:
        s = lax.axis_index("sub")
        odd, high = s % 2 == 1, (s // 2) % 2 == 1
        inner_one, inner_two, outer_two, outer_one, own = [a[CAP:].astype(F32) for a in arrivals]
        near[...] = own + inner_one + inner_two + outer_two + outer_one
        after = jnp.where(odd, outer_one, inner_one)
        before = jnp.where(odd, inner_one, outer_one)
        after_two = jnp.where(high, outer_two, inner_two)
        behind = after * (1.0 if len(z.missing) > 0 else 0.0)
        if len(z.missing) > 1:
            behind = behind + after_two
        ahead = before * (1.0 if len(z.missing) > 2 else 0.0)
        replies[1][CAP:] = jnp.where(high, behind, ahead).astype(BF)
        replies[2][CAP:] = jnp.where(high, ahead, behind).astype(BF)


def spread_first(z, mask, table, *refs):
    g = lax.axis_index("grp")
    blocks, out, data = refs[:LINKS], refs[-2], refs[-1]
    for link, b in enumerate(blocks):
        data[link * CAP : (link + 1) * CAP] = b[:CAP]
    half = z.own // 2
    for f in range(z.faces):
        out[f] = data[table[z.t_slot + f], :, : z.lanes]
    for member in range(z.grps):
        for i in range(half):
            f = member * z.own + i
            left = data[table[z.t_slot + f], :, z.lanes : z.rhs]
            right = data[table[z.t_slot + f + half], :, z.lanes : z.rhs]
            out[z.faces + member * half + i] = jnp.concatenate([left, right], axis=1)
    for order, target in enumerate((mask, mask ^ 1)):
        slots = [table[z.t_slot + (g ^ target) * z.own + i] for i in range(z.own)]
        at = z.head + order * z.each
        if z.pieces > 1:
            for p in range(z.each):
                mine = slots[p * z.pieces : (p + 1) * z.pieces]
                out[at + p] = jnp.concatenate([data[k, :, z.rhs : z.rhs + z.extra] for k in mine], axis=1)
        else:
            for f in range(z.own):
                for p in range(z.slabs):
                    low = z.rhs + p * 128
                    out[at + f * z.slabs + p] = data[slots[f], :, low : low + 128]


def spread_second(z, table, *refs):
    n = LINKS + (1 if z.near else 0)
    blocks, near = refs[:LINKS], refs[LINKS:n]
    outs, data = refs[n : n + z.grps], refs[-1]
    g = lax.axis_index("grp")
    for k, b in enumerate(blocks):
        data[k * CAP : (k + 1) * CAP] = b[:CAP]
    for j, o in enumerate(outs):
        for i in range(z.own):
            o[i] = data[table[z.t_slot + (g ^ j) * z.own + i]]
    if z.near:
        value = (near[0][...] + blocks[1][CAP:].astype(F32) + blocks[2][CAP:].astype(F32)).astype(BF)
        for o in outs:
            o[z.own :] = value


def to_dense(z, value):
    half = z.share // 2
    tail = jnp.concatenate([value[:half, z.lanes :], value[half:, z.lanes :]], axis=1)
    return jnp.concatenate([value[:, : z.lanes], tail], axis=0)


def from_dense(z, value):
    tail = value[z.share :]
    tail = jnp.concatenate([tail[:, : z.tail], tail[:, z.tail :]], axis=0)
    return jnp.concatenate([value[: z.share], tail], axis=1)


def lay_out(z, jj, a, averages):
    g = lax.axis_index("grp")
    half = z.own // 2
    for f in range(z.faces):
        member, i = f // z.own, f % z.own
        rows = pl.ds(pl.multiple_of(f * MODES + (g ^ jj) * z.share, z.share), z.share)
        averages[rows, : z.lanes] = a[f]
        low = (i // half) * z.tail
        averages[rows, z.lanes :] = a[z.faces + member * half + i % half, :, low : low + z.tail]


def begin_kernel(z, a0, a1, averages):
    lay_out(z, 0, a0, averages)
    lay_out(z, 1, a1, averages)


def add_kernel(z, a2, before, averages):
    lay_out(z, 2, a2, averages)


def second_kernel(z, table, mixed, *refs):
    n = z.grps
    shares, refs = refs[:n], refs[n:]
    earlier, ext_in, refs = refs[0], refs[1], refs[3:]
    outs, refs = refs[:n], refs[n:]
    own_out, hits_out, sums_out, averages, coeffs, scales = refs
    g = lax.axis_index("grp")
    lay_out(z, 3, shares[3], averages)
    coeffs[...] = earlier[...] - 0.5 * jnp.dot(mixed[...], averages[...], preferred_element_type=F32)
    for j, o in enumerate(outs):
        for f in range(z.own):
            rows = pl.ds(pl.multiple_of(f * MODES + (g ^ j) * z.share, z.share), z.share)
            o[f] = to_dense(z, coeffs[rows, :]).astype(BF)
    own = averages[pl.ds(pl.multiple_of(g * z.rows, z.rows), z.rows), :]
    own_out[...] = own
    for i in range(z.own):
        for jj, a in enumerate(shares):
            rows = pl.ds(pl.multiple_of(i * MODES + (g ^ jj) * z.share, z.share), z.share)
            if z.pieces > 1:
                low = (i % z.pieces) * z.extra
                scales[rows, :] = a[z.head + jj % 2 * z.each + i // z.pieces, :, low : low + z.extra]
            else:
                for p in range(z.slabs):
                    scales[rows, p * 128 : (p + 1) * 128] = a[z.head + jj % 2 * z.each + i * z.slabs + p]
    hits_out[...] = scales[:, z.vertices :]
    flat = scales[:, : z.vertices]
    ext = ext_in[...].reshape(z.own * MODES, z.wide - z.rhs)
    one = lax.dot_general(ext[:, : z.vertices], own, CONTRACT_FIRST, preferred_element_type=F32)
    two = lax.dot_general(flat, coeffs[...].astype(BF), CONTRACT_FIRST, preferred_element_type=F32)
    between = lax.dot_general(flat, ext[:, z.vertices : z.extra], CONTRACT_FIRST, preferred_element_type=F32)
    between = -0.5 * between
    if z.near:
        blank = jnp.zeros((z.share, z.rhs - z.vertices), F32)
        between = jnp.concatenate([between, blank], axis=1)
        sums_out[0] = to_dense(z, one).astype(BF)
        sums_out[1] = to_dense(z, two).astype(BF)
        sums_out[2] = to_dense(z, between).astype(BF)
        for i in range(3, n):
            sums_out[i] = jnp.zeros_like(sums_out[i])
        for j, o in enumerate(outs):
            o[z.own] = sums_out[g ^ j]
    else:
        sums_out[...] = jnp.zeros_like(sums_out)
        sums_out[0, :, : z.rhs] = one
        sums_out[0, :, z.rhs : z.rhs + z.vertices] = between
        sums_out[1, :, : z.rhs] = two


def prior_kernel(z, tables, earlier, start, out):
    for i in range(0, z.own, 2):
        at = slice(i * FPTS, (i + 2) * FPTS)
        pair = two_blocks(tables[i], tables[i + 1])
        lifted = lax.dot_general(
            earlier[i * MODES : (i + 2) * MODES, :], pair, CONTRACT_FIRST, preferred_element_type=F32
        )
        out[:, at] = start[:, at] - 0.5 * lifted


def last_kernel(z, table, *refs):
    n = z.grps
    shares, refs = refs[:n], refs[n:]
    tables, coarse, sums, hits, prior, out, averages, whole, gained, done, sems = refs
    g = lax.axis_index("grp")
    if z.near:
        for j, c in enumerate(shares):
            gained[g ^ j] = c[z.own]
        one, two = from_dense(z, gained[0].astype(F32)), from_dense(z, gained[1].astype(F32))
        between = gained[2, : z.share, : z.vertices].astype(F32)
    else:
        one, two = sums[0, :, : z.rhs], sums[1, :, : z.rhs]
        between = sums[0, :, z.rhs : z.rhs + z.vertices]
    two = two + jnp.dot(between, one, precision=lax.Precision.HIGHEST, preferred_element_type=F32)
    whole[...] = one + two
    high, low = split_two(one)
    flat = hits[...]
    shift = jnp.dot(flat, high, preferred_element_type=F32) + jnp.dot(flat, low, preferred_element_type=F32)
    rows = [whole[pl.ds(table[z.t_corner + i], 1), :] for i in range(z.corners)]
    high, low = split_two(jnp.concatenate(rows, axis=0))
    both = jnp.concatenate([high.astype(F32), low.astype(F32)], axis=0).astype(BF)
    basis = coarse[...].astype(F32)
    basis = jnp.concatenate([basis, basis], axis=0).astype(BF)
    coarse_corr = lax.dot_general(both, basis, CONTRACT_FIRST, preferred_element_type=F32)
    copies = []
    for i in range(0, z.own, 2):
        fixed = []
        for f in (i, i + 1):
            for j, c in enumerate(shares):
                averages[f, share_rows(z, g ^ j), :] = from_dense(z, c[f].astype(F32))
            fixed.append(averages[f] - 0.5 * shift[f * MODES : (f + 1) * MODES, :])
        lifted = lax.dot_general(
            jnp.concatenate(fixed, axis=0).astype(BF),
            two_blocks(tables[i], tables[i + 1]),
            CONTRACT_FIRST,
            preferred_element_type=F32,
        )
        at = slice(i * FPTS, (i + 2) * FPTS)
        done[:, at] = prior[:, at] - 0.5 * (lifted + coarse_corr[:, at])
        at = pl.ds(i * FPTS, 2 * FPTS)
        copies.append(pltpu.make_async_copy(done.at[:, at], out.at[:, at], sems.at[i // 2]))
        copies[-1].start()
    for c in copies:
        c.wait()


def paired(blocks):
    count = lax.axis_size("sub")
    assert count % 4 == 0
    pairs = [[], [], [], []]
    for s in range(count):
        pairs[0].append((s, s ^ 1))
        pairs[1].append((s, s ^ 2))
        pairs[2].append((s, (s + (2 if (s // 2) % 2 else -2)) % count))
        pairs[3].append((s, (s + (1 if s % 2 else -1)) % count))
    met = []
    for k, p in enumerate(pairs):
        met.append(lax.ppermute(blocks[k], "sub", p))
    return [*met, blocks[4]]


def swapped(value, mask):
    count = lax.axis_size("grp")
    return lax.ppermute(value, "grp", [(s, s ^ mask) for s in range(count)])


def exchanged(blocks):
    met = [blocks[0]]
    for j in range(1, len(blocks)):
        met.append(swapped(blocks[j], j))
    return met


def run(schur, rhs, start, project, coarse_basis, owner_of_face, mortar_of_face, mortar_order, subdomain_map, vertex_ids):
    subs, grps = lax.axis_size("sub"), lax.axis_size("grp")
    z = Sizes(subs, grps, schur, project, coarse_basis, rhs)
    shape = jax.ShapeDtypeStruct
    matrix, target, first = schur[0], rhs[0].T, start[0].T

    trace_b = pl.pallas_call(
        functools.partial(narrow_kernel, z),
        out_shape=pltpu.VMEM((z.rhs + z.corners, z.rows), BF),
        in_specs=[HBM] * 2,
        out_specs=VMEM,
        scratch_shapes=[
            pltpu.VMEM((z.rhs, z.rows), F32),
            pltpu.VMEM((z.corners, z.rows), BF),
            pltpu.SemaphoreType.DMA((3,)),
        ],
        compiler_params=pltpu.CompilerParams(vmem_limit_bytes=16 << 20),
    )(*[pltpu.with_memory_space_constraint(a, pltpu.HBM) for a in (first, coarse_basis[0])])
    block_two = swapped(trace_b, 2)
    block_one = swapped(trace_b, 1)

    table = pl.pallas_call(
        functools.partial(table_kernel, z),
        out_shape=pltpu.SMEM((z.t_end,), jnp.int32),
        in_specs=[SMEM] * 5,
        out_specs=SMEM,
        scratch_shapes=[pltpu.SMEM((LINKS,), jnp.int32), pltpu.SMEM((z.faces + 1,), jnp.int32), pltpu.SMEM((LINKS,), jnp.int32)],
    )(owner_of_face.transpose(0, 2, 1), mortar_of_face, mortar_order, subdomain_map, vertex_ids)
    loaded = [matrix, target, coarse_basis[0]]
    matrix, target, coarse, own_tables = pl.pallas_call(
        functools.partial(load_kernel, z),
        out_shape=[pltpu.VMEM(a.shape, a.dtype) for a in loaded] + [pltpu.VMEM((z.own, MODES, FPTS), BF)],
        in_specs=[HBM] * 4,
        out_specs=[VMEM] * 4,
        scratch_shapes=[
            pltpu.VMEM((z.own, MODES * FPTS), BF),
            pltpu.VMEM((z.own * MODES // 2, 2 * FPTS), F32),
            pltpu.SemaphoreType.DMA((4,)),
        ],
        compiler_params=pltpu.CompilerParams(vmem_limit_bytes=4 << 20),
    )(*[pltpu.with_memory_space_constraint(a, pltpu.HBM) for a in (*loaded, project[0])])
    block_three = swapped(block_two, 1)
    begun_shape = shape((z.rows, z.rhs + z.corners), F32)
    begun = call(early_kernel, z, begun_shape, (matrix, trace_b, target))
    begun, table, raw = lax.optimization_barrier((begun, table, project[0]))
    pair_two = swapped(raw, 2)
    begun = call(further_kernel, z, begun_shape, (matrix, block_one, begun), (), (1,))
    begun = call(further_kernel, z, begun_shape, (matrix, block_two, begun), (), (2,))

    width = z.wide - z.rhs
    part = shape((z.own, z.share, z.wide), BF)
    part_more = shape((z.own + z.more, z.dense, z.lanes), BF)
    link = shape((CAP, z.share, z.wide), BF)
    thin = shape((CAP, z.dense, z.lanes), BF)
    thin_more = shape((CAP + z.more, z.dense, z.lanes), BF)
    sums_shape = shape((grps, z.dense, z.lanes), BF) if z.near else shape((2, z.vertices, z.wide), F32)

    *parts, wide, ext = call(
        first_kernel,
        z,
        [part] * grps + [shape((z.own * MODES, z.rhs), F32), shape((z.own, MODES, width), BF)],
        (table, matrix, block_three, begun, own_tables, coarse),
        (
            pltpu.VMEM((z.rows, z.wide), BF),
            pltpu.VMEM((z.own, MODES, z.wide), BF),
        ),
    )
    parts = exchanged(parts)
    outgoing = call(pack_kernel, z, [link] * LINKS, (table, *parts), (pltpu.VMEM((z.faces, z.share, z.wide), BF),), (False,))
    arrived = paired(outgoing)
    pair_one = swapped(raw, 1)
    arrived, pair_one, pair_two = lax.optimization_barrier((arrived, pair_one, pair_two))
    replies = call(
        average_kernel,
        z,
        [link] * LINKS,
        (table, *arrived),
        (pltpu.VMEM((MORT_OWN + 1, z.share, z.wide), F32), pltpu.VMEM((MORT_OWN + 1, z.share, z.wide), BF)),
        (False,),
    )
    answered = paired(replies)
    pair_three = swapped(pair_two, 1)
    answered, pair_three = lax.optimization_barrier((answered, pair_three))
    def spread_for(mask):
        return call(
            spread_first,
            z,
            shape((z.packed, z.share, z.lanes), BF),
            (table, *answered),
            (pltpu.VMEM((SLOTS, z.share, z.wide), BF),),
            (mask,),
        )

    spread_far = spread_for(2)
    spread = spread_for(0)
    spread_two = swapped(spread_far, 2)
    spread_one = swapped(spread, 1)
    spread_three = swapped(spread_two, 1)
    shares = [spread, spread_one, spread_two, spread_three]
    laid_shape = shape((z.all_rows, z.rhs), BF)
    laid = call(begin_kernel, z, laid_shape, (spread, spread_one))
    laid = call(add_kernel, z, laid_shape, (spread_two, laid), aliases={1: 0})
    mixed = call(
        mix_kernel,
        z,
        shape((z.rows, z.all_rows), BF),
        (matrix, own_tables, pair_one, pair_two, pair_three),
        (pltpu.VMEM((z.rows, z.all_rows), BF), pltpu.VMEM((z.own * MODES // 2, 2 * FPTS), F32)),
    )
    *parts, earlier, hits, sums, _ = call(
        second_kernel,
        z,
        [part_more] * grps
        + [shape((z.rows, z.rhs), BF), shape((z.own * MODES, z.vertices), BF), sums_shape, laid_shape],
        (table, mixed, *shares, wide, ext, laid),
        (
            pltpu.VMEM((z.rows, z.rhs), F32),
            pltpu.VMEM((z.own * MODES, z.extra), BF),
        ),
        aliases={4 + grps: grps + 3},
    )
    if not z.near:
        sums = lax.psum(sums, ("sub", "grp"))
    parts = exchanged(parts)
    outgoing = call(
        pack_kernel, z, [thin_more] * LINKS, (table, *parts), (pltpu.VMEM((z.faces, z.dense, z.lanes), BF),), (z.near,)
    )
    arrived = paired(outgoing)
    total_shape = [shape((z.more, z.dense, z.lanes), F32)] if z.near else []
    results = call(
        average_kernel,
        z,
        [thin, thin_more, thin_more, thin, thin] + total_shape,
        (table, *arrived),
        (pltpu.VMEM((MORT_OWN + 1, z.dense, z.lanes), F32), pltpu.VMEM((MORT_OWN + 1, z.dense, z.lanes), BF)),
        (True,),
    )
    answered = paired(results[:LINKS])
    outs = call(
        spread_second,
        z,
        [part_more] * grps,
        (table, *answered, *results[LINKS:]),
        (pltpu.VMEM((SLOTS, z.dense, z.lanes), BF),),
    )
    shares = exchanged(outs)
    prior = call(prior_kernel, z, shape((z.rhs, z.rows), F32), (own_tables, earlier, first))
    inputs = (table, *shares, own_tables, coarse, sums, hits, prior)
    result = pl.pallas_call(
        functools.partial(last_kernel, z),
        out_shape=pltpu.HBM((z.rhs, z.rows), F32),
        in_specs=[SMEM] + [VMEM] * (len(inputs) - 1),
        out_specs=HBM,
        scratch_shapes=[
            pltpu.VMEM((z.own, MODES, z.rhs), F32),
            pltpu.VMEM((z.vertices, z.rhs), F32),
            pltpu.VMEM((grps, z.dense, z.lanes), BF),
            pltpu.VMEM((z.rhs, z.rows), F32),
            pltpu.SemaphoreType.DMA((z.own // 2,)),
        ],
        compiler_params=pltpu.CompilerParams(vmem_limit_bytes=16 << 20),
    )(
        *[
            pltpu.with_memory_space_constraint(a, pltpu.SMEM if a.dtype == jnp.int32 else pltpu.VMEM)
            for a in inputs
        ]
    )
    return result.T[None]


def solution(mesh):
    return jax.shard_map(
        run,
        mesh=mesh,
        in_specs=(
            P("sub", "grp", None),
            P("sub", "grp", None),
            P("sub", "grp", None),
            P("sub", "grp", None),
            P("sub", None, "grp"),
            P(),
            P(),
            P(),
            P(),
            P(),
        ),
        out_specs=P("sub", "grp", None),
        check_vma=False,
    )
```
